32 devices in a mesh: blk: 8 (over z, core), col: 4 (over y, x).
Axes of the slice: x: 2, y: 2, z: 4, core: 2. Of those that a mesh axis runs over, the one named last changes fastest.
Arguments:
- stiffness: bfloat16 [64, 3, 128, 128], P('blk'), may hold values from -0.3125 to 0.3125
- block_cols: int32 [64, 3], P('blk'), may hold values from 0 to 63, as said below
- basis: bfloat16 [8192, 3, 512], P('blk', None, 'col'), may hold values from -1.1953125 to 1.1953125
- patch_reach: int32 [8, 512, 2], P(None, 'col'), may hold values from 0 to 8
Outputs:
- coarse: float32 [4096, 5, 512], P(('blk', 'col'))
The draws below stay inside these ranges and needn't reach their ends.
Inputs may be any that keep to these rules, and one draw needn't show every extreme that they name: `block_cols`: block row b lists block row b first and then two other distinct block rows among b - 2 .. b + 2 (periodic); the first block row of each slab lists b - 2 and b + 2.
All inputs are finite; a program needn't handle non-finite values.
Results may differ from the reference program's by a relative error of at most 0.0029.
Values may be sent and summed in bfloat16 or wider, within the bound.
No kernel may reach another device: no remote copies, remote signals or barrier semaphores. Data moves between devices by JAX's collectives and lax.ppermute only.
A program may use at most 64 MiB of HBM per device.

```python
import jax
import jax.numpy as jnp
from jax import lax

BS = 128
S = 3
RB = 8
NSLAB = 8
CS = 512
NB = 64


def draw_block_cols(key, part):
    pair_table = jnp.array([[-2, -1], [-2, 1], [-2, 2], [-1, 1], [-1, 2], [1, 2]], jnp.int32)
    chosen_pair = jax.random.randint(key, (NB,), 0, 6)
    offsets = pair_table[chosen_pair]
    row_ids = jnp.arange(NB, dtype=jnp.int32)
    first_row = row_ids % RB == 0
    offsets = jnp.where(first_row[:, None], jnp.array([[-2, 2]], jnp.int32), offsets)
    offsets = jnp.concatenate([jnp.zeros((NB, 1), jnp.int32), offsets], 1)
    return ((row_ids[:, None] + offsets) % NB).astype(jnp.int32)


def with_ends(result, rng, smallest, largest):
    longest = result.shape.index(max(result.shape))
    spots = []
    for shift in (0, 1):
        where = [jax.random.randint(jax.random.fold_in(rng, axis), (), 0, length) for axis, length in enumerate(result.shape)]
        where[longest] = (where[longest] + shift) % result.shape[longest]
        spots.append(tuple(where))
    return result.at[spots[0]].set(smallest).at[spots[1]].set(largest)


def block_scale(rng, shape, split, least, largest):
    loudness, own = 1.0, jax.random.fold_in(rng, 6)
    for dim, blocks in split:
        draws = jnp.exp(jax.random.uniform(jax.random.fold_in(own, dim), (blocks,), jnp.float32, least / len(split), largest / len(split)))
        loudness = loudness * jnp.repeat(draws, shape[dim] // blocks).reshape([-1 if axis == dim else 1 for axis in range(len(shape))])
    return loudness


def centred(rng, shape, spread, reach, shards=(), kind=jnp.bfloat16):
    level = block_scale(rng, shape, shards, -0.22, 0.18) if shards else 1.0
    drawn = jax.random.normal(rng, shape, jnp.float32) * spread * level
    return jnp.minimum(jnp.maximum(drawn, -reach), reach).astype(kind)


def setup_inputs(seed: int = 0) -> dict:
    streams_of = jax.random.split(jax.random.key(seed), 5)
    return {
        "stiffness": centred(streams_of[0], (NB, S, BS, BS), (S * BS) ** -0.5, 0.3125, ((0, 8),)),
        "block_cols": draw_block_cols(jax.random.fold_in(streams_of[4], 71), 0),
        "basis": centred(streams_of[2], (NB * BS, 3, CS), 0.2, 1.1953125, ((0, 8), (2, 4))),
        "patch_reach": with_ends(jax.random.randint(streams_of[3], (NSLAB, CS, 2), 0, RB + 1), jax.random.fold_in(streams_of[3], 1), 0, RB).astype(jnp.int32),
    }


def reference(stiffness, block_cols, basis, patch_reach):
    slab_count = patch_reach.shape[0]
    col_count = patch_reach.shape[1]
    block_size = stiffness.shape[2]
    row_count = RB * block_size
    shaped = basis.reshape(slab_count, row_count, 3, col_count)
    owners = jnp.arange(slab_count, dtype=jnp.int32)
    reach_low = patch_reach[(owners - 1) % slab_count][:, :, 1]
    reach_high = patch_reach[(owners + 1) % slab_count][:, :, 0]
    block_row = jnp.arange(row_count, dtype=jnp.int32) // block_size
    lower_mask = block_row[None, :, None] < reach_low[:, None, :]
    upper_mask = block_row[None, :, None] >= RB - reach_high[:, None, :]
    support = jnp.stack([lower_mask, jnp.ones_like(lower_mask), upper_mask], 2)
    masked = jnp.where(support, shaped, jnp.zeros_like(shaped))
    rim_width = 2 * block_size
    lower_rim = jnp.roll(masked, 1, 0)[:, row_count - rim_width:]
    upper_rim = jnp.roll(masked, -1, 0)[:, :rim_width]
    zero_rim = jnp.zeros((slab_count, rim_width, 1, col_count), masked.dtype)
    lower_rim = jnp.concatenate([lower_rim[:, :, 1:], zero_rim], 2)
    upper_rim = jnp.concatenate([zero_rim, upper_rim[:, :, :2]], 2)
    extended = jnp.concatenate([lower_rim, masked, upper_rim], 1)
    extended = extended.reshape(slab_count, RB + 4, block_size, 3 * col_count)
    stiff_slabs = stiffness.reshape(slab_count, RB, S, block_size, block_size)
    cols_slabs = block_cols.reshape(slab_count, RB, S)

    def one_slab(items):
        slab_index, stiff_part, cols_part, ext_part, basis_part = items
        position = ((cols_part - slab_index * RB + 2) % NB).astype(jnp.int32)
        picked = jnp.take(ext_part, position, axis=0)
        stiff_image = jnp.einsum("rsij,rsjc->ric", stiff_part.astype(jnp.float32), picked.astype(jnp.float32))
        stiff_image = stiff_image.astype(jnp.bfloat16).reshape(row_count, 3, col_count)
        return jnp.einsum("rgl,rhc->glhc", basis_part.astype(jnp.float32), stiff_image.astype(jnp.float32))

    tile_sums = lax.map(one_slab, (owners, stiff_slabs, cols_slabs, extended, masked))
    from_prev = jnp.roll(tile_sums[:, 2], 1, 0)
    from_next = jnp.roll(tile_sums[:, 0], -1, 0)
    own_part = tile_sums[:, 1]

    def place_tile(tile, offset_pos):
        return jnp.pad(tile, ((0, 0), (0, 0), (offset_pos, 2 - offset_pos), (0, 0)))

    coarse = place_tile(from_prev, 0) + place_tile(own_part, 1) + place_tile(from_next, 2)
    return coarse.reshape(slab_count * col_count, 5, col_count)
```

```python
import functools

import jax
import jax.numpy as jnp
from jax import lax
from jax.experimental import pallas as pl
from jax.experimental.pallas import tpu as pltpu
from jax.sharding import PartitionSpec as P

BF16 = jnp.bfloat16
F32 = jnp.float32
VMEM = pl.BlockSpec(memory_space=pltpu.VMEM)
SMEM = pl.BlockSpec(memory_space=pltpu.SMEM)
HBM = pl.BlockSpec(memory_space=pl.ANY)
RIM = 2


def shape(dims, dtype):
    return jax.ShapeDtypeStruct(dims, dtype)


def dot(left, right):
    return jnp.dot(left, right, preferred_element_type=F32)


def call(kernel, out_shape, in_specs, out_specs, args, scratch=(), flops=0, aliases=None, name=None):
    outs = jax.tree.leaves(out_shape)
    moved = sum(x.size * x.dtype.itemsize for x in (*args, *outs))
    return pl.pallas_call(
        kernel,
        out_shape=out_shape,
        in_specs=in_specs,
        out_specs=out_specs,
        scratch_shapes=list(scratch),
        input_output_aliases=aliases or {},
        cost_estimate=pl.CostEstimate(flops=flops, bytes_accessed=moved, transcendentals=0),
        compiler_params=pltpu.CompilerParams(vmem_limit_bytes=24 << 20),
        name=name,
    )(*args)


def block_image(stiffness, source, b, block_size, starts):
    blocks = [source[pl.ds(pl.multiple_of(start * block_size, block_size), block_size), :] for start in starts]
    left = jnp.concatenate([stiffness[b, k] for k in range(len(starts))], axis=1)
    return dot(left, jnp.concatenate(blocks, axis=0)).astype(BF16)


def positions(cols, b, blocks, slots, total_blocks):
    first = lax.axis_index("blk") * blocks
    return [
        jnp.clip(lax.rem(cols[k, b] - first + RIM + total_blocks, total_blocks), 0, blocks + 2 * RIM - 1)
        for k in range(slots)
    ]


def mask_and_inner(total_blocks, cols, basis, reach, stiffness, masked, to_next, to_prev, inner):
    blocks, slots, size, _ = stiffness.shape
    groups, _, width = basis.shape
    slabs = reach.shape[0]
    slab = lax.axis_index("blk")
    low = reach[pl.ds(lax.rem(slab + slabs - 1, slabs), 1), 1, :]
    high = reach[pl.ds(lax.rem(slab + 1, slabs), 1), 0, :]
    for b in range(blocks):
        rows = slice(b * size, (b + 1) * size)
        keep = {0: (b < low).astype(F32).astype(BF16), 2: (b >= blocks - high).astype(F32).astype(BF16)}
        for g in range(groups):
            value = basis[g, rows, :]
            masked[rows, g * width : (g + 1) * width] = value * keep[g] if g in keep else value
    to_next[...] = masked[(blocks - RIM) * size :, width:]
    to_prev[...] = masked[: RIM * size, : 2 * width]
    for b in range(RIM, blocks - RIM):
        starts = [jnp.clip(p - RIM, 0, blocks - 1) for p in positions(cols, b, blocks, slots, total_blocks)]
        inner[(b - RIM) * size : (b - RIM + 1) * size, :] = block_image(stiffness, masked, b, size, starts)


def outer_image(total_blocks, cols, stiffness, masked, from_prev, from_next, outer, extended):
    blocks, slots, size, _ = stiffness.shape
    rows, wide = masked.shape
    rim = RIM * size
    width = wide // 3
    extended[:rim, : 2 * width] = from_prev[...]
    extended[:rim, 2 * width :] = jnp.zeros((rim, width), BF16)
    extended[rim : rim + rows, :] = masked[...]
    extended[rim + rows :, :width] = jnp.zeros((rim, width), BF16)
    extended[rim + rows :, width:] = from_next[...]
    for n, b in enumerate([*range(RIM), *range(blocks - RIM, blocks)]):
        starts = positions(cols, b, blocks, slots, total_blocks)
        outer[n * size : (n + 1) * size, :] = block_image(stiffness, extended, b, size, starts)


def store_tile(tile, own, up, down, n):
    width = own.shape[1]
    down[n] = tile[:width].astype(BF16)
    own[n] = tile[width : 2 * width]
    up[n] = tile[2 * width :].astype(BF16)


def own_tile(size, masked, inner, outer, own, up, down, left_inner, left_outer):
    rows = masked.shape[0]
    rim = RIM * size
    left_inner[...] = masked[rim : rows - rim, :].T
    left_outer[:, :rim] = masked[:rim, :].T
    left_outer[:, rim:] = masked[rows - rim :, :].T
    tile = dot(left_inner[...], inner[...]) + dot(left_outer[...], outer[...])
    store_tile(tile, own, up, down, 0)


def other_tiles(count, left_inner, left_outer, *refs):
    images, (own, up, down) = refs[: 2 * count], refs[2 * count :]
    for n in range(count):
        tile = dot(left_inner[...], images[2 * n][...]) + dot(left_outer[...], images[2 * n + 1][...])
        store_tile(tile, own, up, down, n)


def add_tiles(sources, *refs):
    count = len(sources)
    terms, refs = refs[: 3 * count], refs[3 * count :]
    coarse, total, sem = refs[-3:]
    width = total.shape[2]
    me = lax.axis_index("col")
    copies = []
    n = 0
    for group, source in enumerate(sources):
        own, prev, nxt = terms[3 * group : 3 * group + 3]
        for m, step in enumerate(source):
            for d in range(5):
                value = None
                for offset, ref in ((0, prev), (1, own), (2, nxt)):
                    if 0 <= d - offset <= 2:
                        lanes = slice((d - offset) * width, (d - offset + 1) * width)
                        term = ref[m, :, lanes].astype(F32)
                        value = term if value is None else value + term
                total[n, d] = value
            start = pl.multiple_of(lax.bitwise_xor(me, step) * width, width)
            copy = pltpu.make_async_copy(total.at[n], coarse.at[:, :, pl.ds(start, width)], sem.at[n])
            copy.start()
            copies.append(copy)
            n += 1
    for copy in copies:
        copy.wait()


def tile_shapes(count, width, wide):
    return (
        shape((count, width, wide), F32),
        shape((count, width, wide), BF16),
        shape((count, width, wide), BF16),
    )


def shards(stiffness, block_cols, basis, patch_reach):
    blocks, slots, size, _ = stiffness.shape
    rows, groups, width = basis.shape
    wide = groups * width
    slabs = lax.axis_size("blk")
    total_blocks = blocks * slabs
    ring = [(i, (i + 1) % slabs) for i in range(slabs)]
    back = [(j, i) for i, j in ring]

    def to_next(value):
        return lax.ppermute(value, "blk", ring)

    def to_prev(value):
        return lax.ppermute(value, "blk", back)

    def swap(value, step):
        return lax.ppermute(value, "col", [(i, i ^ step) for i in range(4)])

    cols = block_cols.T
    flat = basis.transpose(1, 0, 2)
    reach = patch_reach.transpose(0, 2, 1)
    inner_rows = (blocks - 2 * RIM) * size
    rim = RIM * size
    row_flops = 2 * slots * size * size * wide
    masked, last, leading, inner = call(
        functools.partial(mask_and_inner, total_blocks),
        (shape((rows, wide), BF16), shape((rim, 2 * width), BF16), shape((rim, 2 * width), BF16), shape((inner_rows, wide), BF16)),
        [SMEM, VMEM, VMEM, VMEM],
        [VMEM] * 4,
        (cols, flat, reach, stiffness),
        flops=row_flops * (blocks - 2 * RIM),
        name="mask_and_inner",
    )
    inner_x = swap(inner, 1)
    inner_y = swap(inner, 2)
    before = to_next(last)
    after = to_prev(leading)
    outer = call(
        functools.partial(outer_image, total_blocks),
        shape((2 * rim, wide), BF16),
        [SMEM] + [VMEM] * 4,
        VMEM,
        (cols, stiffness, masked, before, after),
        scratch=[pltpu.VMEM((rows + 2 * rim, wide), BF16)],
        flops=row_flops * 2 * RIM,
        name="outer_image",
    )
    outer_x = swap(outer, 1)
    outer_y = swap(outer, 2)
    tile_flops = 2 * rows * wide * wide
    own_a, up_a, down_a, left_inner, left_outer = call(
        functools.partial(own_tile, size),
        (*tile_shapes(1, width, wide), shape((wide, inner_rows), BF16), shape((wide, 2 * rim), BF16)),
        [VMEM] * 3,
        [VMEM] * 5,
        (masked, inner, outer),
        flops=tile_flops,
        name="own_tile",
    )
    prev_a = to_next(up_a)
    next_a = to_prev(down_a)
    inner_d = swap(inner_x, 2)
    outer_d = swap(outer_y, 1)

    def tiles(images, name):
        count = len(images) // 2
        return call(
            functools.partial(other_tiles, count),
            tile_shapes(count, width, wide),
            [VMEM] * (2 + 2 * count),
            [VMEM] * 3,
            (left_inner, left_outer, *images),
            flops=tile_flops * count,
            name=name,
        )

    own_b, up_b, down_b = tiles((inner_x, outer_x, inner_y, outer_y), "side_tiles")
    prev_b = to_next(up_b)
    next_b = to_prev(down_b)
    own_c, up_c, down_c = tiles((inner_d, outer_d), "diagonal_tile")
    prev_c = to_next(up_c)
    next_c = to_prev(down_c)

    def add(sources, terms, name, base=None):
        count = sum(map(len, sources))
        extra = () if base is None else (base,)
        return call(
            functools.partial(add_tiles, sources),
            shape((5, width, 4 * width), F32),
            [VMEM] * len(terms) + [HBM] * len(extra),
            HBM,
            (*terms, *extra),
            scratch=[pltpu.VMEM((count, 5, width, width), F32), pltpu.SemaphoreType.DMA((count,))],
            flops=5 * count * width * width,
            aliases={len(terms): 0} if extra else None,
            name=name,
        )

    coarse = add(((0,), (1, 2)), (own_a, prev_a, next_a, own_b, prev_b, next_b), "add_near")
    coarse = add(((3,),), (own_c, prev_c, next_c), "add_diagonal", coarse)
    return coarse.transpose(1, 0, 2)


def gathered(stiffness, block_cols, basis, patch_reach):
    blocks, slots, size, _ = stiffness.shape
    rows, groups, width = basis.shape
    slabs = lax.axis_size("blk")
    slab = lax.axis_index("blk")
    total_blocks = blocks * slabs
    ring = [(i, (i + 1) % slabs) for i in range(slabs)]
    back = [(j, i) for i, j in ring]
    low = lax.dynamic_index_in_dim(patch_reach, (slab - 1) % slabs, 0, False)[:, 1]
    high = lax.dynamic_index_in_dim(patch_reach, (slab + 1) % slabs, 0, False)[:, 0]
    block_row = jnp.arange(rows, dtype=jnp.int32) // size
    lower = block_row[:, None] < low[None, :]
    upper = block_row[:, None] >= blocks - high[None, :]
    support = jnp.stack([lower, jnp.ones_like(lower), upper], 1)
    masked = jnp.where(support, basis, jnp.zeros_like(basis))
    rim = RIM * size
    before = lax.ppermute(masked[rows - rim :, 1:], "blk", ring)
    after = lax.ppermute(masked[:rim, :2], "blk", back)
    none = jnp.zeros((rim, 1, width), masked.dtype)
    extended = jnp.concatenate(
        [jnp.concatenate([before, none], 1), masked, jnp.concatenate([none, after], 1)], 0
    ).reshape(blocks + 2 * RIM, size, groups * width)
    position = (block_cols - slab * blocks + RIM) % total_blocks
    picked = jnp.take(extended, position, axis=0)
    image = jnp.einsum("rsij,rsjc->ric", stiffness, picked, preferred_element_type=F32)
    image = image.astype(BF16).reshape(rows, groups, width)
    image = lax.all_gather(image, "col", axis=2, tiled=True)
    tiles = jnp.einsum("rgl,rhc->glhc", masked, image, preferred_element_type=F32)
    from_prev = lax.ppermute(tiles[2], "blk", ring)
    from_next = lax.ppermute(tiles[0], "blk", back)

    def place(tile, offset):
        return jnp.pad(tile, ((0, 0), (offset, 2 - offset), (0, 0)))

    return place(from_prev, 0) + place(tiles[1], 1) + place(from_next, 2)


def solution(mesh):
    in_specs = (
        P("blk", None, None, None),
        P("blk", None),
        P("blk", None, "col"),
        P(None, "col", None),
    )
    out_specs = P(("blk", "col"), None, None)
    body = shards if mesh.shape["col"] == 4 else gathered
    return jax.shard_map(body, mesh=mesh, in_specs=in_specs, out_specs=out_specs, check_vma=False)
```

```python
import functools

import jax
import jax.numpy as jnp
from jax import lax
from jax.experimental import pallas as pl
from jax.experimental.pallas import tpu as pltpu
from jax.sharding import PartitionSpec as P

BF16 = jnp.bfloat16
F32 = jnp.float32
VMEM = pl.BlockSpec(memory_space=pltpu.VMEM)
SMEM = pl.BlockSpec(memory_space=pltpu.SMEM)
HBM = pl.BlockSpec(memory_space=pltpu.HBM)
RIM = 2


def shape(dims, dtype):
    return jax.ShapeDtypeStruct(dims, dtype)


def dot(left, right):
    return jnp.dot(left, right, preferred_element_type=F32)


def call(kernel, out_shape, in_specs, out_specs, args, scratch=(), flops=0, aliases=None, name=None, vmem=24):
    outs = jax.tree.leaves(out_shape)
    moved = sum(x.size * x.dtype.itemsize for x in (*args, *outs))
    return pl.pallas_call(
        kernel,
        out_shape=out_shape,
        in_specs=in_specs,
        out_specs=out_specs,
        scratch_shapes=list(scratch),
        input_output_aliases=aliases or {},
        cost_estimate=pl.CostEstimate(flops=flops, bytes_accessed=moved, transcendentals=0),
        compiler_params=pltpu.CompilerParams(vmem_limit_bytes=vmem << 20),
        name=name,
    )(*args)


def block_image(stiffness, source, b, block_size, starts):
    blocks = [source[pl.ds(pl.multiple_of(start * block_size, block_size), block_size), :] for start in starts]
    left = jnp.concatenate([stiffness[b, k] for k in range(len(starts))], axis=1)
    return dot(left, jnp.concatenate(blocks, axis=0)).astype(BF16)


def positions(cols, b, blocks, slots, total_blocks):
    first = lax.axis_index("blk") * blocks
    return [
        jnp.clip(lax.rem(cols[k, b] - first + RIM + total_blocks, total_blocks), 0, blocks + 2 * RIM - 1)
        for k in range(slots)
    ]


def mask_and_inner(
    total_blocks, cols_hbm, basis_hbm, reach_hbm, stiffness_hbm, masked, to_next, to_prev, inner, cols, basis, reach, stiffness, sem
):
    blocks, slots, size, _ = stiffness.shape
    groups, _, width = basis.shape
    slabs = reach.shape[0]
    slab = lax.axis_index("blk")
    copies = [
        pltpu.make_async_copy(source, target, sem.at[n])
        for n, (source, target) in enumerate(
            ((basis_hbm, basis), (stiffness_hbm, stiffness), (reach_hbm, reach), (cols_hbm, cols))
        )
    ]
    for copy in copies:
        copy.start()
    copies[2].wait()
    copies[0].wait()
    low = reach[pl.ds(lax.rem(slab + slabs - 1, slabs), 1), 1, :]
    high = reach[pl.ds(lax.rem(slab + 1, slabs), 1), 0, :]
    for b in range(blocks):
        rows = slice(b * size, (b + 1) * size)
        keep = {0: (b < low).astype(F32).astype(BF16), 2: (b >= blocks - high).astype(F32).astype(BF16)}
        for g in range(groups):
            value = basis[g, rows, :]
            masked[rows, g * width : (g + 1) * width] = value * keep[g] if g in keep else value
    to_next[...] = masked[(blocks - RIM) * size :, width:]
    to_prev[...] = masked[: RIM * size, : 2 * width]
    copies[3].wait()
    copies[1].wait()
    for b in range(RIM, blocks - RIM):
        starts = [jnp.clip(p - RIM, 0, blocks - 1) for p in positions(cols, b, blocks, slots, total_blocks)]
        inner[(b - RIM) * size : (b - RIM + 1) * size, :] = block_image(stiffness, masked, b, size, starts)


def outer_image(total_blocks, cols, stiffness, masked, from_prev, from_next, outer, extended):
    blocks, slots, size, _ = stiffness.shape
    rows, wide = masked.shape
    rim = RIM * size
    width = wide // 3
    extended[:rim, : 2 * width] = from_prev[...]
    extended[:rim, 2 * width :] = jnp.zeros((rim, width), BF16)
    extended[rim : rim + rows, :] = masked[...]
    extended[rim + rows :, :width] = jnp.zeros((rim, width), BF16)
    extended[rim + rows :, width:] = from_next[...]
    for n, b in enumerate([*range(RIM), *range(blocks - RIM, blocks)]):
        starts = positions(cols, b, blocks, slots, total_blocks)
        outer[n * size : (n + 1) * size, :] = block_image(stiffness, extended, b, size, starts)


def store_tile(tile, own, up, down, n):
    width = own.shape[1]
    down[n] = tile[:width].astype(BF16)
    own[n] = tile[width : 2 * width]
    up[n] = tile[2 * width :].astype(BF16)


def own_tile(size, masked, inner, outer, own, up, down, left_inner, left_outer):
    rows = masked.shape[0]
    rim = RIM * size
    left_inner[...] = masked[rim : rows - rim, :].T
    left_outer[:, :rim] = masked[:rim, :].T
    left_outer[:, rim:] = masked[rows - rim :, :].T
    tile = dot(left_inner[...], inner[...]) + dot(left_outer[...], outer[...])
    store_tile(tile, own, up, down, 0)


def other_tiles(count, left_inner, left_outer, *refs):
    images, (own, up, down) = refs[:-3], refs[-3:]
    each = len(images) // count
    for n in range(count):
        tile, start = None, [0, 0]
        for m, image in enumerate(images[n * each : (n + 1) * each]):
            which = m * 2 // each
            left = (left_inner, left_outer)[which][:, start[which] : start[which] + image.shape[0]]
            start[which] += image.shape[0]
            part = dot(left, image[...])
            tile = part if tile is None else tile + part
        store_tile(tile, own, up, down, n)


def add_tiles(sources, *refs):
    count = len(sources)
    terms, refs = refs[: 3 * count], refs[3 * count :]
    coarse, total, sem = refs[-3:]
    width = total.shape[2]
    me = lax.axis_index("col")
    copies = []
    n = 0
    for group, source in enumerate(sources):
        own, prev, nxt = terms[3 * group : 3 * group + 3]
        for m, step in enumerate(source):
            for d in range(5):
                value = None
                for offset, ref in ((0, prev), (1, own), (2, nxt)):
                    if 0 <= d - offset <= 2:
                        lanes = slice((d - offset) * width, (d - offset + 1) * width)
                        term = ref[m, :, lanes].astype(F32)
                        value = term if value is None else value + term
                total[n, d] = value
            start = pl.multiple_of(lax.bitwise_xor(me, step) * width, width)
            copy = pltpu.make_async_copy(total.at[n], coarse.at[:, :, pl.ds(start, width)], sem.at[n])
            copy.start()
            copies.append(copy)
            n += 1
    for copy in copies:
        copy.wait()


def tile_shapes(count, width, wide):
    return (
        shape((count, width, wide), F32),
        shape((count, width, wide), BF16),
        shape((count, width, wide), BF16),
    )


def shards(stiffness, block_cols, basis, patch_reach):
    blocks, slots, size, _ = stiffness.shape
    rows, groups, width = basis.shape
    wide = groups * width
    slabs = lax.axis_size("blk")
    total_blocks = blocks * slabs
    ring = [(i, (i + 1) % slabs) for i in range(slabs)]
    back = [(j, i) for i, j in ring]

    def to_next(value):
        return lax.ppermute(value, "blk", ring)

    def to_prev(value):
        return lax.ppermute(value, "blk", back)

    def swap(value, step):
        return lax.ppermute(value, "col", [(i, i ^ step) for i in range(4)])

    cols = block_cols.T
    flat = basis.transpose(1, 0, 2)
    reach = patch_reach.transpose(0, 2, 1)
    inner_rows = (blocks - 2 * RIM) * size
    rim = RIM * size
    row_flops = 2 * slots * size * size * wide
    masked, last, leading, inner = call(
        functools.partial(mask_and_inner, total_blocks),
        (shape((rows, wide), BF16), shape((rim, 2 * width), BF16), shape((rim, 2 * width), BF16), shape((inner_rows, wide), BF16)),
        [HBM] * 4,
        [VMEM] * 4,
        (cols, flat, reach, stiffness),
        scratch=[
            pltpu.SMEM(cols.shape, cols.dtype),
            pltpu.VMEM(flat.shape, BF16),
            pltpu.VMEM(reach.shape, reach.dtype),
            pltpu.VMEM(stiffness.shape, BF16),
            pltpu.SemaphoreType.DMA((4,)),
        ],
        flops=row_flops * (blocks - 2 * RIM),
        vmem=52,
        name="mask_and_inner",
    )
    inner_x = swap(inner, 1)
    inner_y = swap(inner, 2)
    before = to_next(last)
    after = to_prev(leading)
    outer = call(
        functools.partial(outer_image, total_blocks),
        shape((2 * rim, wide), BF16),
        [SMEM] + [VMEM] * 4,
        VMEM,
        (cols, stiffness, masked, before, after),
        scratch=[pltpu.VMEM((rows + 2 * rim, wide), BF16)],
        flops=row_flops * 2 * RIM,
        name="outer_image",
    )
    outer_x = swap(outer, 1)
    outer_y = swap(outer, 2)
    tile_flops = 2 * rows * wide * wide
    own_a, up_a, down_a, left_inner, left_outer = call(
        functools.partial(own_tile, size),
        (*tile_shapes(1, width, wide), shape((wide, inner_rows), BF16), shape((wide, 2 * rim), BF16)),
        [VMEM] * 3,
        [VMEM] * 5,
        (masked, inner, outer),
        flops=tile_flops,
        name="own_tile",
    )
    prev_a = to_next(up_a)
    next_a = to_prev(down_a)
    half = inner_rows // 2
    diagonal = (swap(inner_y[:half], 1), swap(inner_x[half:], 2), swap(outer_y[:rim], 1), swap(outer_x[rim:], 2))

    def tiles(count, images, name):
        return call(
            functools.partial(other_tiles, count),
            tile_shapes(count, width, wide),
            [VMEM] * (2 + len(images)),
            [VMEM] * 3,
            (left_inner, left_outer, *images),
            flops=tile_flops * count,
            name=name,
        )

    own_b, up_b, down_b = tiles(2, (inner_x, outer_x, inner_y, outer_y), "side_tiles")
    prev_b = to_next(up_b)
    next_b = to_prev(down_b)
    own_c, up_c, down_c = tiles(1, diagonal, "diagonal_tile")
    prev_c = to_next(up_c)
    next_c = to_prev(down_c)

    def add(sources, terms, name, base=None):
        count = sum(map(len, sources))
        extra = () if base is None else (base,)
        return call(
            functools.partial(add_tiles, sources),
            shape((5, width, 4 * width), F32),
            [VMEM] * len(terms) + [HBM] * len(extra),
            HBM,
            (*terms, *extra),
            scratch=[pltpu.VMEM((count, 5, width, width), F32), pltpu.SemaphoreType.DMA((count,))],
            flops=5 * count * width * width,
            aliases={len(terms): 0} if extra else None,
            name=name,
        )

    coarse = add(((0,), (1, 2)), (own_a, prev_a, next_a, own_b, prev_b, next_b), "add_near")
    coarse = add(((3,),), (own_c, prev_c, next_c), "add_diagonal", coarse)
    return coarse.transpose(1, 0, 2)


def gathered(stiffness, block_cols, basis, patch_reach):
    blocks, slots, size, _ = stiffness.shape
    rows, groups, width = basis.shape
    slabs = lax.axis_size("blk")
    slab = lax.axis_index("blk")
    total_blocks = blocks * slabs
    ring = [(i, (i + 1) % slabs) for i in range(slabs)]
    back = [(j, i) for i, j in ring]
    low = lax.dynamic_index_in_dim(patch_reach, (slab - 1) % slabs, 0, False)[:, 1]
    high = lax.dynamic_index_in_dim(patch_reach, (slab + 1) % slabs, 0, False)[:, 0]
    block_row = jnp.arange(rows, dtype=jnp.int32) // size
    lower = block_row[:, None] < low[None, :]
    upper = block_row[:, None] >= blocks - high[None, :]
    support = jnp.stack([lower, jnp.ones_like(lower), upper], 1)
    masked = jnp.where(support, basis, jnp.zeros_like(basis))
    rim = RIM * size
    before = lax.ppermute(masked[rows - rim :, 1:], "blk", ring)
    after = lax.ppermute(masked[:rim, :2], "blk", back)
    none = jnp.zeros((rim, 1, width), masked.dtype)
    extended = jnp.concatenate(
        [jnp.concatenate([before, none], 1), masked, jnp.concatenate([none, after], 1)], 0
    ).reshape(blocks + 2 * RIM, size, groups * width)
    position = (block_cols - slab * blocks + RIM) % total_blocks
    picked = jnp.take(extended, position, axis=0)
    image = jnp.einsum("rsij,rsjc->ric", stiffness, picked, preferred_element_type=F32)
    image = image.astype(BF16).reshape(rows, groups, width)
    image = lax.all_gather(image, "col", axis=2, tiled=True)
    tiles = jnp.einsum("rgl,rhc->glhc", masked, image, preferred_element_type=F32)
    from_prev = lax.ppermute(tiles[2], "blk", ring)
    from_next = lax.ppermute(tiles[0], "blk", back)

    def place(tile, offset):
        return jnp.pad(tile, ((0, 0), (offset, 2 - offset), (0, 0)))

    return place(from_prev, 0) + place(tiles[1], 1) + place(from_next, 2)


def solution(mesh):
    in_specs = (
        P("blk", None, None, None),
        P("blk", None),
        P("blk", None, "col"),
        P(None, "col", None),
    )
    out_specs = P(("blk", "col"), None, None)
    body = shards if mesh.shape["col"] == 4 else gathered
    return jax.shard_map(body, mesh=mesh, in_specs=in_specs, out_specs=out_specs, check_vma=False)
```

```python
import functools

import jax
import jax.numpy as jnp
from jax import lax
from jax.experimental import pallas as pl
from jax.experimental.pallas import tpu as pltpu
from jax.sharding import PartitionSpec as P

BF16 = jnp.bfloat16
F32 = jnp.float32
VMEM = pl.BlockSpec(memory_space=pltpu.VMEM)
SMEM = pl.BlockSpec(memory_space=pltpu.SMEM)
HBM = pl.BlockSpec(memory_space=pltpu.HBM)
RIM = 2


def shape(dims, dtype):
    return jax.ShapeDtypeStruct(dims, dtype)


def dot(left, right):
    return jnp.dot(left, right, preferred_element_type=F32)


def call(kernel, out_shape, in_specs, out_specs, args, scratch=(), flops=0, aliases=None, name=None, vmem=24 << 10):
    outs = jax.tree.leaves(out_shape)
    moved = sum(x.size * x.dtype.itemsize for x in (*args, *outs))
    return pl.pallas_call(
        kernel,
        out_shape=out_shape,
        in_specs=in_specs,
        out_specs=out_specs,
        scratch_shapes=list(scratch),
        input_output_aliases=aliases or {},
        cost_estimate=pl.CostEstimate(flops=flops, bytes_accessed=moved, transcendentals=0),
        compiler_params=pltpu.CompilerParams(vmem_limit_bytes=vmem << 10),
        name=name,
    )(*args)


def block_image(stiffness, source, b, block_size, starts):
    blocks = [source[pl.ds(pl.multiple_of(start * block_size, block_size), block_size), :] for start in starts]
    left = jnp.concatenate([stiffness[b, k] for k in range(len(starts))], axis=1)
    return dot(left, jnp.concatenate(blocks, axis=0)).astype(BF16)


def positions(cols, b, blocks, slots, total_blocks):
    first = lax.axis_index("blk") * blocks
    return [
        jnp.clip(lax.rem(cols[k, b] - first + RIM + total_blocks, total_blocks), 0, blocks + 2 * RIM - 1)
        for k in range(slots)
    ]


def mask_and_inner(
    total_blocks, cols_hbm, basis_hbm, reach_hbm, stiffness_hbm, masked, to_link, to_chip, inner, cols, basis, reach, stiffness, sem
):
    blocks, slots, size, _ = stiffness.shape
    groups, _, width = basis.shape
    slabs = reach.shape[0]
    slab = lax.axis_index("blk")
    copies = [
        pltpu.make_async_copy(source, target, sem.at[n])
        for n, (source, target) in enumerate(
            ((basis_hbm, basis), (stiffness_hbm, stiffness), (reach_hbm, reach), (cols_hbm, cols))
        )
    ]
    for copy in copies:
        copy.start()
    copies[2].wait()
    copies[0].wait()
    low = reach[pl.ds(lax.rem(slab + slabs - 1, slabs), 1), 1, :]
    high = reach[pl.ds(lax.rem(slab + 1, slabs), 1), 0, :]
    for b in range(blocks):
        rows = slice(b * size, (b + 1) * size)
        keep = {0: (b < low).astype(F32).astype(BF16), 2: (b >= blocks - high).astype(F32).astype(BF16)}
        for g in range(groups):
            value = basis[g, rows, :]
            masked[rows, g * width : (g + 1) * width] = value * keep[g] if g in keep else value
    odd = parity()

    @pl.when(odd == 0)
    def _():
        to_link[...] = masked[: RIM * size, : 2 * width]
        to_chip[...] = masked[(blocks - RIM) * size :, width:]

    @pl.when(odd == 1)
    def _():
        to_link[...] = masked[(blocks - RIM) * size :, width:]
        to_chip[...] = masked[: RIM * size, : 2 * width]

    copies[3].wait()
    copies[1].wait()
    for b in range(RIM, blocks - RIM):
        starts = [jnp.clip(p - RIM, 0, blocks - 1) for p in positions(cols, b, blocks, slots, total_blocks)]
        inner[(b - RIM) * size : (b - RIM + 1) * size, :] = block_image(stiffness, masked, b, size, starts)


def outer_image(total_blocks, cols, stiffness, masked, from_link, from_chip, outer, extended):
    blocks, slots, size, _ = stiffness.shape
    rows, wide = masked.shape
    rim = RIM * size
    width = wide // 3
    odd = parity()

    @pl.when(odd == 0)
    def _():
        extended[:rim, : 2 * width] = from_link[...]
        extended[rim + rows :, width:] = from_chip[...]

    @pl.when(odd == 1)
    def _():
        extended[:rim, : 2 * width] = from_chip[...]
        extended[rim + rows :, width:] = from_link[...]

    extended[:rim, 2 * width :] = jnp.zeros((rim, width), BF16)
    extended[rim : rim + rows, :] = masked[...]
    extended[rim + rows :, :width] = jnp.zeros((rim, width), BF16)
    for n, b in enumerate([*range(RIM), *range(blocks - RIM, blocks)]):
        starts = positions(cols, b, blocks, slots, total_blocks)
        outer[n * size : (n + 1) * size, :] = block_image(stiffness, extended, b, size, starts)


def parity():
    return lax.rem(lax.axis_index("blk"), 2)


def store_tile(tile, own, link, chip, n):
    width = own.shape[1]
    odd = parity()
    own[n] = tile[width : 2 * width]
    down, up = tile[:width].astype(BF16), tile[2 * width :].astype(BF16)

    @pl.when(odd == 0)
    def _():
        link[n] = down
        chip[n] = up

    @pl.when(odd == 1)
    def _():
        link[n] = up
        chip[n] = down


def near_tiles(size, masked, *refs):
    images, (own, link, chip, left_inner, left_outer) = refs[:-5], refs[-5:]
    rows = masked.shape[0]
    rim = RIM * size
    left_inner[...] = masked[rim : rows - rim, :].T
    left_outer[:, :rim] = masked[:rim, :].T
    left_outer[:, rim:] = masked[rows - rim :, :].T
    for n in range(len(images) // 2):
        tile = dot(left_inner[...], images[2 * n][...]) + dot(left_outer[...], images[2 * n + 1][...])
        store_tile(tile, own, link, chip, n)


def diagonal_tile(left_inner, left_outer, *refs):
    images, (own, link, chip) = refs[:-3], refs[-3:]
    tile = None
    for which, left in ((0, left_inner), (1, left_outer)):
        first, second = images[2 * which], images[2 * which + 1]
        half = first.shape[0]
        part = dot(left[:, :half], first[...]) + dot(left[:, half:], second[...])
        tile = part if tile is None else tile + part
    store_tile(tile, own, link, chip, 0)


def add_tiles(sources, *refs):
    count = len(sources)
    terms, refs = refs[: 3 * count], refs[3 * count :]
    coarse, total, sem = refs[-3:]
    width = total.shape[2]
    me = lax.axis_index("col")
    even = parity() == 0
    copies = []
    n = 0
    for group, source in enumerate(sources):
        own, link, chip = terms[3 * group : 3 * group + 3]
        for m, step in enumerate(source):
            prev = jnp.where(even, link[m].astype(F32), chip[m].astype(F32))
            nxt = jnp.where(even, chip[m].astype(F32), link[m].astype(F32))
            for d in range(5):
                value = None
                for offset, term in ((0, prev), (1, own[m]), (2, nxt)):
                    if 0 <= d - offset <= 2:
                        part = term[:, (d - offset) * width : (d - offset + 1) * width]
                        value = part if value is None else value + part
                total[n, d] = value
            start = pl.multiple_of(lax.bitwise_xor(me, step) * width, width)
            copy = pltpu.make_async_copy(total.at[n], coarse.at[:, :, pl.ds(start, width)], sem.at[n])
            copy.start()
            copies.append(copy)
            n += 1
    for copy in copies:
        copy.wait()


def tile_shapes(count, width, wide):
    return (
        shape((count, width, wide), F32),
        shape((count, width, wide), BF16),
        shape((count, width, wide), BF16),
    )


def shards(stiffness, block_cols, basis, patch_reach):
    blocks, slots, size, _ = stiffness.shape
    rows, groups, width = basis.shape
    wide = groups * width
    slabs = lax.axis_size("blk")
    total_blocks = blocks * slabs
    pairs = [(i, i ^ 1) for i in range(slabs)]
    cross = [(i, (i - 1 if i % 2 == 0 else i + 1) % slabs) for i in range(slabs)]

    def over_chip(value):
        return lax.ppermute(value, "blk", pairs)

    def over_link(value):
        return lax.ppermute(value, "blk", cross)

    def swap(value, step):
        return lax.ppermute(value, "col", [(i, i ^ step) for i in range(4)])

    cols = block_cols.T
    flat = basis.transpose(1, 0, 2)
    reach = patch_reach.transpose(0, 2, 1)
    inner_rows = (blocks - 2 * RIM) * size
    rim = RIM * size
    row_flops = 2 * slots * size * size * wide
    masked, rim_link, rim_chip, inner = call(
        functools.partial(mask_and_inner, total_blocks),
        (shape((rows, wide), BF16), shape((rim, 2 * width), BF16), shape((rim, 2 * width), BF16), shape((inner_rows, wide), BF16)),
        [HBM] * 4,
        [VMEM] * 4,
        (cols, flat, reach, stiffness),
        scratch=[
            pltpu.SMEM(cols.shape, cols.dtype),
            pltpu.VMEM(flat.shape, BF16),
            pltpu.VMEM(reach.shape, reach.dtype),
            pltpu.VMEM(stiffness.shape, BF16),
            pltpu.SemaphoreType.DMA((4,)),
        ],
        flops=row_flops * (blocks - 2 * RIM),
        vmem=53248,
        name="mask_and_inner",
    )
    inner_x = swap(inner, 1)
    inner_y = swap(inner, 2)
    rim_link = over_link(rim_link)
    rim_chip = over_chip(rim_chip)
    outer = call(
        functools.partial(outer_image, total_blocks),
        shape((2 * rim, wide), BF16),
        [SMEM] + [VMEM] * 4,
        VMEM,
        (cols, stiffness, masked, rim_link, rim_chip),
        scratch=[pltpu.VMEM((rows + 2 * rim, wide), BF16)],
        flops=row_flops * 2 * RIM,
        name="outer_image",
    )
    outer_x = swap(outer, 1)
    outer_y = swap(outer, 2)
    tile_flops = 2 * rows * wide * wide
    half = inner_rows // 2
    diagonal = (swap(inner_y[:half], 1), swap(inner_x[half:], 2), swap(outer_y[:rim], 1), swap(outer_x[rim:], 2))
    near_own, near_link, near_chip, left_inner, left_outer = call(
        functools.partial(near_tiles, size),
        (*tile_shapes(3, width, wide), shape((wide, inner_rows), BF16), shape((wide, 2 * rim), BF16)),
        [VMEM] * 7,
        [VMEM] * 5,
        (masked, inner, outer, inner_x, outer_x, inner_y, outer_y),
        flops=3 * tile_flops,
        name="near_tiles",
    )
    near_link = over_link(near_link)
    near_chip = over_chip(near_chip)
    far_own, far_link, far_chip = call(
        diagonal_tile,
        tile_shapes(1, width, wide),
        [VMEM] * 6,
        [VMEM] * 3,
        (left_inner, left_outer, *diagonal),
        flops=tile_flops,
        name="diagonal_tile",
    )
    far_link = over_link(far_link)
    far_chip = over_chip(far_chip)

    def add(sources, terms, name, base=None):
        count = sum(map(len, sources))
        extra = () if base is None else (base,)
        return call(
            functools.partial(add_tiles, sources),
            shape((5, width, 4 * width), F32),
            [VMEM] * len(terms) + [HBM] * len(extra),
            HBM,
            (*terms, *extra),
            scratch=[pltpu.VMEM((count, 5, width, width), F32), pltpu.SemaphoreType.DMA((count,))],
            flops=5 * count * width * width,
            aliases={len(terms): 0} if extra else None,
            name=name,
        )

    coarse = add(((0, 1, 2),), (near_own, near_link, near_chip), "add_near")
    coarse = add(((3,),), (far_own, far_link, far_chip), "add_diagonal", coarse)
    return coarse.transpose(1, 0, 2)


def gathered(stiffness, block_cols, basis, patch_reach):
    blocks, slots, size, _ = stiffness.shape
    rows, groups, width = basis.shape
    slabs = lax.axis_size("blk")
    slab = lax.axis_index("blk")
    total_blocks = blocks * slabs
    ring = [(i, (i + 1) % slabs) for i in range(slabs)]
    back = [(j, i) for i, j in ring]
    low = lax.dynamic_index_in_dim(patch_reach, (slab - 1) % slabs, 0, False)[:, 1]
    high = lax.dynamic_index_in_dim(patch_reach, (slab + 1) % slabs, 0, False)[:, 0]
    block_row = jnp.arange(rows, dtype=jnp.int32) // size
    lower = block_row[:, None] < low[None, :]
    upper = block_row[:, None] >= blocks - high[None, :]
    support = jnp.stack([lower, jnp.ones_like(lower), upper], 1)
    masked = jnp.where(support, basis, jnp.zeros_like(basis))
    rim = RIM * size
    before = lax.ppermute(masked[rows - rim :, 1:], "blk", ring)
    after = lax.ppermute(masked[:rim, :2], "blk", back)
    none = jnp.zeros((rim, 1, width), masked.dtype)
    extended = jnp.concatenate(
        [jnp.concatenate([before, none], 1), masked, jnp.concatenate([none, after], 1)], 0
    ).reshape(blocks + 2 * RIM, size, groups * width)
    position = (block_cols - slab * blocks + RIM) % total_blocks
    picked = jnp.take(extended, position, axis=0)
    image = jnp.einsum("rsij,rsjc->ric", stiffness, picked, preferred_element_type=F32)
    image = image.astype(BF16).reshape(rows, groups, width)
    image = lax.all_gather(image, "col", axis=2, tiled=True)
    tiles = jnp.einsum("rgl,rhc->glhc", masked, image, preferred_element_type=F32)
    from_prev = lax.ppermute(tiles[2], "blk", ring)
    from_next = lax.ppermute(tiles[0], "blk", back)

    def place(tile, offset):
        return jnp.pad(tile, ((0, 0), (offset, 2 - offset), (0, 0)))

    return place(from_prev, 0) + place(tiles[1], 1) + place(from_next, 2)


def solution(mesh):
    in_specs = (
        P("blk", None, None, None),
        P("blk", None),
        P("blk", None, "col"),
        P(None, "col", None),
    )
    out_specs = P(("blk", "col"), None, None)
    body = shards if mesh.shape["col"] == 4 else gathered
    return jax.shard_map(body, mesh=mesh, in_specs=in_specs, out_specs=out_specs, check_vma=False)
```

```python
import functools

import jax
import jax.numpy as jnp
from jax import lax
from jax.experimental import pallas as pl
from jax.experimental.pallas import tpu as pltpu
from jax.sharding import PartitionSpec as P

BF16 = jnp.bfloat16
F32 = jnp.float32
VMEM = pl.BlockSpec(memory_space=pltpu.VMEM)
SMEM = pl.BlockSpec(memory_space=pltpu.SMEM)
HBM = pl.BlockSpec(memory_space=pltpu.HBM)
RIM = 2


def shape(dims, dtype):
    return jax.ShapeDtypeStruct(dims, dtype)


def dot(left, right):
    return jnp.dot(left, right, preferred_element_type=F32)


def call(kernel, out_shape, in_specs, out_specs, args, scratch=(), flops=0, aliases=None, name=None, vmem=24 << 10):
    outs = jax.tree.leaves(out_shape)
    moved = sum(x.size * x.dtype.itemsize for x in (*args, *outs))
    return pl.pallas_call(
        kernel,
        out_shape=out_shape,
        in_specs=in_specs,
        out_specs=out_specs,
        scratch_shapes=list(scratch),
        input_output_aliases=aliases or {},
        cost_estimate=pl.CostEstimate(flops=flops, bytes_accessed=moved if flops else 0, transcendentals=0),
        compiler_params=pltpu.CompilerParams(vmem_limit_bytes=vmem << 10),
        name=name,
    )(*args)


def block_image(stiffness, source, b, block_size, starts):
    blocks = [source[pl.ds(pl.multiple_of(start * block_size, block_size), block_size), :] for start in starts]
    left = jnp.concatenate([stiffness[b, k] for k in range(len(starts))], axis=1)
    return dot(left, jnp.concatenate(blocks, axis=0)).astype(BF16)


def positions(cols, b, blocks, slots, total_blocks):
    first = lax.axis_index("blk") * blocks
    return [
        jnp.clip(lax.rem(cols[k, b] - first + RIM + total_blocks, total_blocks), 0, blocks + 2 * RIM - 1)
        for k in range(slots)
    ]


def mask_and_inner(
    total_blocks, cols_hbm, basis_hbm, reach_hbm, stiffness_hbm, masked, to_link, to_chip, inner, cols, basis, reach, stiffness, sem
):
    blocks, slots, size, _ = stiffness.shape
    groups, _, width = basis.shape
    slabs = reach.shape[0]
    slab = lax.axis_index("blk")
    copies = [
        pltpu.make_async_copy(source, target, sem.at[n])
        for n, (source, target) in enumerate(
            ((basis_hbm, basis), (stiffness_hbm, stiffness), (reach_hbm, reach), (cols_hbm, cols))
        )
    ]
    for copy in copies:
        copy.start()
    copies[2].wait()
    copies[0].wait()
    low = reach[pl.ds(lax.rem(slab + slabs - 1, slabs), 1), 1, :]
    high = reach[pl.ds(lax.rem(slab + 1, slabs), 1), 0, :]
    for b in range(blocks):
        rows = slice(b * size, (b + 1) * size)
        keep = {0: (b < low).astype(F32).astype(BF16), 2: (b >= blocks - high).astype(F32).astype(BF16)}
        for g in range(groups):
            value = basis[g, rows, :]
            masked[rows, g * width : (g + 1) * width] = value * keep[g] if g in keep else value
    odd = parity()

    @pl.when(odd == 0)
    def _():
        to_link[...] = masked[: RIM * size, : 2 * width]
        to_chip[...] = masked[(blocks - RIM) * size :, width:]

    @pl.when(odd == 1)
    def _():
        to_link[...] = masked[(blocks - RIM) * size :, width:]
        to_chip[...] = masked[: RIM * size, : 2 * width]

    copies[3].wait()
    copies[1].wait()
    for b in range(RIM, blocks - RIM):
        starts = [jnp.clip(p - RIM, 0, blocks - 1) for p in positions(cols, b, blocks, slots, total_blocks)]
        inner[(b - RIM) * size : (b - RIM + 1) * size, :] = block_image(stiffness, masked, b, size, starts)


def outer_image(total_blocks, cols, stiffness, masked, from_link, from_chip, outer, extended):
    blocks, slots, size, _ = stiffness.shape
    rows, wide = masked.shape
    rim = RIM * size
    width = wide // 3
    odd = parity()

    @pl.when(odd == 0)
    def _():
        extended[:rim, : 2 * width] = from_link[...]
        extended[rim + rows :, width:] = from_chip[...]

    @pl.when(odd == 1)
    def _():
        extended[:rim, : 2 * width] = from_chip[...]
        extended[rim + rows :, width:] = from_link[...]

    extended[:rim, 2 * width :] = jnp.zeros((rim, width), BF16)
    extended[rim : rim + rows, :] = masked[...]
    extended[rim + rows :, :width] = jnp.zeros((rim, width), BF16)
    for n, b in enumerate([*range(RIM), *range(blocks - RIM, blocks)]):
        starts = positions(cols, b, blocks, slots, total_blocks)
        outer[n * size : (n + 1) * size, :] = block_image(stiffness, extended, b, size, starts)


def parity():
    return lax.rem(lax.axis_index("blk"), 2)


def store_tile(tile, own, link, chip, n):
    width = own.shape[1]
    odd = parity()
    own[n] = tile[width : 2 * width]
    down, up = tile[:width].astype(BF16), tile[2 * width :].astype(BF16)

    @pl.when(odd == 0)
    def _():
        link[n] = down
        chip[n] = up

    @pl.when(odd == 1)
    def _():
        link[n] = up
        chip[n] = down


def near_tiles(size, masked, *refs):
    images, (own, link, chip, left_inner, left_outer) = refs[:-5], refs[-5:]
    rows = masked.shape[0]
    rim = RIM * size
    left_inner[...] = masked[rim : rows - rim, :].T
    left_outer[:, :rim] = masked[:rim, :].T
    left_outer[:, rim:] = masked[rows - rim :, :].T
    for n in range(len(images) // 2):
        tile = dot(left_inner[...], images[2 * n][...]) + dot(left_outer[...], images[2 * n + 1][...])
        store_tile(tile, own, link, chip, n)


def diagonal_tile(left_inner, left_outer, *refs):
    images, (own, link, chip) = refs[:-3], refs[-3:]
    tile = None
    for which, left in ((0, left_inner), (1, left_outer)):
        first, second = images[2 * which], images[2 * which + 1]
        half = first.shape[0]
        part = dot(left[:, :half], first[...]) + dot(left[:, half:], second[...])
        tile = part if tile is None else tile + part
    store_tile(tile, own, link, chip, 0)


def add_tiles(sources, *refs):
    count = len(sources)
    terms, refs = refs[: 3 * count], refs[3 * count :]
    coarse, total, sem = refs[-3:]
    width = total.shape[2]
    me = lax.axis_index("col")
    even = parity() == 0
    copies = []
    n = 0
    for group, source in enumerate(sources):
        own, link, chip = terms[3 * group : 3 * group + 3]
        for m, step in enumerate(source):
            prev = jnp.where(even, link[m].astype(F32), chip[m].astype(F32))
            nxt = jnp.where(even, chip[m].astype(F32), link[m].astype(F32))
            for d in range(5):
                value = None
                for offset, term in ((0, prev), (1, own[m]), (2, nxt)):
                    if 0 <= d - offset <= 2:
                        part = term[:, (d - offset) * width : (d - offset + 1) * width]
                        value = part if value is None else value + part
                total[n, d] = value
            start = pl.multiple_of(lax.bitwise_xor(me, step) * width, width)
            copy = pltpu.make_async_copy(total.at[n], coarse.at[:, :, pl.ds(start, width)], sem.at[n])
            copy.start()
            copies.append(copy)
            n += 1
    for copy in copies:
        copy.wait()


def tile_shapes(count, width, wide):
    return (
        shape((count, width, wide), F32),
        shape((count, width, wide), BF16),
        shape((count, width, wide), BF16),
    )


def shards(stiffness, block_cols, basis, patch_reach):
    blocks, slots, size, _ = stiffness.shape
    rows, groups, width = basis.shape
    wide = groups * width
    slabs = lax.axis_size("blk")
    total_blocks = blocks * slabs
    pairs = [(i, i ^ 1) for i in range(slabs)]
    cross = [(i, (i - 1 if i % 2 == 0 else i + 1) % slabs) for i in range(slabs)]

    def over_chip(value):
        return lax.ppermute(value, "blk", pairs)

    def over_link(value):
        return lax.ppermute(value, "blk", cross)

    def swap(value, step):
        return lax.ppermute(value, "col", [(i, i ^ step) for i in range(4)])

    cols = block_cols.T
    flat = basis.transpose(1, 0, 2)
    reach = patch_reach.transpose(0, 2, 1)
    inner_rows = (blocks - 2 * RIM) * size
    rim = RIM * size
    row_flops = 2 * slots * size * size * wide
    masked, rim_link, rim_chip, inner = call(
        functools.partial(mask_and_inner, total_blocks),
        (shape((rows, wide), BF16), shape((rim, 2 * width), BF16), shape((rim, 2 * width), BF16), shape((inner_rows, wide), BF16)),
        [HBM] * 4,
        [VMEM] * 4,
        (cols, flat, reach, stiffness),
        scratch=[
            pltpu.SMEM(cols.shape, cols.dtype),
            pltpu.VMEM(flat.shape, BF16),
            pltpu.VMEM(reach.shape, reach.dtype),
            pltpu.VMEM(stiffness.shape, BF16),
            pltpu.SemaphoreType.DMA((4,)),
        ],
        flops=row_flops * (blocks - 2 * RIM),
        vmem=53248,
        name="mask_and_inner",
    )
    inner_x = swap(inner, 1)
    inner_y = swap(inner, 2)
    rim_link = over_link(rim_link)
    rim_chip = over_chip(rim_chip)
    outer = call(
        functools.partial(outer_image, total_blocks),
        shape((2 * rim, wide), BF16),
        [SMEM] + [VMEM] * 4,
        VMEM,
        (cols, stiffness, masked, rim_link, rim_chip),
        scratch=[pltpu.VMEM((rows + 2 * rim, wide), BF16)],
        flops=row_flops * 2 * RIM,
        name="outer_image",
    )
    outer, inner_x, inner_y = lax.optimization_barrier((outer, inner_x, inner_y))
    outer_x = swap(outer, 1)
    outer_y = swap(outer, 2)
    tile_flops = 2 * rows * wide * wide
    half = inner_rows // 2
    diagonal = (swap(inner_y[:half], 1), swap(inner_x[half:], 2), swap(outer_y[:rim], 1), swap(outer_x[rim:], 2))
    near_own, near_link, near_chip, left_inner, left_outer = call(
        functools.partial(near_tiles, size),
        (*tile_shapes(3, width, wide), shape((wide, inner_rows), BF16), shape((wide, 2 * rim), BF16)),
        [VMEM] * 7,
        [VMEM] * 5,
        (masked, inner, outer, inner_x, outer_x, inner_y, outer_y),
        flops=3 * tile_flops,
        name="near_tiles",
    )
    near_link = over_link(near_link)
    near_chip = over_chip(near_chip)
    far_own, far_link, far_chip = call(
        diagonal_tile,
        tile_shapes(1, width, wide),
        [VMEM] * 6,
        [VMEM] * 3,
        (left_inner, left_outer, *diagonal),
        flops=tile_flops,
        name="diagonal_tile",
    )
    far_link = over_link(far_link)
    far_chip = over_chip(far_chip)

    def add(sources, terms, name, base=None):
        count = sum(map(len, sources))
        extra = () if base is None else (base,)
        return call(
            functools.partial(add_tiles, sources),
            shape((5, width, 4 * width), F32),
            [VMEM] * len(terms) + [HBM] * len(extra),
            HBM,
            (*terms, *extra),
            scratch=[pltpu.VMEM((count, 5, width, width), F32), pltpu.SemaphoreType.DMA((count,))],
            flops=5 * count * width * width,
            aliases={len(terms): 0} if extra else None,
            name=name,
        )

    coarse = add(((0, 1, 2),), (near_own, near_link, near_chip), "add_near")
    coarse = add(((3,),), (far_own, far_link, far_chip), "add_diagonal", coarse)
    return coarse.transpose(1, 0, 2)


def gathered(stiffness, block_cols, basis, patch_reach):
    blocks, slots, size, _ = stiffness.shape
    rows, groups, width = basis.shape
    slabs = lax.axis_size("blk")
    slab = lax.axis_index("blk")
    total_blocks = blocks * slabs
    ring = [(i, (i + 1) % slabs) for i in range(slabs)]
    back = [(j, i) for i, j in ring]
    low = lax.dynamic_index_in_dim(patch_reach, (slab - 1) % slabs, 0, False)[:, 1]
    high = lax.dynamic_index_in_dim(patch_reach, (slab + 1) % slabs, 0, False)[:, 0]
    block_row = jnp.arange(rows, dtype=jnp.int32) // size
    lower = block_row[:, None] < low[None, :]
    upper = block_row[:, None] >= blocks - high[None, :]
    support = jnp.stack([lower, jnp.ones_like(lower), upper], 1)
    masked = jnp.where(support, basis, jnp.zeros_like(basis))
    rim = RIM * size
    before = lax.ppermute(masked[rows - rim :, 1:], "blk", ring)
    after = lax.ppermute(masked[:rim, :2], "blk", back)
    none = jnp.zeros((rim, 1, width), masked.dtype)
    extended = jnp.concatenate(
        [jnp.concatenate([before, none], 1), masked, jnp.concatenate([none, after], 1)], 0
    ).reshape(blocks + 2 * RIM, size, groups * width)
    position = (block_cols - slab * blocks + RIM) % total_blocks
    picked = jnp.take(extended, position, axis=0)
    image = jnp.einsum("rsij,rsjc->ric", stiffness, picked, preferred_element_type=F32)
    image = image.astype(BF16).reshape(rows, groups, width)
    image = lax.all_gather(image, "col", axis=2, tiled=True)
    tiles = jnp.einsum("rgl,rhc->glhc", masked, image, preferred_element_type=F32)
    from_prev = lax.ppermute(tiles[2], "blk", ring)
    from_next = lax.ppermute(tiles[0], "blk", back)

    def place(tile, offset):
        return jnp.pad(tile, ((0, 0), (offset, 2 - offset), (0, 0)))

    return place(from_prev, 0) + place(tiles[1], 1) + place(from_next, 2)


def solution(mesh):
    in_specs = (
        P("blk", None, None, None),
        P("blk", None),
        P("blk", None, "col"),
        P(None, "col", None),
    )
    out_specs = P(("blk", "col"), None, None)
    body = shards if mesh.shape["col"] == 4 else gathered
    return jax.shard_map(body, mesh=mesh, in_specs=in_specs, out_specs=out_specs, check_vma=False)
```

```python
import functools

import jax
import jax.numpy as jnp
from jax import lax
from jax.experimental import pallas as pl
from jax.experimental.pallas import tpu as pltpu
from jax.sharding import PartitionSpec as P

BF16 = jnp.bfloat16
F32 = jnp.float32
VMEM = pl.BlockSpec(memory_space=pltpu.VMEM)
SMEM = pl.BlockSpec(memory_space=pltpu.SMEM)
HBM = pl.BlockSpec(memory_space=pltpu.HBM)
RIM = 2


def shape(dims, dtype):
    return jax.ShapeDtypeStruct(dims, dtype)


def dot(left, right):
    return jnp.dot(left, right, preferred_element_type=F32)


def call(kernel, out_shape, in_specs, out_specs, args, scratch=(), flops=0, aliases=None, name=None, vmem=24 << 10):
    outs = jax.tree.leaves(out_shape)
    moved = sum(x.size * x.dtype.itemsize for x in (*args, *outs))
    return pl.pallas_call(
        kernel,
        out_shape=out_shape,
        in_specs=in_specs,
        out_specs=out_specs,
        scratch_shapes=list(scratch),
        input_output_aliases=aliases or {},
        cost_estimate=pl.CostEstimate(flops=flops, bytes_accessed=moved, transcendentals=0),
        compiler_params=pltpu.CompilerParams(vmem_limit_bytes=vmem << 10),
        name=name,
    )(*args)


def block_image(stiffness, source, b, block_size, starts):
    blocks = [source[pl.ds(pl.multiple_of(start * block_size, block_size), block_size), :] for start in starts]
    left = jnp.concatenate([stiffness[b, k] for k in range(len(starts))], axis=1)
    return dot(left, jnp.concatenate(blocks, axis=0)).astype(BF16)


def positions(cols, b, blocks, slots, total_blocks):
    first = lax.axis_index("blk") * blocks
    return [
        jnp.clip(lax.rem(cols[k, b] - first + RIM + total_blocks, total_blocks), 0, blocks + 2 * RIM - 1)
        for k in range(slots)
    ]


def mask_and_inner(
    total_blocks, cols_hbm, basis_hbm, reach_hbm, stiffness_hbm, masked, to_link, to_chip, inner, cols, basis, reach, stiffness, sem
):
    blocks, slots, size, _ = stiffness.shape
    groups, _, width = basis.shape
    slabs = reach.shape[0]
    slab = lax.axis_index("blk")
    copies = [
        pltpu.make_async_copy(source, target, sem.at[n])
        for n, (source, target) in enumerate(
            ((basis_hbm, basis), (stiffness_hbm, stiffness), (reach_hbm, reach), (cols_hbm, cols))
        )
    ]
    for copy in copies:
        copy.start()
    copies[2].wait()
    copies[0].wait()
    low = reach[pl.ds(lax.rem(slab + slabs - 1, slabs), 1), 1, :]
    high = reach[pl.ds(lax.rem(slab + 1, slabs), 1), 0, :]
    for b in range(blocks):
        rows = slice(b * size, (b + 1) * size)
        keep = {0: (b < low).astype(F32).astype(BF16), 2: (b >= blocks - high).astype(F32).astype(BF16)}
        for g in range(groups):
            value = basis[g, rows, :]
            masked[rows, g * width : (g + 1) * width] = value * keep[g] if g in keep else value
    odd = parity()

    @pl.when(odd == 0)
    def _():
        to_link[...] = masked[: RIM * size, : 2 * width]
        to_chip[...] = masked[(blocks - RIM) * size :, width:]

    @pl.when(odd == 1)
    def _():
        to_link[...] = masked[(blocks - RIM) * size :, width:]
        to_chip[...] = masked[: RIM * size, : 2 * width]

    copies[3].wait()
    copies[1].wait()
    for b in range(RIM, blocks - RIM):
        starts = [jnp.clip(p - RIM, 0, blocks - 1) for p in positions(cols, b, blocks, slots, total_blocks)]
        inner[(b - RIM) * size : (b - RIM + 1) * size, :] = block_image(stiffness, masked, b, size, starts)


def outer_image(total_blocks, cols, stiffness, masked, from_link, from_chip, outer, extended):
    blocks, slots, size, _ = stiffness.shape
    rows, wide = masked.shape
    rim = RIM * size
    width = wide // 3
    odd = parity()

    @pl.when(odd == 0)
    def _():
        extended[:rim, : 2 * width] = from_link[...]
        extended[rim + rows :, width:] = from_chip[...]

    @pl.when(odd == 1)
    def _():
        extended[:rim, : 2 * width] = from_chip[...]
        extended[rim + rows :, width:] = from_link[...]

    extended[:rim, 2 * width :] = jnp.zeros((rim, width), BF16)
    extended[rim : rim + rows, :] = masked[...]
    extended[rim + rows :, :width] = jnp.zeros((rim, width), BF16)
    for n, b in enumerate([*range(RIM), *range(blocks - RIM, blocks)]):
        starts = positions(cols, b, blocks, slots, total_blocks)
        outer[n * size : (n + 1) * size, :] = block_image(stiffness, extended, b, size, starts)


def parity():
    return lax.rem(lax.axis_index("blk"), 2)


def store_tile(tile, own, link, chip, n):
    width = own.shape[1]
    odd = parity()
    own[n] = tile[width : 2 * width]
    down, up = tile[:width].astype(BF16), tile[2 * width :].astype(BF16)

    @pl.when(odd == 0)
    def _():
        link[n] = down
        chip[n] = up

    @pl.when(odd == 1)
    def _():
        link[n] = up
        chip[n] = down


def own_tile(size, masked, inner, outer, own, link, chip, left_inner, left_outer):
    rows = masked.shape[0]
    rim = RIM * size
    left_inner[...] = masked[rim : rows - rim, :].T
    left_outer[:, :rim] = masked[:rim, :].T
    left_outer[:, rim:] = masked[rows - rim :, :].T
    store_tile(dot(left_inner[...], inner[...]) + dot(left_outer[...], outer[...]), own, link, chip, 0)


def near_tiles(left_inner, left_outer, *refs):
    images, (own, link, chip) = refs[:-3], refs[-3:]
    for n in range(len(images) // 2):
        tile = dot(left_inner[...], images[2 * n][...]) + dot(left_outer[...], images[2 * n + 1][...])
        store_tile(tile, own, link, chip, n)


def diagonal_tile(left_inner, left_outer, *refs):
    images, (own, link, chip) = refs[:-3], refs[-3:]
    tile = None
    for which, left in ((0, left_inner), (1, left_outer)):
        first, second = images[2 * which], images[2 * which + 1]
        half = first.shape[0]
        part = dot(left[:, :half], first[...]) + dot(left[:, half:], second[...])
        tile = part if tile is None else tile + part
    store_tile(tile, own, link, chip, 0)


def add_tiles(sources, *refs):
    count = len(sources)
    terms, refs = refs[: 3 * count], refs[3 * count :]
    coarse, total, sem = refs[-3:]
    width = total.shape[2]
    me = lax.axis_index("col")
    even = parity() == 0
    copies = []
    n = 0
    for group, source in enumerate(sources):
        own, link, chip = terms[3 * group : 3 * group + 3]
        for m, step in enumerate(source):
            prev = jnp.where(even, link[m].astype(F32), chip[m].astype(F32))
            nxt = jnp.where(even, chip[m].astype(F32), link[m].astype(F32))
            for d in range(5):
                value = None
                for offset, term in ((0, prev), (1, own[m]), (2, nxt)):
                    if 0 <= d - offset <= 2:
                        part = term[:, (d - offset) * width : (d - offset + 1) * width]
                        value = part if value is None else value + part
                total[n, d] = value
            start = pl.multiple_of(lax.bitwise_xor(me, step) * width, width)
            copy = pltpu.make_async_copy(total.at[n], coarse.at[:, :, pl.ds(start, width)], sem.at[n])
            copy.start()
            copies.append(copy)
            n += 1
    for copy in copies:
        copy.wait()


def tile_shapes(count, width, wide):
    return (
        shape((count, width, wide), F32),
        shape((count, width, wide), BF16),
        shape((count, width, wide), BF16),
    )


def shards(stiffness, block_cols, basis, patch_reach):
    blocks, slots, size, _ = stiffness.shape
    rows, groups, width = basis.shape
    wide = groups * width
    slabs = lax.axis_size("blk")
    total_blocks = blocks * slabs
    pairs = [(i, i ^ 1) for i in range(slabs)]
    cross = [(i, (i - 1 if i % 2 == 0 else i + 1) % slabs) for i in range(slabs)]

    def over_chip(value):
        return lax.ppermute(value, "blk", pairs)

    def over_link(value):
        return lax.ppermute(value, "blk", cross)

    def swap(value, step):
        return lax.ppermute(value, "col", [(i, i ^ step) for i in range(4)])

    cols = block_cols.T
    flat = basis.transpose(1, 0, 2)
    reach = patch_reach.transpose(0, 2, 1)
    inner_rows = (blocks - 2 * RIM) * size
    rim = RIM * size
    row_flops = 2 * slots * size * size * wide
    masked, rim_link, rim_chip, inner = call(
        functools.partial(mask_and_inner, total_blocks),
        (shape((rows, wide), BF16), shape((rim, 2 * width), BF16), shape((rim, 2 * width), BF16), shape((inner_rows, wide), BF16)),
        [HBM] * 4,
        [VMEM] * 4,
        (cols, flat, reach, stiffness),
        scratch=[
            pltpu.SMEM(cols.shape, cols.dtype),
            pltpu.VMEM(flat.shape, BF16),
            pltpu.VMEM(reach.shape, reach.dtype),
            pltpu.VMEM(stiffness.shape, BF16),
            pltpu.SemaphoreType.DMA((4,)),
        ],
        flops=row_flops * (blocks - 2 * RIM),
        vmem=53248,
        name="mask_and_inner",
    )
    inner_x = swap(inner, 1)
    inner_y = swap(inner, 2)
    rim_link = over_link(rim_link)
    rim_chip = over_chip(rim_chip)
    outer = call(
        functools.partial(outer_image, total_blocks),
        shape((2 * rim, wide), BF16),
        [SMEM] + [VMEM] * 4,
        VMEM,
        (cols, stiffness, masked, rim_link, rim_chip),
        scratch=[pltpu.VMEM((rows + 2 * rim, wide), BF16)],
        flops=row_flops * 2 * RIM,
        name="outer_image",
    )
    outer_x = swap(outer, 1)
    outer_y = swap(outer, 2)
    tile_flops = 2 * rows * wide * wide
    own_own, own_link, own_chip, left_inner, left_outer = call(
        functools.partial(own_tile, size),
        (*tile_shapes(1, width, wide), shape((wide, inner_rows), BF16), shape((wide, 2 * rim), BF16)),
        [VMEM] * 3,
        [VMEM] * 5,
        (masked, inner, outer),
        flops=tile_flops,
        name="own_tile",
    )
    own_link = over_link(own_link)
    own_chip = over_chip(own_chip)
    half = inner_rows // 2
    inner_d = (swap(inner_y[:half], 1), swap(inner_x[half:], 2))
    outer_x, outer_y, own_link, own_chip = lax.optimization_barrier((outer_x, outer_y, own_link, own_chip))
    diagonal = (*inner_d, swap(outer_y[:rim], 1), swap(outer_x[rim:], 2))
    near_own, near_link, near_chip = call(
        near_tiles,
        tile_shapes(2, width, wide),
        [VMEM] * 6,
        [VMEM] * 3,
        (left_inner, left_outer, inner_x, outer_x, inner_y, outer_y),
        flops=2 * tile_flops,
        name="near_tiles",
    )
    near_link = over_link(near_link)
    near_chip = over_chip(near_chip)
    far_own, far_link, far_chip = call(
        diagonal_tile,
        tile_shapes(1, width, wide),
        [VMEM] * 6,
        [VMEM] * 3,
        (left_inner, left_outer, *diagonal),
        flops=tile_flops,
        name="diagonal_tile",
    )
    far_link = over_link(far_link)
    far_chip = over_chip(far_chip)

    def add(sources, terms, name, base=None):
        count = sum(map(len, sources))
        extra = () if base is None else (base,)
        return call(
            functools.partial(add_tiles, sources),
            shape((5, width, 4 * width), F32),
            [VMEM] * len(terms) + [HBM] * len(extra),
            HBM,
            (*terms, *extra),
            scratch=[pltpu.VMEM((count, 5, width, width), F32), pltpu.SemaphoreType.DMA((count,))],
            flops=5 * count * width * width,
            aliases={len(terms): 0} if extra else None,
            name=name,
        )

    coarse = add(((0,), (1, 2)), (own_own, own_link, own_chip, near_own, near_link, near_chip), "add_near")
    coarse = add(((3,),), (far_own, far_link, far_chip), "add_diagonal", coarse)
    return coarse.transpose(1, 0, 2)


def gathered(stiffness, block_cols, basis, patch_reach):
    blocks, slots, size, _ = stiffness.shape
    rows, groups, width = basis.shape
    slabs = lax.axis_size("blk")
    slab = lax.axis_index("blk")
    total_blocks = blocks * slabs
    ring = [(i, (i + 1) % slabs) for i in range(slabs)]
    back = [(j, i) for i, j in ring]
    low = lax.dynamic_index_in_dim(patch_reach, (slab - 1) % slabs, 0, False)[:, 1]
    high = lax.dynamic_index_in_dim(patch_reach, (slab + 1) % slabs, 0, False)[:, 0]
    block_row = jnp.arange(rows, dtype=jnp.int32) // size
    lower = block_row[:, None] < low[None, :]
    upper = block_row[:, None] >= blocks - high[None, :]
    support = jnp.stack([lower, jnp.ones_like(lower), upper], 1)
    masked = jnp.where(support, basis, jnp.zeros_like(basis))
    rim = RIM * size
    before = lax.ppermute(masked[rows - rim :, 1:], "blk", ring)
    after = lax.ppermute(masked[:rim, :2], "blk", back)
    none = jnp.zeros((rim, 1, width), masked.dtype)
    extended = jnp.concatenate(
        [jnp.concatenate([before, none], 1), masked, jnp.concatenate([none, after], 1)], 0
    ).reshape(blocks + 2 * RIM, size, groups * width)
    position = (block_cols - slab * blocks + RIM) % total_blocks
    picked = jnp.take(extended, position, axis=0)
    image = jnp.einsum("rsij,rsjc->ric", stiffness, picked, preferred_element_type=F32)
    image = image.astype(BF16).reshape(rows, groups, width)
    image = lax.all_gather(image, "col", axis=2, tiled=True)
    tiles = jnp.einsum("rgl,rhc->glhc", masked, image, preferred_element_type=F32)
    from_prev = lax.ppermute(tiles[2], "blk", ring)
    from_next = lax.ppermute(tiles[0], "blk", back)

    def place(tile, offset):
        return jnp.pad(tile, ((0, 0), (offset, 2 - offset), (0, 0)))

    return place(from_prev, 0) + place(tiles[1], 1) + place(from_next, 2)


def solution(mesh):
    in_specs = (
        P("blk", None, None, None),
        P("blk", None),
        P("blk", None, "col"),
        P(None, "col", None),
    )
    out_specs = P(("blk", "col"), None, None)
    body = shards if mesh.shape["col"] == 4 else gathered
    return jax.shard_map(body, mesh=mesh, in_specs=in_specs, out_specs=out_specs, check_vma=False)
```

```python
import functools

import jax
import jax.numpy as jnp
from jax import lax
from jax.experimental import pallas as pl
from jax.experimental.pallas import tpu as pltpu
from jax.sharding import PartitionSpec as P

BF16 = jnp.bfloat16
F32 = jnp.float32
VMEM = pl.BlockSpec(memory_space=pltpu.VMEM)
SMEM = pl.BlockSpec(memory_space=pltpu.SMEM)
HBM = pl.BlockSpec(memory_space=pltpu.HBM)
RIM = 2


def shape(dims, dtype):
    return jax.ShapeDtypeStruct(dims, dtype)


def dot(left, right):
    return jnp.dot(left, right, preferred_element_type=F32)


def call(kernel, out_shape, in_specs, out_specs, args, scratch=(), flops=0, aliases=None, name=None):
    outs = jax.tree.leaves(out_shape)
    moved = sum(x.size * x.dtype.itemsize for x in (*args, *outs))
    return pl.pallas_call(
        kernel,
        out_shape=out_shape,
        in_specs=in_specs,
        out_specs=out_specs,
        scratch_shapes=list(scratch),
        input_output_aliases=aliases or {},
        cost_estimate=pl.CostEstimate(flops=flops, bytes_accessed=moved, transcendentals=0),
        compiler_params=pltpu.CompilerParams(vmem_limit_bytes=24 << 20),
        name=name,
    )(*args)


def block_image(stiffness, source, b, block_size, starts):
    blocks = [source[pl.ds(pl.multiple_of(start * block_size, block_size), block_size), :] for start in starts]
    left = jnp.concatenate([stiffness[b, k] for k in range(len(starts))], axis=1)
    return dot(left, jnp.concatenate(blocks, axis=0)).astype(BF16)


def positions(cols, b, blocks, slots, total_blocks):
    first = lax.axis_index("blk") * blocks
    return [
        jnp.clip(lax.rem(cols[k, b] - first + RIM + total_blocks, total_blocks), 0, blocks + 2 * RIM - 1)
        for k in range(slots)
    ]


def mask_and_inner(
    total_blocks, cols_hbm, basis_hbm, reach_hbm, stiffness_hbm, masked, to_link, to_chip, inner, cols, basis, reach, stiffness, sem
):
    blocks, slots, size, _ = stiffness.shape
    groups, _, width = basis.shape
    slabs = reach.shape[0]
    slab = lax.axis_index("blk")
    inner_blocks = pl.ds(RIM, blocks - 2 * RIM)
    moves = [(reach_hbm, reach), (cols_hbm, cols)]
    moves += [
        (basis_hbm.at[:, pl.ds(b * size, RIM * size)], basis.at[:, pl.ds(b * size, RIM * size)])
        for b in range(0, blocks, RIM)
    ]
    moves.append((stiffness_hbm.at[inner_blocks], stiffness.at[inner_blocks]))
    copies = [pltpu.make_async_copy(source, target, sem.at[n]) for n, (source, target) in enumerate(moves)]
    for copy in copies:
        copy.start()
    copies[0].wait()
    low = reach[pl.ds(lax.rem(slab + slabs - 1, slabs), 1), 1, :]
    high = reach[pl.ds(lax.rem(slab + 1, slabs), 1), 0, :]
    for b in range(blocks):
        if b % RIM == 0:
            copies[2 + b // RIM].wait()
        rows = slice(b * size, (b + 1) * size)
        keep = {0: (b < low).astype(F32).astype(BF16), 2: (b >= blocks - high).astype(F32).astype(BF16)}
        for g in range(groups):
            value = basis[g, rows, :]
            masked[rows, g * width : (g + 1) * width] = value * keep[g] if g in keep else value
    odd = parity()

    @pl.when(odd == 0)
    def _():
        to_link[...] = masked[: RIM * size, : 2 * width]
        to_chip[...] = masked[(blocks - RIM) * size :, width:]

    @pl.when(odd == 1)
    def _():
        to_link[...] = masked[(blocks - RIM) * size :, width:]
        to_chip[...] = masked[: RIM * size, : 2 * width]

    copies[1].wait()
    copies[-1].wait()
    for b in range(RIM, blocks - RIM):
        starts = [jnp.clip(p - RIM, 0, blocks - 1) for p in positions(cols, b, blocks, slots, total_blocks)]
        inner[(b - RIM) * size : (b - RIM + 1) * size, :] = block_image(stiffness, masked, b, size, starts)


def outer_image(total_blocks, cols, stiffness, masked, from_link, from_chip, outer, extended):
    blocks, slots, size, _ = stiffness.shape
    rows, wide = masked.shape
    rim = RIM * size
    width = wide // 3
    odd = parity()

    @pl.when(odd == 0)
    def _():
        extended[:rim, : 2 * width] = from_link[...]
        extended[rim + rows :, width:] = from_chip[...]

    @pl.when(odd == 1)
    def _():
        extended[:rim, : 2 * width] = from_chip[...]
        extended[rim + rows :, width:] = from_link[...]

    extended[:rim, 2 * width :] = jnp.zeros((rim, width), BF16)
    extended[rim : rim + rows, :] = masked[...]
    extended[rim + rows :, :width] = jnp.zeros((rim, width), BF16)
    for n, b in enumerate([*range(RIM), *range(blocks - RIM, blocks)]):
        starts = positions(cols, b, blocks, slots, total_blocks)
        outer[n * size : (n + 1) * size, :] = block_image(stiffness, extended, b, size, starts)


def parity():
    return lax.rem(lax.axis_index("blk"), 2)


def store_tile(tile, own, link, chip, n):
    width = own.shape[1]
    odd = parity()
    own[n] = tile[width : 2 * width]
    down, up = tile[:width].astype(BF16), tile[2 * width :].astype(BF16)

    @pl.when(odd == 0)
    def _():
        link[n] = down
        chip[n] = up

    @pl.when(odd == 1)
    def _():
        link[n] = up
        chip[n] = down


def own_tile(size, masked, inner, outer, own, link, chip, left_inner, left_outer):
    rows = masked.shape[0]
    rim = RIM * size
    left_inner[...] = masked[rim : rows - rim, :].T
    left_outer[:, :rim] = masked[:rim, :].T
    left_outer[:, rim:] = masked[rows - rim :, :].T
    store_tile(dot(left_inner[...], inner[...]) + dot(left_outer[...], outer[...]), own, link, chip, 0)


def near_tiles(left_inner, left_outer, *refs):
    images, (own, link, chip) = refs[:-3], refs[-3:]
    for n in range(len(images) // 2):
        tile = dot(left_inner[...], images[2 * n][...]) + dot(left_outer[...], images[2 * n + 1][...])
        store_tile(tile, own, link, chip, n)


def diagonal_tile(left_inner, left_outer, *refs):
    images, (own, link, chip) = refs[:-3], refs[-3:]
    tile = None
    for which, left in ((0, left_inner), (1, left_outer)):
        first, second = images[2 * which], images[2 * which + 1]
        half = first.shape[0]
        part = dot(left[:, :half], first[...]) + dot(left[:, half:], second[...])
        tile = part if tile is None else tile + part
    store_tile(tile, own, link, chip, 0)


def add_tiles(sources, *refs):
    count = len(sources)
    terms, refs = refs[: 3 * count], refs[3 * count :]
    coarse, total, sem = refs[-3:]
    width = total.shape[2]
    me = lax.axis_index("col")
    even = parity() == 0
    copies = []
    n = 0
    for group, source in enumerate(sources):
        own, link, chip = terms[3 * group : 3 * group + 3]
        for m, step in enumerate(source):
            prev = jnp.where(even, link[m].astype(F32), chip[m].astype(F32))
            nxt = jnp.where(even, chip[m].astype(F32), link[m].astype(F32))
            for d in range(5):
                value = None
                for offset, term in ((0, prev), (1, own[m]), (2, nxt)):
                    if 0 <= d - offset <= 2:
                        part = term[:, (d - offset) * width : (d - offset + 1) * width]
                        value = part if value is None else value + part
                total[n, d] = value
            start = pl.multiple_of(lax.bitwise_xor(me, step) * width, width)
            copy = pltpu.make_async_copy(total.at[n], coarse.at[:, :, pl.ds(start, width)], sem.at[n])
            copy.start()
            copies.append(copy)
            n += 1
    for copy in copies:
        copy.wait()


def tile_shapes(count, width, wide):
    return (
        shape((count, width, wide), F32),
        shape((count, width, wide), BF16),
        shape((count, width, wide), BF16),
    )


def shards(stiffness, block_cols, basis, patch_reach):
    blocks, slots, size, _ = stiffness.shape
    rows, groups, width = basis.shape
    wide = groups * width
    slabs = lax.axis_size("blk")
    total_blocks = blocks * slabs
    pairs = [(i, i ^ 1) for i in range(slabs)]
    cross = [(i, (i - 1 if i % 2 == 0 else i + 1) % slabs) for i in range(slabs)]

    def over_chip(value):
        return lax.ppermute(value, "blk", pairs)

    def over_link(value):
        return lax.ppermute(value, "blk", cross)

    def swap(value, step):
        return lax.ppermute(value, "col", [(i, i ^ step) for i in range(4)])

    cols = block_cols.T
    flat = basis.transpose(1, 0, 2)
    reach = patch_reach.transpose(0, 2, 1)
    inner_rows = (blocks - 2 * RIM) * size
    rim = RIM * size
    row_flops = 2 * slots * size * size * wide
    masked, rim_link, rim_chip, inner = call(
        functools.partial(mask_and_inner, total_blocks),
        (shape((rows, wide), BF16), shape((rim, 2 * width), BF16), shape((rim, 2 * width), BF16), shape((inner_rows, wide), BF16)),
        [HBM] * 4,
        [VMEM] * 4,
        tuple(pltpu.with_memory_space_constraint(x, pltpu.HBM) for x in (cols, flat, reach, stiffness)),
        scratch=[
            pltpu.SMEM(cols.shape, cols.dtype),
            pltpu.VMEM(flat.shape, BF16),
            pltpu.VMEM(reach.shape, reach.dtype),
            pltpu.VMEM(stiffness.shape, BF16),
            pltpu.SemaphoreType.DMA((3 + blocks // RIM,)),
        ],
        flops=row_flops * (blocks - 2 * RIM),
        name="mask_and_inner",
    )
    inner_x = swap(inner, 1)
    inner_y = swap(inner, 2)
    rim_link = over_link(rim_link)
    rim_chip = over_chip(rim_chip)
    outer = call(
        functools.partial(outer_image, total_blocks),
        shape((2 * rim, wide), BF16),
        [SMEM] + [VMEM] * 4,
        VMEM,
        (cols, stiffness, masked, rim_link, rim_chip),
        scratch=[pltpu.VMEM((rows + 2 * rim, wide), BF16)],
        flops=row_flops * 2 * RIM,
        name="outer_image",
    )
    outer_x = swap(outer, 1)
    outer_y = swap(outer, 2)
    tile_flops = 2 * rows * wide * wide
    own_own, own_link, own_chip, left_inner, left_outer = call(
        functools.partial(own_tile, size),
        (*tile_shapes(1, width, wide), shape((wide, inner_rows), BF16), shape((wide, 2 * rim), BF16)),
        [VMEM] * 3,
        [VMEM] * 5,
        (masked, inner, outer),
        flops=tile_flops,
        name="own_tile",
    )
    own_link = over_link(own_link)
    own_chip = over_chip(own_chip)
    half = inner_rows // 2
    inner_d = (swap(inner_y[:half], 1), swap(inner_x[half:], 2))
    outer_x, outer_y, own_link, own_chip = lax.optimization_barrier((outer_x, outer_y, own_link, own_chip))
    diagonal = (*inner_d, swap(outer_y[:rim], 1), swap(outer_x[rim:], 2))
    near_own, near_link, near_chip = call(
        near_tiles,
        tile_shapes(2, width, wide),
        [VMEM] * 6,
        [VMEM] * 3,
        (left_inner, left_outer, inner_x, outer_x, inner_y, outer_y),
        flops=2 * tile_flops,
        name="near_tiles",
    )
    near_link = over_link(near_link)
    near_chip = over_chip(near_chip)
    far_own, far_link, far_chip = call(
        diagonal_tile,
        tile_shapes(1, width, wide),
        [VMEM] * 6,
        [VMEM] * 3,
        (left_inner, left_outer, *diagonal),
        flops=tile_flops,
        name="diagonal_tile",
    )
    far_link = over_link(far_link)
    far_chip = over_chip(far_chip)

    def add(sources, terms, name, base=None):
        count = sum(map(len, sources))
        extra = () if base is None else (base,)
        return call(
            functools.partial(add_tiles, sources),
            shape((5, width, 4 * width), F32),
            [VMEM] * len(terms) + [HBM] * len(extra),
            HBM,
            (*terms, *extra),
            scratch=[pltpu.VMEM((count, 5, width, width), F32), pltpu.SemaphoreType.DMA((count,))],
            flops=5 * count * width * width,
            aliases={len(terms): 0} if extra else None,
            name=name,
        )

    coarse = add(((0,), (1, 2)), (own_own, own_link, own_chip, near_own, near_link, near_chip), "add_near")
    coarse = add(((3,),), (far_own, far_link, far_chip), "add_diagonal", coarse)
    return coarse.transpose(1, 0, 2)


def gathered(stiffness, block_cols, basis, patch_reach):
    blocks, slots, size, _ = stiffness.shape
    rows, groups, width = basis.shape
    slabs = lax.axis_size("blk")
    slab = lax.axis_index("blk")
    total_blocks = blocks * slabs
    ring = [(i, (i + 1) % slabs) for i in range(slabs)]
    back = [(j, i) for i, j in ring]
    low = lax.dynamic_index_in_dim(patch_reach, (slab - 1) % slabs, 0, False)[:, 1]
    high = lax.dynamic_index_in_dim(patch_reach, (slab + 1) % slabs, 0, False)[:, 0]
    block_row = jnp.arange(rows, dtype=jnp.int32) // size
    lower = block_row[:, None] < low[None, :]
    upper = block_row[:, None] >= blocks - high[None, :]
    support = jnp.stack([lower, jnp.ones_like(lower), upper], 1)
    masked = jnp.where(support, basis, jnp.zeros_like(basis))
    rim = RIM * size
    before = lax.ppermute(masked[rows - rim :, 1:], "blk", ring)
    after = lax.ppermute(masked[:rim, :2], "blk", back)
    none = jnp.zeros((rim, 1, width), masked.dtype)
    extended = jnp.concatenate(
        [jnp.concatenate([before, none], 1), masked, jnp.concatenate([none, after], 1)], 0
    ).reshape(blocks + 2 * RIM, size, groups * width)
    position = (block_cols - slab * blocks + RIM) % total_blocks
    picked = jnp.take(extended, position, axis=0)
    image = jnp.einsum("rsij,rsjc->ric", stiffness, picked, preferred_element_type=F32)
    image = image.astype(BF16).reshape(rows, groups, width)
    image = lax.all_gather(image, "col", axis=2, tiled=True)
    tiles = jnp.einsum("rgl,rhc->glhc", masked, image, preferred_element_type=F32)
    from_prev = lax.ppermute(tiles[2], "blk", ring)
    from_next = lax.ppermute(tiles[0], "blk", back)

    def place(tile, offset):
        return jnp.pad(tile, ((0, 0), (offset, 2 - offset), (0, 0)))

    return place(from_prev, 0) + place(tiles[1], 1) + place(from_next, 2)


def solution(mesh):
    in_specs = (
        P("blk", None, None, None),
        P("blk", None),
        P("blk", None, "col"),
        P(None, "col", None),
    )
    out_specs = P(("blk", "col"), None, None)
    body = shards if mesh.shape["col"] == 4 else gathered
    return jax.shard_map(body, mesh=mesh, in_specs=in_specs, out_specs=out_specs, check_vma=False)
```

```python
import functools

import jax
import jax.numpy as jnp
from jax import lax
from jax.experimental import pallas as pl
from jax.experimental.pallas import tpu as pltpu
from jax.sharding import PartitionSpec as P

BF16 = jnp.bfloat16
F32 = jnp.float32
VMEM = pl.BlockSpec(memory_space=pltpu.VMEM)
SMEM = pl.BlockSpec(memory_space=pltpu.SMEM)
HBM = pl.BlockSpec(memory_space=pltpu.HBM)
RIM = 2


def shape(dims, dtype):
    return jax.ShapeDtypeStruct(dims, dtype)


def dot(left, right):
    return jnp.dot(left, right, preferred_element_type=F32)


def call(kernel, out_shape, in_specs, out_specs, args, scratch=(), flops=0, aliases=None, name=None):
    outs = jax.tree.leaves(out_shape)
    moved = sum(x.size * x.dtype.itemsize for x in (*args, *outs))
    return pl.pallas_call(
        kernel,
        out_shape=out_shape,
        in_specs=in_specs,
        out_specs=out_specs,
        scratch_shapes=list(scratch),
        input_output_aliases=aliases or {},
        cost_estimate=pl.CostEstimate(flops=flops, bytes_accessed=moved, transcendentals=0),
        compiler_params=pltpu.CompilerParams(vmem_limit_bytes=24 << 20),
        name=name,
    )(*args)


def block_image(stiffness, source, b, block_size, starts):
    blocks = [source[pl.ds(pl.multiple_of(start * block_size, block_size), block_size), :] for start in starts]
    left = jnp.concatenate([stiffness[b, k] for k in range(len(starts))], axis=1)
    return dot(left, jnp.concatenate(blocks, axis=0)).astype(BF16)


def positions(cols, b, blocks, slots, total_blocks):
    first = lax.axis_index("blk") * blocks
    return [
        jnp.clip(lax.rem(cols[k, b] - first + RIM + total_blocks, total_blocks), 0, blocks + 2 * RIM - 1)
        for k in range(slots)
    ]


def mask_and_inner(
    total_blocks, cols_hbm, basis_hbm, reach_hbm, stiffness_hbm, masked, to_link, to_chip, inner, cols, basis, reach, stiffness, sem
):
    blocks, slots, size, _ = stiffness.shape
    groups, _, width = basis.shape
    slabs = reach.shape[0]
    slab = lax.axis_index("blk")
    inner_blocks = pl.ds(RIM, blocks - 2 * RIM)
    moves = [(reach_hbm, reach), (cols_hbm, cols)]
    moves += [
        (basis_hbm.at[:, pl.ds(b * size, RIM * size)], basis.at[:, pl.ds(b * size, RIM * size)])
        for b in range(0, blocks, RIM)
    ]
    moves.append((stiffness_hbm.at[inner_blocks], stiffness.at[inner_blocks]))
    copies = [pltpu.make_async_copy(source, target, sem.at[n]) for n, (source, target) in enumerate(moves)]
    for copy in copies:
        copy.start()
    copies[0].wait()
    low = reach[pl.ds(lax.rem(slab + slabs - 1, slabs), 1), 1, :]
    high = reach[pl.ds(lax.rem(slab + 1, slabs), 1), 0, :]
    for b in range(blocks):
        if b % RIM == 0:
            copies[2 + b // RIM].wait()
        rows = slice(b * size, (b + 1) * size)
        keep = {0: (b < low).astype(F32).astype(BF16), 2: (b >= blocks - high).astype(F32).astype(BF16)}
        for g in range(groups):
            value = basis[g, rows, :]
            masked[rows, g * width : (g + 1) * width] = value * keep[g] if g in keep else value
    odd = parity()

    @pl.when(odd == 0)
    def _():
        to_link[...] = masked[: RIM * size, : 2 * width]
        to_chip[...] = masked[(blocks - RIM) * size :, width:]

    @pl.when(odd == 1)
    def _():
        to_link[...] = masked[(blocks - RIM) * size :, width:]
        to_chip[...] = masked[: RIM * size, : 2 * width]

    copies[1].wait()
    copies[-1].wait()
    for b in range(RIM, blocks - RIM):
        starts = [jnp.clip(p - RIM, 0, blocks - 1) for p in positions(cols, b, blocks, slots, total_blocks)]
        inner[(b - RIM) * size : (b - RIM + 1) * size, :] = block_image(stiffness, masked, b, size, starts)


def outer_image(total_blocks, cols, stiffness, masked, from_link, from_chip, outer, extended):
    blocks, slots, size, _ = stiffness.shape
    rows, wide = masked.shape
    rim = RIM * size
    width = wide // 3
    odd = parity()

    @pl.when(odd == 0)
    def _():
        extended[:rim, : 2 * width] = from_link[...]
        extended[rim + rows :, width:] = from_chip[...]

    @pl.when(odd == 1)
    def _():
        extended[:rim, : 2 * width] = from_chip[...]
        extended[rim + rows :, width:] = from_link[...]

    extended[:rim, 2 * width :] = jnp.zeros((rim, width), BF16)
    extended[rim : rim + rows, :] = masked[...]
    extended[rim + rows :, :width] = jnp.zeros((rim, width), BF16)
    for n, b in enumerate([*range(RIM), *range(blocks - RIM, blocks)]):
        starts = positions(cols, b, blocks, slots, total_blocks)
        outer[n * size : (n + 1) * size, :] = block_image(stiffness, extended, b, size, starts)


def parity():
    return lax.rem(lax.axis_index("blk"), 2)


def store_tile(tile, own, link, chip):
    width = own.shape[0]
    odd = parity()
    own[...] = tile[width : 2 * width].astype(own.dtype)
    down, up = tile[:width].astype(BF16), tile[2 * width :].astype(BF16)

    @pl.when(odd == 0)
    def _():
        link[...] = down
        chip[...] = up

    @pl.when(odd == 1)
    def _():
        link[...] = up
        chip[...] = down


def first_tile(size, masked, inner, outer, own, link, chip, left_inner, left_outer):
    rows = masked.shape[0]
    rim = RIM * size
    left_inner[...] = masked[rim : rows - rim, :].T
    left_outer[:, :rim] = masked[:rim, :].T
    left_outer[:, rim:] = masked[rows - rim :, :].T
    second_tile(left_inner, left_outer, inner, outer, own, link, chip)


def second_tile(left_inner, left_outer, inner, outer, own, link, chip):
    store_tile(dot(left_inner[...], inner[...]) + dot(left_outer[...], outer[...]), own, link, chip)


def add_tiles(steps, *refs):
    count = len(steps)
    terms = refs[: 3 * count]
    coarse, total, sem = refs[-3:]
    width = total.shape[2]
    me = lax.axis_index("col")
    even = parity() == 0
    copies = []
    for n, (even_step, odd_step) in enumerate(steps):
        own, link, chip = (ref[...].astype(F32) for ref in terms[3 * n : 3 * n + 3])
        prev = jnp.where(even, link, chip)
        nxt = jnp.where(even, chip, link)
        for d in range(5):
            value = None
            for offset, term in ((0, prev), (1, own), (2, nxt)):
                if 0 <= d - offset <= 2:
                    part = term[:, (d - offset) * width : (d - offset + 1) * width]
                    value = part if value is None else value + part
            total[n, d] = value
        column = lax.bitwise_xor(me, jnp.where(even, even_step, odd_step))
        start = pl.multiple_of(column * width, width)
        copy = pltpu.make_async_copy(total.at[n], coarse.at[:, :, pl.ds(start, width)], sem.at[n])
        copy.start()
        copies.append(copy)
    for copy in copies:
        copy.wait()


def tile_shapes(width, wide, own):
    return shape((width, wide), own), shape((width, wide), BF16), shape((width, wide), BF16)


def shards(stiffness, block_cols, basis, patch_reach):
    blocks, slots, size, _ = stiffness.shape
    rows, groups, width = basis.shape
    wide = groups * width
    slabs = lax.axis_size("blk")
    total_blocks = blocks * slabs
    pairs = [(i, i ^ 1) for i in range(slabs)]
    cross = [(i, (i - 1 if i % 2 == 0 else i + 1) % slabs) for i in range(slabs)]

    def over_chip(value):
        return lax.ppermute(value, "blk", pairs)

    def over_link(value):
        return lax.ppermute(value, "blk", cross)

    def to(value, slab_of, column_of):
        perm = [(4 * i + q, 4 * (slab_of(i) % slabs) + column_of(i, q)) for i in range(slabs) for q in range(4)]
        return lax.ppermute(value, ("blk", "col"), perm)

    def partner(i, q):
        return q ^ (1 + i % 2)

    def side(i, q):
        return q ^ (2 - i % 2)

    def to_partner(value):
        return to(value, lambda i: i, partner)

    def to_side(value):
        return to(value, lambda i: i, side)

    def spread(own, link, chip):
        own = to_partner(own)
        link = to(link, lambda i: i + 1 if i % 2 else i - 1, partner)
        chip = to(chip, lambda i: i ^ 1, partner)
        return own, link, chip

    cols = block_cols.T
    flat = basis.transpose(1, 0, 2)
    reach = patch_reach.transpose(0, 2, 1)
    inner_rows = (blocks - 2 * RIM) * size
    rim = RIM * size
    row_flops = 2 * slots * size * size * wide
    masked, rim_link, rim_chip, inner = call(
        functools.partial(mask_and_inner, total_blocks),
        (shape((rows, wide), BF16), shape((rim, 2 * width), BF16), shape((rim, 2 * width), BF16), shape((inner_rows, wide), BF16)),
        [HBM] * 4,
        [VMEM] * 4,
        tuple(pltpu.with_memory_space_constraint(x, pltpu.HBM) for x in (cols, flat, reach, stiffness)),
        scratch=[
            pltpu.SMEM(cols.shape, cols.dtype),
            pltpu.VMEM(flat.shape, BF16),
            pltpu.VMEM(reach.shape, reach.dtype),
            pltpu.VMEM(stiffness.shape, BF16),
            pltpu.SemaphoreType.DMA((3 + blocks // RIM,)),
        ],
        flops=row_flops * (blocks - 2 * RIM),
        name="mask_and_inner",
    )
    masked_p = to_partner(masked)
    inner_r = to_side(inner)
    rim_link = over_link(rim_link)
    rim_chip = over_chip(rim_chip)
    outer = call(
        functools.partial(outer_image, total_blocks),
        shape((2 * rim, wide), BF16),
        [SMEM] + [VMEM] * 4,
        VMEM,
        (cols, stiffness, masked, rim_link, rim_chip),
        scratch=[pltpu.VMEM((rows + 2 * rim, wide), BF16)],
        flops=row_flops * 2 * RIM,
        name="outer_image",
    )
    outer_r = to_side(outer)
    tile_flops = 2 * rows * wide * wide
    lefts = (shape((wide, inner_rows), BF16), shape((wide, 2 * rim), BF16))

    def first(masked, own, name):
        return call(
            functools.partial(first_tile, size),
            (*tile_shapes(width, wide, own), *lefts),
            [VMEM] * 3,
            [VMEM] * 5,
            (masked, inner, outer),
            flops=tile_flops,
            name=name,
        )

    def second(left_inner, left_outer, own, name):
        return call(
            second_tile,
            tile_shapes(width, wide, own),
            [VMEM] * 4,
            [VMEM] * 3,
            (left_inner, left_outer, inner_r, outer_r),
            flops=tile_flops,
            name=name,
        )

    own, own_link, own_chip, left_inner, left_outer = first(masked, F32, "own_tile")
    own_link, own_chip = over_link(own_link), over_chip(own_chip)
    *part, far_inner, far_outer = first(masked_p, BF16, "partner_tile")
    outer_r, _ = lax.optimization_barrier((outer_r, part[1]))
    part, part_link, part_chip = spread(*part)
    far, far_link, far_chip = spread(*second(far_inner, far_outer, BF16, "far_tile"))
    near, near_link, near_chip = second(left_inner, left_outer, F32, "near_tile")
    near_link, near_chip = over_link(near_link), over_chip(near_chip)

    def add(steps, terms, name, base=None):
        extra = () if base is None else (base,)
        return call(
            functools.partial(add_tiles, steps),
            shape((5, width, 4 * width), F32),
            [VMEM] * len(terms) + [HBM] * len(extra),
            HBM,
            (*terms, *extra),
            scratch=[pltpu.VMEM((len(steps), 5, width, width), F32), pltpu.SemaphoreType.DMA((len(steps),))],
            flops=5 * len(steps) * width * width,
            aliases={len(terms): 0} if extra else None,
            name=name,
        )

    coarse = add(((0, 0),), (own, own_link, own_chip), "add_own")
    coarse = add(
        ((2, 1), (1, 2), (3, 3)),
        (near, part_link, part_chip, part, near_link, near_chip, far, far_link, far_chip),
        "add_rest",
        coarse,
    )
    return coarse.transpose(1, 0, 2)


def gathered(stiffness, block_cols, basis, patch_reach):
    blocks, slots, size, _ = stiffness.shape
    rows, groups, width = basis.shape
    slabs = lax.axis_size("blk")
    slab = lax.axis_index("blk")
    total_blocks = blocks * slabs
    ring = [(i, (i + 1) % slabs) for i in range(slabs)]
    back = [(j, i) for i, j in ring]
    low = lax.dynamic_index_in_dim(patch_reach, (slab - 1) % slabs, 0, False)[:, 1]
    high = lax.dynamic_index_in_dim(patch_reach, (slab + 1) % slabs, 0, False)[:, 0]
    block_row = jnp.arange(rows, dtype=jnp.int32) // size
    lower = block_row[:, None] < low[None, :]
    upper = block_row[:, None] >= blocks - high[None, :]
    support = jnp.stack([lower, jnp.ones_like(lower), upper], 1)
    masked = jnp.where(support, basis, jnp.zeros_like(basis))
    rim = RIM * size
    before = lax.ppermute(masked[rows - rim :, 1:], "blk", ring)
    after = lax.ppermute(masked[:rim, :2], "blk", back)
    none = jnp.zeros((rim, 1, width), masked.dtype)
    extended = jnp.concatenate(
        [jnp.concatenate([before, none], 1), masked, jnp.concatenate([none, after], 1)], 0
    ).reshape(blocks + 2 * RIM, size, groups * width)
    position = (block_cols - slab * blocks + RIM) % total_blocks
    picked = jnp.take(extended, position, axis=0)
    image = jnp.einsum("rsij,rsjc->ric", stiffness, picked, preferred_element_type=F32)
    image = image.astype(BF16).reshape(rows, groups, width)
    image = lax.all_gather(image, "col", axis=2, tiled=True)
    tiles = jnp.einsum("rgl,rhc->glhc", masked, image, preferred_element_type=F32)
    from_prev = lax.ppermute(tiles[2], "blk", ring)
    from_next = lax.ppermute(tiles[0], "blk", back)

    def place(tile, offset):
        return jnp.pad(tile, ((0, 0), (offset, 2 - offset), (0, 0)))

    return place(from_prev, 0) + place(tiles[1], 1) + place(from_next, 2)


def solution(mesh):
    in_specs = (
        P("blk", None, None, None),
        P("blk", None),
        P("blk", None, "col"),
        P(None, "col", None),
    )
    out_specs = P(("blk", "col"), None, None)
    body = shards if mesh.shape["col"] == 4 and mesh.shape["blk"] % 2 == 0 else gathered
    return jax.shard_map(body, mesh=mesh, in_specs=in_specs, out_specs=out_specs, check_vma=False)
```

```python
import functools

import jax
import jax.numpy as jnp
from jax import lax
from jax.experimental import pallas as pl
from jax.experimental.pallas import tpu as pltpu
from jax.sharding import PartitionSpec as P

BF16 = jnp.bfloat16
F32 = jnp.float32
VMEM = pl.BlockSpec(memory_space=pltpu.VMEM)
SMEM = pl.BlockSpec(memory_space=pltpu.SMEM)
HBM = pl.BlockSpec(memory_space=pltpu.HBM)
RIM = 2


def shape(dims, dtype):
    return jax.ShapeDtypeStruct(dims, dtype)


def dot(left, right):
    return jnp.dot(left, right, preferred_element_type=F32)


def call(kernel, out_shape, in_specs, out_specs, args, scratch=(), flops=0, aliases=None, name=None):
    outs = jax.tree.leaves(out_shape)
    moved = sum(x.size * x.dtype.itemsize for x in (*args, *outs))
    return pl.pallas_call(
        kernel,
        out_shape=out_shape,
        in_specs=in_specs,
        out_specs=out_specs,
        scratch_shapes=list(scratch),
        input_output_aliases=aliases or {},
        cost_estimate=pl.CostEstimate(flops=flops, bytes_accessed=moved, transcendentals=0),
        compiler_params=pltpu.CompilerParams(vmem_limit_bytes=24 << 20),
        name=name,
    )(*args)


def block_image(stiffness, source, b, block_size, starts):
    blocks = [source[pl.ds(pl.multiple_of(start * block_size, block_size), block_size), :] for start in starts]
    left = jnp.concatenate([stiffness[b, k] for k in range(len(starts))], axis=1)
    return dot(left, jnp.concatenate(blocks, axis=0)).astype(BF16)


def positions(cols, b, blocks, slots, total_blocks):
    first = lax.axis_index("blk") * blocks
    return [
        jnp.clip(lax.rem(cols[k, b] - first + RIM + total_blocks, total_blocks), 0, blocks + 2 * RIM - 1)
        for k in range(slots)
    ]


def mask_and_inner(
    total_blocks, cols_hbm, basis_hbm, reach_hbm, stiffness_hbm, masked, to_link, to_chip, inner, cols, basis, reach, stiffness, sem
):
    blocks, slots, size, _ = stiffness.shape
    groups, _, width = basis.shape
    slabs = reach.shape[0]
    slab = lax.axis_index("blk")
    inner_blocks = pl.ds(RIM, blocks - 2 * RIM)
    moves = [(reach_hbm, reach), (cols_hbm, cols)]
    moves += [
        (basis_hbm.at[:, pl.ds(b * size, RIM * size)], basis.at[:, pl.ds(b * size, RIM * size)])
        for b in range(0, blocks, RIM)
    ]
    moves.append((stiffness_hbm.at[inner_blocks], stiffness.at[inner_blocks]))
    copies = [pltpu.make_async_copy(source, target, sem.at[n]) for n, (source, target) in enumerate(moves)]
    for copy in copies:
        copy.start()
    copies[0].wait()
    low = reach[pl.ds(lax.rem(slab + slabs - 1, slabs), 1), 1, :]
    high = reach[pl.ds(lax.rem(slab + 1, slabs), 1), 0, :]
    for b in range(blocks):
        if b % RIM == 0:
            copies[2 + b // RIM].wait()
        rows = slice(b * size, (b + 1) * size)
        keep = {0: (b < low).astype(F32).astype(BF16), 2: (b >= blocks - high).astype(F32).astype(BF16)}
        for g in range(groups):
            value = basis[g, rows, :]
            masked[rows, g * width : (g + 1) * width] = value * keep[g] if g in keep else value
    odd = parity()

    @pl.when(odd == 0)
    def _():
        to_link[...] = masked[: RIM * size, : 2 * width]
        to_chip[...] = masked[(blocks - RIM) * size :, width:]

    @pl.when(odd == 1)
    def _():
        to_link[...] = masked[(blocks - RIM) * size :, width:]
        to_chip[...] = masked[: RIM * size, : 2 * width]

    copies[1].wait()
    copies[-1].wait()
    for b in range(RIM, blocks - RIM):
        starts = [jnp.clip(p - RIM, 0, blocks - 1) for p in positions(cols, b, blocks, slots, total_blocks)]
        inner[(b - RIM) * size : (b - RIM + 1) * size, :] = block_image(stiffness, masked, b, size, starts)


def outer_image(total_blocks, cols, stiffness, masked, from_link, from_chip, outer, extended):
    blocks, slots, size, _ = stiffness.shape
    rows, wide = masked.shape
    rim = RIM * size
    width = wide // 3
    odd = parity()

    @pl.when(odd == 0)
    def _():
        extended[:rim, : 2 * width] = from_link[...]
        extended[rim + rows :, width:] = from_chip[...]

    @pl.when(odd == 1)
    def _():
        extended[:rim, : 2 * width] = from_chip[...]
        extended[rim + rows :, width:] = from_link[...]

    extended[:rim, 2 * width :] = jnp.zeros((rim, width), BF16)
    extended[rim : rim + rows, :] = masked[...]
    extended[rim + rows :, :width] = jnp.zeros((rim, width), BF16)
    for n, b in enumerate([*range(RIM), *range(blocks - RIM, blocks)]):
        starts = positions(cols, b, blocks, slots, total_blocks)
        outer[n * size : (n + 1) * size, :] = block_image(stiffness, extended, b, size, starts)


def parity():
    return lax.rem(lax.axis_index("blk"), 2)


def store_tile(tile, own, link, chip):
    width = own.shape[0]
    odd = parity()
    own[...] = tile[width : 2 * width].astype(own.dtype)
    down, up = tile[:width].astype(BF16), tile[2 * width :].astype(BF16)

    @pl.when(odd == 0)
    def _():
        link[...] = down
        chip[...] = up

    @pl.when(odd == 1)
    def _():
        link[...] = up
        chip[...] = down


def turn(size, masked, left_inner, left_outer):
    rows = masked.shape[0]
    rim = RIM * size
    left_inner[...] = masked[rim : rows - rim, :].T
    left_outer[:, :rim] = masked[:rim, :].T
    left_outer[:, rim:] = masked[rows - rim :, :].T


def own_tile(size, masked, inner, outer, own, link, chip, left_inner, left_outer):
    turn(size, masked, left_inner, left_outer)
    store_tile(dot(left_inner[...], inner[...]) + dot(left_outer[...], outer[...]), own, link, chip)


def partner_tile(size, masked, inner, outer, near_left, inner_r, own, link, chip, far_outer, far, near, far_inner):
    turn(size, masked, far_inner, far_outer)
    store_tile(dot(far_inner[...], inner[...]) + dot(far_outer[...], outer[...]), own, link, chip)
    far[...] = dot(far_inner[...], inner_r[...])
    near[...] = dot(near_left[...], inner_r[...])


def late_tile(base, left_outer, outer, own, link, chip):
    store_tile(base[...] + dot(left_outer[...], outer[...]), own, link, chip)


def add_tiles(steps, *refs):
    count = len(steps)
    terms = refs[: 3 * count]
    coarse, total, sem = refs[-3:]
    width = total.shape[2]
    me = lax.axis_index("col")
    even = parity() == 0
    copies = []
    for n, (even_step, odd_step) in enumerate(steps):
        own, link, chip = (ref[...].astype(F32) for ref in terms[3 * n : 3 * n + 3])
        prev = jnp.where(even, link, chip)
        nxt = jnp.where(even, chip, link)
        for d in range(5):
            value = None
            for offset, term in ((0, prev), (1, own), (2, nxt)):
                if 0 <= d - offset <= 2:
                    part = term[:, (d - offset) * width : (d - offset + 1) * width]
                    value = part if value is None else value + part
            total[n, d] = value
        column = lax.bitwise_xor(me, jnp.where(even, even_step, odd_step))
        start = pl.multiple_of(column * width, width)
        copy = pltpu.make_async_copy(total.at[n], coarse.at[:, :, pl.ds(start, width)], sem.at[n])
        copy.start()
        copies.append(copy)
    for copy in copies:
        copy.wait()


def tile_shapes(width, wide, own):
    return shape((width, wide), own), shape((width, wide), BF16), shape((width, wide), BF16)


def shards(stiffness, block_cols, basis, patch_reach):
    blocks, slots, size, _ = stiffness.shape
    rows, groups, width = basis.shape
    wide = groups * width
    slabs = lax.axis_size("blk")
    total_blocks = blocks * slabs
    pairs = [(i, i ^ 1) for i in range(slabs)]
    cross = [(i, (i - 1 if i % 2 == 0 else i + 1) % slabs) for i in range(slabs)]

    def over_chip(value):
        return lax.ppermute(value, "blk", pairs)

    def over_link(value):
        return lax.ppermute(value, "blk", cross)

    def to(value, slab_of, column_of):
        perm = [(4 * i + q, 4 * (slab_of(i) % slabs) + column_of(i, q)) for i in range(slabs) for q in range(4)]
        return lax.ppermute(value, ("blk", "col"), perm)

    def partner(i, q):
        return q ^ (1 + i % 2)

    def side(i, q):
        return q ^ (2 - i % 2)

    def to_partner(value):
        return to(value, lambda i: i, partner)

    def to_side(value):
        return to(value, lambda i: i, side)

    def spread(own, link, chip):
        own = to_partner(own)
        link = to(link, lambda i: i + 1 if i % 2 else i - 1, partner)
        chip = to(chip, lambda i: i ^ 1, partner)
        return own, link, chip

    cols = block_cols.T
    flat = basis.transpose(1, 0, 2)
    reach = patch_reach.transpose(0, 2, 1)
    inner_rows = (blocks - 2 * RIM) * size
    rim = RIM * size
    row_flops = 2 * slots * size * size * wide
    masked, rim_link, rim_chip, inner = call(
        functools.partial(mask_and_inner, total_blocks),
        (shape((rows, wide), BF16), shape((rim, 2 * width), BF16), shape((rim, 2 * width), BF16), shape((inner_rows, wide), BF16)),
        [HBM] * 4,
        [VMEM] * 4,
        tuple(pltpu.with_memory_space_constraint(x, pltpu.HBM) for x in (cols, flat, reach, stiffness)),
        scratch=[
            pltpu.SMEM(cols.shape, cols.dtype),
            pltpu.VMEM(flat.shape, BF16),
            pltpu.VMEM(reach.shape, reach.dtype),
            pltpu.VMEM(stiffness.shape, BF16),
            pltpu.SemaphoreType.DMA((3 + blocks // RIM,)),
        ],
        flops=row_flops * (blocks - 2 * RIM),
        name="mask_and_inner",
    )
    masked_p = to_partner(masked)
    inner_r = to_side(inner)
    rim_link = over_link(rim_link)
    rim_chip = over_chip(rim_chip)
    outer = call(
        functools.partial(outer_image, total_blocks),
        shape((2 * rim, wide), BF16),
        [SMEM] + [VMEM] * 4,
        VMEM,
        (cols, stiffness, masked, rim_link, rim_chip),
        scratch=[pltpu.VMEM((rows + 2 * rim, wide), BF16)],
        flops=row_flops * 2 * RIM,
        name="outer_image",
    )
    outer_r = to_side(outer)
    tile_flops = 2 * rows * wide * wide
    left_shapes = (shape((wide, inner_rows), BF16), shape((wide, 2 * rim), BF16))
    base_shape = shape((wide, wide), F32)

    own, own_link, own_chip, left_inner, left_outer = call(
        functools.partial(own_tile, size),
        (*tile_shapes(width, wide, F32), *left_shapes),
        [VMEM] * 3,
        [VMEM] * 5,
        (masked, inner, outer),
        flops=tile_flops,
        name="own_tile",
    )
    own_link, own_chip = over_link(own_link), over_chip(own_chip)
    part, part_link, part_chip, far_outer, far_base, near_base = call(
        functools.partial(partner_tile, size),
        (*tile_shapes(width, wide, BF16), left_shapes[1], base_shape, base_shape),
        [VMEM] * 5,
        [VMEM] * 6,
        (masked_p, inner, outer, left_inner, inner_r),
        scratch=[pltpu.VMEM((wide, inner_rows), BF16)],
        flops=2 * tile_flops,
        name="partner_tile",
    )
    part, part_link, part_chip = spread(part, part_link, part_chip)

    outer_r, own_link, own_chip = lax.optimization_barrier((outer_r, own_link, own_chip))

    def late(base, left, own, name):
        return call(
            late_tile,
            tile_shapes(width, wide, own),
            [VMEM] * 3,
            [VMEM] * 3,
            (base, left, outer_r),
            flops=tile_flops // 2,
            name=name,
        )

    far, far_link, far_chip = spread(*late(far_base, far_outer, BF16, "far_tile"))
    near_base, part, part_link, part_chip = lax.optimization_barrier((near_base, part, part_link, part_chip))
    near, near_link, near_chip = late(near_base, left_outer, F32, "near_tile")
    near_link, near_chip = over_link(near_link), over_chip(near_chip)

    def add(steps, terms, name, base=None):
        extra = () if base is None else (base,)
        return call(
            functools.partial(add_tiles, steps),
            shape((5, width, 4 * width), F32),
            [VMEM] * len(terms) + [HBM] * len(extra),
            HBM,
            (*terms, *extra),
            scratch=[pltpu.VMEM((len(steps), 5, width, width), F32), pltpu.SemaphoreType.DMA((len(steps),))],
            flops=5 * len(steps) * width * width,
            aliases={len(terms): 0} if extra else None,
            name=name,
        )

    coarse = add(((0, 0),), (own, own_link, own_chip), "add_own")
    coarse = add(
        ((2, 1), (1, 2), (3, 3)),
        (near, part_link, part_chip, part, near_link, near_chip, far, far_link, far_chip),
        "add_rest",
        coarse,
    )
    return coarse.transpose(1, 0, 2)


def gathered(stiffness, block_cols, basis, patch_reach):
    blocks, slots, size, _ = stiffness.shape
    rows, groups, width = basis.shape
    slabs = lax.axis_size("blk")
    slab = lax.axis_index("blk")
    total_blocks = blocks * slabs
    ring = [(i, (i + 1) % slabs) for i in range(slabs)]
    back = [(j, i) for i, j in ring]
    low = lax.dynamic_index_in_dim(patch_reach, (slab - 1) % slabs, 0, False)[:, 1]
    high = lax.dynamic_index_in_dim(patch_reach, (slab + 1) % slabs, 0, False)[:, 0]
    block_row = jnp.arange(rows, dtype=jnp.int32) // size
    lower = block_row[:, None] < low[None, :]
    upper = block_row[:, None] >= blocks - high[None, :]
    support = jnp.stack([lower, jnp.ones_like(lower), upper], 1)
    masked = jnp.where(support, basis, jnp.zeros_like(basis))
    rim = RIM * size
    before = lax.ppermute(masked[rows - rim :, 1:], "blk", ring)
    after = lax.ppermute(masked[:rim, :2], "blk", back)
    none = jnp.zeros((rim, 1, width), masked.dtype)
    extended = jnp.concatenate(
        [jnp.concatenate([before, none], 1), masked, jnp.concatenate([none, after], 1)], 0
    ).reshape(blocks + 2 * RIM, size, groups * width)
    position = (block_cols - slab * blocks + RIM) % total_blocks
    picked = jnp.take(extended, position, axis=0)
    image = jnp.einsum("rsij,rsjc->ric", stiffness, picked, preferred_element_type=F32)
    image = image.astype(BF16).reshape(rows, groups, width)
    image = lax.all_gather(image, "col", axis=2, tiled=True)
    tiles = jnp.einsum("rgl,rhc->glhc", masked, image, preferred_element_type=F32)
    from_prev = lax.ppermute(tiles[2], "blk", ring)
    from_next = lax.ppermute(tiles[0], "blk", back)

    def place(tile, offset):
        return jnp.pad(tile, ((0, 0), (offset, 2 - offset), (0, 0)))

    return place(from_prev, 0) + place(tiles[1], 1) + place(from_next, 2)


def solution(mesh):
    in_specs = (
        P("blk", None, None, None),
        P("blk", None),
        P("blk", None, "col"),
        P(None, "col", None),
    )
    out_specs = P(("blk", "col"), None, None)
    body = shards if mesh.shape["col"] == 4 and mesh.shape["blk"] % 2 == 0 else gathered
    return jax.shard_map(body, mesh=mesh, in_specs=in_specs, out_specs=out_specs, check_vma=False)
```

```python
import functools

import jax
import jax.numpy as jnp
from jax import lax
from jax.experimental import pallas as pl
from jax.experimental.pallas import tpu as pltpu
from jax.sharding import PartitionSpec as P

BF16 = jnp.bfloat16
F32 = jnp.float32
VMEM = pl.BlockSpec(memory_space=pltpu.VMEM)
SMEM = pl.BlockSpec(memory_space=pltpu.SMEM)
HBM = pl.BlockSpec(memory_space=pltpu.HBM)
RIM = 2


def shape(dims, dtype):
    return jax.ShapeDtypeStruct(dims, dtype)


def dot(left, right):
    return jnp.dot(left, right, preferred_element_type=F32)


def call(kernel, out_shape, in_specs, out_specs, args, scratch=(), flops=0, aliases=None, name=None):
    outs = jax.tree.leaves(out_shape)
    moved = sum(x.size * x.dtype.itemsize for x in (*args, *outs))
    return pl.pallas_call(
        kernel,
        out_shape=out_shape,
        in_specs=in_specs,
        out_specs=out_specs,
        scratch_shapes=list(scratch),
        input_output_aliases=aliases or {},
        cost_estimate=pl.CostEstimate(flops=flops, bytes_accessed=moved, transcendentals=0),
        compiler_params=pltpu.CompilerParams(vmem_limit_bytes=24 << 20),
        name=name,
    )(*args)


def block_image(stiffness, source, b, block_size, starts):
    blocks = [source[pl.ds(pl.multiple_of(start * block_size, block_size), block_size), :] for start in starts]
    left = jnp.concatenate([stiffness[b, k] for k in range(len(starts))], axis=1)
    return dot(left, jnp.concatenate(blocks, axis=0)).astype(BF16)


def positions(cols, b, blocks, slots, total_blocks):
    first = lax.axis_index("blk") * blocks
    return [
        jnp.clip(lax.rem(cols[k, b] - first + RIM + total_blocks, total_blocks), 0, blocks + 2 * RIM - 1)
        for k in range(slots)
    ]


def mask_and_inner(
    total_blocks, cols_hbm, basis_hbm, reach_hbm, stiffness_hbm, masked, to_link, to_chip, inner, cols, basis, reach, stiffness, sem
):
    blocks, slots, size, _ = stiffness.shape
    groups, _, width = basis.shape
    slabs = reach.shape[0]
    slab = lax.axis_index("blk")
    inner_blocks = pl.ds(RIM, blocks - 2 * RIM)
    moves = [(reach_hbm, reach), (cols_hbm, cols)]
    moves += [
        (basis_hbm.at[:, pl.ds(b * size, RIM * size)], basis.at[:, pl.ds(b * size, RIM * size)])
        for b in range(0, blocks, RIM)
    ]
    moves.append((stiffness_hbm.at[inner_blocks], stiffness.at[inner_blocks]))
    copies = [pltpu.make_async_copy(source, target, sem.at[n]) for n, (source, target) in enumerate(moves)]
    for copy in copies:
        copy.start()
    copies[0].wait()
    low = reach[pl.ds(lax.rem(slab + slabs - 1, slabs), 1), 1, :]
    high = reach[pl.ds(lax.rem(slab + 1, slabs), 1), 0, :]
    for b in range(blocks):
        if b % RIM == 0:
            copies[2 + b // RIM].wait()
        rows = slice(b * size, (b + 1) * size)
        keep = {0: (b < low).astype(F32).astype(BF16), 2: (b >= blocks - high).astype(F32).astype(BF16)}
        for g in range(groups):
            value = basis[g, rows, :]
            masked[rows, g * width : (g + 1) * width] = value * keep[g] if g in keep else value
    odd = parity()

    @pl.when(odd == 0)
    def _():
        to_link[...] = masked[: RIM * size, : 2 * width]
        to_chip[...] = masked[(blocks - RIM) * size :, width:]

    @pl.when(odd == 1)
    def _():
        to_link[...] = masked[(blocks - RIM) * size :, width:]
        to_chip[...] = masked[: RIM * size, : 2 * width]

    copies[1].wait()
    copies[-1].wait()
    for b in range(RIM, blocks - RIM):
        starts = [jnp.clip(p - RIM, 0, blocks - 1) for p in positions(cols, b, blocks, slots, total_blocks)]
        inner[(b - RIM) * size : (b - RIM + 1) * size, :] = block_image(stiffness, masked, b, size, starts)


def outer_image(total_blocks, cols, stiffness, masked, from_link, from_chip, outer, extended):
    blocks, slots, size, _ = stiffness.shape
    rows, wide = masked.shape
    rim = RIM * size
    width = wide // 3
    odd = parity()

    @pl.when(odd == 0)
    def _():
        extended[:rim, : 2 * width] = from_link[...]
        extended[rim + rows :, width:] = from_chip[...]

    @pl.when(odd == 1)
    def _():
        extended[:rim, : 2 * width] = from_chip[...]
        extended[rim + rows :, width:] = from_link[...]

    extended[:rim, 2 * width :] = jnp.zeros((rim, width), BF16)
    extended[rim : rim + rows, :] = masked[...]
    extended[rim + rows :, :width] = jnp.zeros((rim, width), BF16)
    for n, b in enumerate([*range(RIM), *range(blocks - RIM, blocks)]):
        starts = positions(cols, b, blocks, slots, total_blocks)
        outer[n * size : (n + 1) * size, :] = block_image(stiffness, extended, b, size, starts)


def parity():
    return lax.rem(lax.axis_index("blk"), 2)


def store_tile(tile, own, link, chip):
    width = tile.shape[0] // 3
    odd = parity()
    own[...] = tile[width : 2 * width].astype(own.dtype)
    down, up = tile[:width].astype(BF16), tile[2 * width :].astype(BF16)

    @pl.when(odd == 0)
    def _():
        link[...] = down
        chip[...] = up

    @pl.when(odd == 1)
    def _():
        link[...] = up
        chip[...] = down


def turn(size, masked, left_inner, left_outer):
    rows = masked.shape[0]
    rim = RIM * size
    left_inner[...] = masked[rim : rows - rim, :].T
    left_outer[:, :rim] = masked[:rim, :].T
    left_outer[:, rim:] = masked[rows - rim :, :].T


def own_tile(size, masked, inner, outer, own, link, chip, left_inner, left_outer):
    turn(size, masked, left_inner, left_outer)
    store_tile(dot(left_inner[...], inner[...]) + dot(left_outer[...], outer[...]), own, link, chip)


def partner_tiles(size, masked, inner, outer, inner_r, outer_r, own, link, chip, left_inner, left_outer):
    turn(size, masked, left_inner, left_outer)
    wide = masked.shape[1]
    for n, (first, second) in enumerate(((inner, outer), (inner_r, outer_r))):
        lanes = slice(n * wide, (n + 1) * wide)
        tile = dot(left_inner[...], first[...]) + dot(left_outer[...], second[...])
        store_tile(tile, own.at[:, lanes], link.at[:, lanes], chip.at[:, lanes])


def half_tile(left_inner, inner, base):
    base[...] = dot(left_inner[...], inner[...])


def near_tile(base, left_outer, outer, own, link, chip):
    store_tile(base[...] + dot(left_outer[...], outer[...]), own, link, chip)


def add_tiles(steps, *refs):
    count = len(steps)
    terms = refs[: 3 * count]
    coarse, total, sem = refs[-3:]
    width = total.shape[2]
    me = lax.axis_index("col")
    even = parity() == 0
    copies = []
    for n, ((even_step, odd_step), chunks) in enumerate(steps):
        own, link, chip = (
            ref[:, m * 3 * width : (m + 1) * 3 * width].astype(F32) for ref, m in zip(terms[3 * n : 3 * n + 3], chunks)
        )
        prev = jnp.where(even, link, chip)
        nxt = jnp.where(even, chip, link)
        for d in range(5):
            value = None
            for offset, term in ((0, prev), (1, own), (2, nxt)):
                if 0 <= d - offset <= 2:
                    part = term[:, (d - offset) * width : (d - offset + 1) * width]
                    value = part if value is None else value + part
            total[n, d] = value
        column = lax.bitwise_xor(me, jnp.where(even, even_step, odd_step))
        start = pl.multiple_of(column * width, width)
        copy = pltpu.make_async_copy(total.at[n], coarse.at[:, :, pl.ds(start, width)], sem.at[n])
        copy.start()
        copies.append(copy)
    for copy in copies:
        copy.wait()


def tile_shapes(width, wide, own):
    return shape((width, wide), own), shape((width, wide), BF16), shape((width, wide), BF16)


def shards(stiffness, block_cols, basis, patch_reach):
    blocks, slots, size, _ = stiffness.shape
    rows, groups, width = basis.shape
    wide = groups * width
    slabs = lax.axis_size("blk")
    total_blocks = blocks * slabs
    pairs = [(i, i ^ 1) for i in range(slabs)]
    cross = [(i, (i - 1 if i % 2 == 0 else i + 1) % slabs) for i in range(slabs)]

    def over_chip(value):
        return lax.ppermute(value, "blk", pairs)

    def over_link(value):
        return lax.ppermute(value, "blk", cross)

    def to(value, slab_of, column_of):
        perm = [(4 * i + q, 4 * (slab_of(i) % slabs) + column_of(i, q)) for i in range(slabs) for q in range(4)]
        return lax.ppermute(value, ("blk", "col"), perm)

    def partner(i, q):
        return q ^ (1 + i % 2)

    def side(i, q):
        return q ^ (2 - i % 2)

    def to_partner(value):
        return to(value, lambda i: i, partner)

    def to_side(value):
        return to(value, lambda i: i, side)

    def spread(own, link, chip):
        own = to_partner(own)
        link = to(link, lambda i: i + 1 if i % 2 else i - 1, partner)
        chip = to(chip, lambda i: i ^ 1, partner)
        return own, link, chip

    cols = block_cols.T
    flat = basis.transpose(1, 0, 2)
    reach = patch_reach.transpose(0, 2, 1)
    inner_rows = (blocks - 2 * RIM) * size
    rim = RIM * size
    row_flops = 2 * slots * size * size * wide
    masked, rim_link, rim_chip, inner = call(
        functools.partial(mask_and_inner, total_blocks),
        (shape((rows, wide), BF16), shape((rim, 2 * width), BF16), shape((rim, 2 * width), BF16), shape((inner_rows, wide), BF16)),
        [HBM] * 4,
        [VMEM] * 4,
        tuple(pltpu.with_memory_space_constraint(x, pltpu.HBM) for x in (cols, flat, reach, stiffness)),
        scratch=[
            pltpu.SMEM(cols.shape, cols.dtype),
            pltpu.VMEM(flat.shape, BF16),
            pltpu.VMEM(reach.shape, reach.dtype),
            pltpu.VMEM(stiffness.shape, BF16),
            pltpu.SemaphoreType.DMA((3 + blocks // RIM,)),
        ],
        flops=row_flops * (blocks - 2 * RIM),
        name="mask_and_inner",
    )
    masked_p = to_partner(masked)
    inner_r = to_side(inner)
    rim_link = over_link(rim_link)
    rim_chip = over_chip(rim_chip)
    outer = call(
        functools.partial(outer_image, total_blocks),
        shape((2 * rim, wide), BF16),
        [SMEM] + [VMEM] * 4,
        VMEM,
        (cols, stiffness, masked, rim_link, rim_chip),
        scratch=[pltpu.VMEM((rows + 2 * rim, wide), BF16)],
        flops=row_flops * 2 * RIM,
        name="outer_image",
    )
    outer_r = to_side(outer)
    tile_flops = 2 * rows * wide * wide
    left_shapes = (shape((wide, inner_rows), BF16), shape((wide, 2 * rim), BF16))
    base_shape = shape((wide, wide), F32)

    own, own_link, own_chip, left_inner, left_outer = call(
        functools.partial(own_tile, size),
        (*tile_shapes(width, wide, F32), *left_shapes),
        [VMEM] * 3,
        [VMEM] * 5,
        (masked, inner, outer),
        flops=tile_flops,
        name="own_tile",
    )
    own_link, own_chip = over_link(own_link), over_chip(own_chip)
    base = call(
        half_tile,
        shape((wide, wide), F32),
        [VMEM] * 2,
        VMEM,
        (left_inner, inner_r),
        flops=tile_flops // 2,
        name="half_tile",
    )
    outer_r, own_link, own_chip = lax.optimization_barrier((outer_r, own_link, own_chip))
    masked_p, base = lax.optimization_barrier((masked_p, base))
    near, near_link, near_chip = call(
        near_tile,
        tile_shapes(width, wide, F32),
        [VMEM] * 3,
        [VMEM] * 3,
        (base, left_outer, outer_r),
        flops=tile_flops // 2,
        name="near_tile",
    )
    near_link, near_chip = over_link(near_link), over_chip(near_chip)
    part, part_link, part_chip = spread(
        *call(
            functools.partial(partner_tiles, size),
            tile_shapes(width, 2 * wide, BF16),
            [VMEM] * 5,
            [VMEM] * 3,
            (masked_p, inner, outer, inner_r, outer_r),
            scratch=[pltpu.VMEM((wide, inner_rows), BF16), pltpu.VMEM((wide, 2 * rim), BF16)],
            flops=2 * tile_flops,
            name="partner_tiles",
        )
    )

    def add(steps, terms, name, base=None):
        extra = () if base is None else (base,)
        return call(
            functools.partial(add_tiles, steps),
            shape((5, width, 4 * width), F32),
            [VMEM] * len(terms) + [HBM] * len(extra),
            HBM,
            (*terms, *extra),
            scratch=[pltpu.VMEM((len(steps), 5, width, width), F32), pltpu.SemaphoreType.DMA((len(steps),))],
            flops=5 * len(steps) * width * width,
            aliases={len(terms): 0} if extra else None,
            name=name,
        )

    coarse = add((((0, 0), (0, 0, 0)),), (own, own_link, own_chip), "add_own")
    coarse = add(
        (((2, 1), (0, 0, 0)), ((1, 2), (0, 0, 0)), ((3, 3), (1, 1, 1))),
        (near, part_link, part_chip, part, near_link, near_chip, part, part_link, part_chip),
        "add_rest",
        coarse,
    )
    return coarse.transpose(1, 0, 2)


def gathered(stiffness, block_cols, basis, patch_reach):
    blocks, slots, size, _ = stiffness.shape
    rows, groups, width = basis.shape
    slabs = lax.axis_size("blk")
    slab = lax.axis_index("blk")
    total_blocks = blocks * slabs
    ring = [(i, (i + 1) % slabs) for i in range(slabs)]
    back = [(j, i) for i, j in ring]
    low = lax.dynamic_index_in_dim(patch_reach, (slab - 1) % slabs, 0, False)[:, 1]
    high = lax.dynamic_index_in_dim(patch_reach, (slab + 1) % slabs, 0, False)[:, 0]
    block_row = jnp.arange(rows, dtype=jnp.int32) // size
    lower = block_row[:, None] < low[None, :]
    upper = block_row[:, None] >= blocks - high[None, :]
    support = jnp.stack([lower, jnp.ones_like(lower), upper], 1)
    masked = jnp.where(support, basis, jnp.zeros_like(basis))
    rim = RIM * size
    before = lax.ppermute(masked[rows - rim :, 1:], "blk", ring)
    after = lax.ppermute(masked[:rim, :2], "blk", back)
    none = jnp.zeros((rim, 1, width), masked.dtype)
    extended = jnp.concatenate(
        [jnp.concatenate([before, none], 1), masked, jnp.concatenate([none, after], 1)], 0
    ).reshape(blocks + 2 * RIM, size, groups * width)
    position = (block_cols - slab * blocks + RIM) % total_blocks
    picked = jnp.take(extended, position, axis=0)
    image = jnp.einsum("rsij,rsjc->ric", stiffness, picked, preferred_element_type=F32)
    image = image.astype(BF16).reshape(rows, groups, width)
    image = lax.all_gather(image, "col", axis=2, tiled=True)
    tiles = jnp.einsum("rgl,rhc->glhc", masked, image, preferred_element_type=F32)
    from_prev = lax.ppermute(tiles[2], "blk", ring)
    from_next = lax.ppermute(tiles[0], "blk", back)

    def place(tile, offset):
        return jnp.pad(tile, ((0, 0), (offset, 2 - offset), (0, 0)))

    return place(from_prev, 0) + place(tiles[1], 1) + place(from_next, 2)


def solution(mesh):
    in_specs = (
        P("blk", None, None, None),
        P("blk", None),
        P("blk", None, "col"),
        P(None, "col", None),
    )
    out_specs = P(("blk", "col"), None, None)
    body = shards if mesh.shape["col"] == 4 and mesh.shape["blk"] % 2 == 0 else gathered
    return jax.shard_map(body, mesh=mesh, in_specs=in_specs, out_specs=out_specs, check_vma=False)
```

```python
import functools

import jax
import jax.numpy as jnp
from jax import lax
from jax.experimental import pallas as pl
from jax.experimental.pallas import tpu as pltpu
from jax.sharding import PartitionSpec as P

BF16 = jnp.bfloat16
F32 = jnp.float32
VMEM = pl.BlockSpec(memory_space=pltpu.VMEM)
SMEM = pl.BlockSpec(memory_space=pltpu.SMEM)
HBM = pl.BlockSpec(memory_space=pltpu.HBM)
RIM = 2


def shape(dims, dtype):
    return jax.ShapeDtypeStruct(dims, dtype)


def dot(left, right):
    return jnp.dot(left, right, preferred_element_type=F32)


def call(kernel, out_shape, in_specs, out_specs, args, scratch=(), flops=0, aliases=None, name=None):
    outs = jax.tree.leaves(out_shape)
    moved = sum(x.size * x.dtype.itemsize for x in (*args, *outs))
    return pl.pallas_call(
        kernel,
        out_shape=out_shape,
        in_specs=in_specs,
        out_specs=out_specs,
        scratch_shapes=list(scratch),
        input_output_aliases=aliases or {},
        cost_estimate=pl.CostEstimate(flops=flops, bytes_accessed=moved, transcendentals=0),
        compiler_params=pltpu.CompilerParams(vmem_limit_bytes=24 << 20),
        name=name,
    )(*args)


def block_image(stiffness, source, b, block_size, starts):
    blocks = [source[pl.ds(pl.multiple_of(start * block_size, block_size), block_size), :] for start in starts]
    left = jnp.concatenate([stiffness[b, k] for k in range(len(starts))], axis=1)
    return dot(left, jnp.concatenate(blocks, axis=0)).astype(BF16)


def positions(cols, b, blocks, slots, total_blocks):
    first = lax.axis_index("blk") * blocks
    return [
        jnp.clip(lax.rem(cols[k, b] - first + RIM + total_blocks, total_blocks), 0, blocks + 2 * RIM - 1)
        for k in range(slots)
    ]


def reaches(reach):
    slabs = reach.shape[0]
    slab = lax.axis_index("blk")
    low = reach[pl.ds(lax.rem(slab + slabs - 1, slabs), 1), 1, :]
    high = reach[pl.ds(lax.rem(slab + 1, slabs), 1), 0, :]
    return low, high


def mask_block(basis, b, blocks, size, low, high, masked):
    groups, _, width = basis.shape
    rows = slice(b * size, (b + 1) * size)
    keep = {0: (b < low).astype(F32).astype(BF16), 2: (b >= blocks - high).astype(F32).astype(BF16)}
    for g in range(groups):
        value = basis[g, rows, :]
        masked[rows, g * width : (g + 1) * width] = value * keep[g] if g in keep else value


def mask_and_inner(
    total_blocks, cols_hbm, basis_hbm, reach_hbm, stiffness_hbm, masked, to_link, to_chip, inner, cols, basis, reach, stiffness, sem
):
    blocks, slots, size, _ = stiffness.shape
    width = basis.shape[2]
    inner_blocks = pl.ds(RIM, blocks - 2 * RIM)
    moves = [(reach_hbm, reach), (cols_hbm, cols)]
    moves += [
        (basis_hbm.at[:, pl.ds(b * size, RIM * size)], basis.at[:, pl.ds(b * size, RIM * size)])
        for b in range(0, blocks, RIM)
    ]
    moves.append((stiffness_hbm.at[inner_blocks], stiffness.at[inner_blocks]))
    copies = [pltpu.make_async_copy(source, target, sem.at[n]) for n, (source, target) in enumerate(moves)]
    for copy in copies:
        copy.start()
    copies[0].wait()
    low, high = reaches(reach)
    for b in range(blocks):
        if b % RIM == 0:
            copies[2 + b // RIM].wait()
        mask_block(basis, b, blocks, size, low, high, masked)
    odd = parity()

    @pl.when(odd == 0)
    def _():
        to_link[...] = masked[: RIM * size, : 2 * width]
        to_chip[...] = masked[(blocks - RIM) * size :, width:]

    @pl.when(odd == 1)
    def _():
        to_link[...] = masked[(blocks - RIM) * size :, width:]
        to_chip[...] = masked[: RIM * size, : 2 * width]

    copies[1].wait()
    copies[-1].wait()
    for b in range(RIM, blocks - RIM):
        starts = [jnp.clip(p - RIM, 0, blocks - 1) for p in positions(cols, b, blocks, slots, total_blocks)]
        inner[(b - RIM) * size : (b - RIM + 1) * size, :] = block_image(stiffness, masked, b, size, starts)


def outer_image(total_blocks, cols, stiffness, masked, from_link, from_chip, outer, extended):
    blocks, slots, size, _ = stiffness.shape
    rows, wide = masked.shape
    rim = RIM * size
    width = wide // 3
    odd = parity()

    @pl.when(odd == 0)
    def _():
        extended[:rim, : 2 * width] = from_link[...]
        extended[rim + rows :, width:] = from_chip[...]

    @pl.when(odd == 1)
    def _():
        extended[:rim, : 2 * width] = from_chip[...]
        extended[rim + rows :, width:] = from_link[...]

    extended[:rim, 2 * width :] = jnp.zeros((rim, width), BF16)
    extended[rim : rim + rows, :] = masked[...]
    extended[rim + rows :, :width] = jnp.zeros((rim, width), BF16)
    for n, b in enumerate([*range(RIM), *range(blocks - RIM, blocks)]):
        starts = positions(cols, b, blocks, slots, total_blocks)
        outer[n * size : (n + 1) * size, :] = block_image(stiffness, extended, b, size, starts)


def parity():
    return lax.rem(lax.axis_index("blk"), 2)


def store_tile(tile, own, link, chip):
    width = own.shape[0]
    odd = parity()
    own[...] = tile[width : 2 * width].astype(own.dtype)
    down, up = tile[:width].astype(BF16), tile[2 * width :].astype(BF16)

    @pl.when(odd == 0)
    def _():
        link[...] = down
        chip[...] = up

    @pl.when(odd == 1)
    def _():
        link[...] = up
        chip[...] = down


def turn(size, masked, left_inner, left_outer):
    rows = masked.shape[0]
    rim = RIM * size
    left_inner[...] = masked[rim : rows - rim, :].T
    left_outer[:, :rim] = masked[:rim, :].T
    left_outer[:, rim:] = masked[rows - rim :, :].T


def own_tile(size, masked, inner, outer, own, link, chip, left_inner, left_outer):
    turn(size, masked, left_inner, left_outer)
    store_tile(dot(left_inner[...], inner[...]) + dot(left_outer[...], outer[...]), own, link, chip)


def partner_tile(
    size, basis, reach, inner, outer, near_left, inner_r, own, link, chip, far_outer, far, near, masked, far_inner
):
    low, high = reaches(reach)
    blocks = basis.shape[1] // size
    for b in range(blocks):
        mask_block(basis, b, blocks, size, low, high, masked)
    turn(size, masked, far_inner, far_outer)
    store_tile(dot(far_inner[...], inner[...]) + dot(far_outer[...], outer[...]), own, link, chip)
    far[...] = dot(far_inner[...], inner_r[...])
    near[...] = dot(near_left[...], inner_r[...])


def late_tile(base, left_outer, outer, own, link, chip):
    store_tile(base[...] + dot(left_outer[...], outer[...]), own, link, chip)


def add_tiles(steps, *refs):
    count = len(steps)
    terms = refs[: 3 * count]
    coarse, total, sem = refs[-3:]
    width = total.shape[2]
    me = lax.axis_index("col")
    even = parity() == 0
    copies = []
    for n, (even_step, odd_step) in enumerate(steps):
        own, link, chip = (ref[...].astype(F32) for ref in terms[3 * n : 3 * n + 3])
        prev = jnp.where(even, link, chip)
        nxt = jnp.where(even, chip, link)
        for d in range(5):
            value = None
            for offset, term in ((0, prev), (1, own), (2, nxt)):
                if 0 <= d - offset <= 2:
                    part = term[:, (d - offset) * width : (d - offset + 1) * width]
                    value = part if value is None else value + part
            total[n, d] = value
        column = lax.bitwise_xor(me, jnp.where(even, even_step, odd_step))
        start = pl.multiple_of(column * width, width)
        copy = pltpu.make_async_copy(total.at[n], coarse.at[:, :, pl.ds(start, width)], sem.at[n])
        copy.start()
        copies.append(copy)
    for copy in copies:
        copy.wait()


def tile_shapes(width, wide, own):
    return shape((width, wide), own), shape((width, wide), BF16), shape((width, wide), BF16)


def shards(stiffness, block_cols, basis, patch_reach):
    blocks, slots, size, _ = stiffness.shape
    rows, groups, width = basis.shape
    wide = groups * width
    slabs = lax.axis_size("blk")
    total_blocks = blocks * slabs
    pairs = [(i, i ^ 1) for i in range(slabs)]
    cross = [(i, (i - 1 if i % 2 == 0 else i + 1) % slabs) for i in range(slabs)]

    def over_chip(value):
        return lax.ppermute(value, "blk", pairs)

    def over_link(value):
        return lax.ppermute(value, "blk", cross)

    def to(value, slab_of, column_of):
        perm = [(4 * i + q, 4 * (slab_of(i) % slabs) + column_of(i, q)) for i in range(slabs) for q in range(4)]
        return lax.ppermute(value, ("blk", "col"), perm)

    def partner(i, q):
        return q ^ (1 + i % 2)

    def side(i, q):
        return q ^ (2 - i % 2)

    def to_partner(value):
        return to(value, lambda i: i, partner)

    def to_side(value):
        return to(value, lambda i: i, side)

    def spread(own, link, chip):
        own = to_partner(own)
        link = to(link, lambda i: i + 1 if i % 2 else i - 1, partner)
        chip = to(chip, lambda i: i ^ 1, partner)
        return own, link, chip

    basis_p = to_partner(basis).transpose(1, 0, 2)
    reach_p = to_partner(patch_reach).transpose(0, 2, 1)
    cols = block_cols.T
    flat = basis.transpose(1, 0, 2)
    reach = patch_reach.transpose(0, 2, 1)
    inner_rows = (blocks - 2 * RIM) * size
    rim = RIM * size
    row_flops = 2 * slots * size * size * wide
    masked, rim_link, rim_chip, inner = call(
        functools.partial(mask_and_inner, total_blocks),
        (shape((rows, wide), BF16), shape((rim, 2 * width), BF16), shape((rim, 2 * width), BF16), shape((inner_rows, wide), BF16)),
        [HBM] * 4,
        [VMEM] * 4,
        tuple(pltpu.with_memory_space_constraint(x, pltpu.HBM) for x in (cols, flat, reach, stiffness)),
        scratch=[
            pltpu.SMEM(cols.shape, cols.dtype),
            pltpu.VMEM(flat.shape, BF16),
            pltpu.VMEM(reach.shape, reach.dtype),
            pltpu.VMEM(stiffness.shape, BF16),
            pltpu.SemaphoreType.DMA((3 + blocks // RIM,)),
        ],
        flops=row_flops * (blocks - 2 * RIM),
        name="mask_and_inner",
    )
    inner_r = to_side(inner)
    rim_link = over_link(rim_link)
    rim_chip = over_chip(rim_chip)
    outer = call(
        functools.partial(outer_image, total_blocks),
        shape((2 * rim, wide), BF16),
        [SMEM] + [VMEM] * 4,
        VMEM,
        (cols, stiffness, masked, rim_link, rim_chip),
        scratch=[pltpu.VMEM((rows + 2 * rim, wide), BF16)],
        flops=row_flops * 2 * RIM,
        name="outer_image",
    )
    outer_r = to_side(outer)
    tile_flops = 2 * rows * wide * wide
    left_shapes = (shape((wide, inner_rows), BF16), shape((wide, 2 * rim), BF16))
    base_shape = shape((wide, wide), F32)

    own, own_link, own_chip, left_inner, left_outer = call(
        functools.partial(own_tile, size),
        (*tile_shapes(width, wide, F32), *left_shapes),
        [VMEM] * 3,
        [VMEM] * 5,
        (masked, inner, outer),
        flops=tile_flops,
        name="own_tile",
    )
    own_link, own_chip = over_link(own_link), over_chip(own_chip)
    part, part_link, part_chip, far_outer, far_base, near_base = call(
        functools.partial(partner_tile, size),
        (*tile_shapes(width, wide, BF16), left_shapes[1], base_shape, base_shape),
        [VMEM] * 6,
        [VMEM] * 6,
        (basis_p, reach_p, inner, outer, left_inner, inner_r),
        scratch=[pltpu.VMEM((rows, wide), BF16), pltpu.VMEM((wide, inner_rows), BF16)],
        flops=2 * tile_flops,
        name="partner_tile",
    )
    part, part_link, part_chip = spread(part, part_link, part_chip)

    outer_r, own_link, own_chip = lax.optimization_barrier((outer_r, own_link, own_chip))

    def late(base, left, own, name):
        return call(
            late_tile,
            tile_shapes(width, wide, own),
            [VMEM] * 3,
            [VMEM] * 3,
            (base, left, outer_r),
            flops=tile_flops // 2,
            name=name,
        )

    far, far_link, far_chip = spread(*late(far_base, far_outer, BF16, "far_tile"))
    near_base, part, part_link, part_chip = lax.optimization_barrier((near_base, part, part_link, part_chip))
    near, near_link, near_chip = late(near_base, left_outer, F32, "near_tile")
    near_link, near_chip = over_link(near_link), over_chip(near_chip)

    def add(steps, terms, name, base=None):
        extra = () if base is None else (base,)
        return call(
            functools.partial(add_tiles, steps),
            shape((5, width, 4 * width), F32),
            [VMEM] * len(terms) + [HBM] * len(extra),
            HBM,
            (*terms, *extra),
            scratch=[pltpu.VMEM((len(steps), 5, width, width), F32), pltpu.SemaphoreType.DMA((len(steps),))],
            flops=5 * len(steps) * width * width,
            aliases={len(terms): 0} if extra else None,
            name=name,
        )

    coarse = add(((0, 0),), (own, own_link, own_chip), "add_own")
    coarse = add(
        ((2, 1), (1, 2), (3, 3)),
        (near, part_link, part_chip, part, near_link, near_chip, far, far_link, far_chip),
        "add_rest",
        coarse,
    )
    return coarse.transpose(1, 0, 2)


def gathered(stiffness, block_cols, basis, patch_reach):
    blocks, slots, size, _ = stiffness.shape
    rows, groups, width = basis.shape
    slabs = lax.axis_size("blk")
    slab = lax.axis_index("blk")
    total_blocks = blocks * slabs
    ring = [(i, (i + 1) % slabs) for i in range(slabs)]
    back = [(j, i) for i, j in ring]
    low = lax.dynamic_index_in_dim(patch_reach, (slab - 1) % slabs, 0, False)[:, 1]
    high = lax.dynamic_index_in_dim(patch_reach, (slab + 1) % slabs, 0, False)[:, 0]
    block_row = jnp.arange(rows, dtype=jnp.int32) // size
    lower = block_row[:, None] < low[None, :]
    upper = block_row[:, None] >= blocks - high[None, :]
    support = jnp.stack([lower, jnp.ones_like(lower), upper], 1)
    masked = jnp.where(support, basis, jnp.zeros_like(basis))
    rim = RIM * size
    before = lax.ppermute(masked[rows - rim :, 1:], "blk", ring)
    after = lax.ppermute(masked[:rim, :2], "blk", back)
    none = jnp.zeros((rim, 1, width), masked.dtype)
    extended = jnp.concatenate(
        [jnp.concatenate([before, none], 1), masked, jnp.concatenate([none, after], 1)], 0
    ).reshape(blocks + 2 * RIM, size, groups * width)
    position = (block_cols - slab * blocks + RIM) % total_blocks
    picked = jnp.take(extended, position, axis=0)
    image = jnp.einsum("rsij,rsjc->ric", stiffness, picked, preferred_element_type=F32)
    image = image.astype(BF16).reshape(rows, groups, width)
    image = lax.all_gather(image, "col", axis=2, tiled=True)
    tiles = jnp.einsum("rgl,rhc->glhc", masked, image, preferred_element_type=F32)
    from_prev = lax.ppermute(tiles[2], "blk", ring)
    from_next = lax.ppermute(tiles[0], "blk", back)

    def place(tile, offset):
        return jnp.pad(tile, ((0, 0), (offset, 2 - offset), (0, 0)))

    return place(from_prev, 0) + place(tiles[1], 1) + place(from_next, 2)


def solution(mesh):
    in_specs = (
        P("blk", None, None, None),
        P("blk", None),
        P("blk", None, "col"),
        P(None, "col", None),
    )
    out_specs = P(("blk", "col"), None, None)
    body = shards if mesh.shape["col"] == 4 and mesh.shape["blk"] % 2 == 0 else gathered
    return jax.shard_map(body, mesh=mesh, in_specs=in_specs, out_specs=out_specs, check_vma=False)
```

```python
import functools

import jax
import jax.numpy as jnp
from jax import lax
from jax.experimental import pallas as pl
from jax.experimental.pallas import tpu as pltpu
from jax.sharding import PartitionSpec as P

BF16 = jnp.bfloat16
F32 = jnp.float32
VMEM = pl.BlockSpec(memory_space=pltpu.VMEM)
SMEM = pl.BlockSpec(memory_space=pltpu.SMEM)
HBM = pl.BlockSpec(memory_space=pltpu.HBM)
RIM = 2


def shape(dims, dtype):
    return jax.ShapeDtypeStruct(dims, dtype)


def dot(left, right):
    return jnp.dot(left, right, preferred_element_type=F32)


def call(kernel, out_shape, in_specs, out_specs, args, scratch=(), flops=0, aliases=None, name=None):
    outs = jax.tree.leaves(out_shape)
    moved = sum(x.size * x.dtype.itemsize for x in (*args, *outs))
    return pl.pallas_call(
        kernel,
        out_shape=out_shape,
        in_specs=in_specs,
        out_specs=out_specs,
        scratch_shapes=list(scratch),
        input_output_aliases=aliases or {},
        cost_estimate=pl.CostEstimate(flops=flops, bytes_accessed=moved, transcendentals=0),
        compiler_params=pltpu.CompilerParams(vmem_limit_bytes=24 << 20),
        name=name,
    )(*args)


def block_image(stiffness, source, b, block_size, starts):
    blocks = [source[pl.ds(pl.multiple_of(start * block_size, block_size), block_size), :] for start in starts]
    left = jnp.concatenate([stiffness[b, k] for k in range(len(starts))], axis=1)
    return dot(left, jnp.concatenate(blocks, axis=0)).astype(BF16)


def positions(cols, b, blocks, slots, total_blocks):
    first = lax.axis_index("blk") * blocks
    return [
        jnp.clip(lax.rem(cols[k, b] - first + RIM + total_blocks, total_blocks), 0, blocks + 2 * RIM - 1)
        for k in range(slots)
    ]


def reaches(reach):
    slabs = reach.shape[0]
    slab = lax.axis_index("blk")
    low = reach[pl.ds(lax.rem(slab + slabs - 1, slabs), 1), 1, :]
    high = reach[pl.ds(lax.rem(slab + 1, slabs), 1), 0, :]
    return low, high


def mask_block(basis, b, blocks, size, low, high, masked):
    groups, _, width = basis.shape
    rows = slice(b * size, (b + 1) * size)
    keep = {0: (b < low).astype(F32).astype(BF16), 2: (b >= blocks - high).astype(F32).astype(BF16)}
    for g in range(groups):
        value = basis[g, rows, :]
        masked[rows, g * width : (g + 1) * width] = value * keep[g] if g in keep else value


def mask_and_inner(
    total_blocks, cols_hbm, basis_hbm, reach_hbm, stiffness_hbm, masked, to_link, to_chip, inner, cols, basis, reach, stiffness, sem
):
    blocks, slots, size, _ = stiffness.shape
    width = basis.shape[2]
    inner_blocks = pl.ds(RIM, blocks - 2 * RIM)
    moves = [(reach_hbm, reach), (cols_hbm, cols)]
    moves += [
        (basis_hbm.at[:, pl.ds(b * size, RIM * size)], basis.at[:, pl.ds(b * size, RIM * size)])
        for b in range(0, blocks, RIM)
    ]
    moves.append((stiffness_hbm.at[inner_blocks], stiffness.at[inner_blocks]))
    copies = [pltpu.make_async_copy(source, target, sem.at[n]) for n, (source, target) in enumerate(moves)]
    for copy in copies:
        copy.start()
    copies[0].wait()
    low, high = reaches(reach)
    for b in range(blocks):
        if b % RIM == 0:
            copies[2 + b // RIM].wait()
        mask_block(basis, b, blocks, size, low, high, masked)
    odd = parity()

    @pl.when(odd == 0)
    def _():
        to_link[...] = masked[: RIM * size, : 2 * width]
        to_chip[...] = masked[(blocks - RIM) * size :, width:]

    @pl.when(odd == 1)
    def _():
        to_link[...] = masked[(blocks - RIM) * size :, width:]
        to_chip[...] = masked[: RIM * size, : 2 * width]

    copies[1].wait()
    copies[-1].wait()
    for b in range(RIM, blocks - RIM):
        starts = [jnp.clip(p - RIM, 0, blocks - 1) for p in positions(cols, b, blocks, slots, total_blocks)]
        inner[(b - RIM) * size : (b - RIM + 1) * size, :] = block_image(stiffness, masked, b, size, starts)


def outer_image(total_blocks, cols, stiffness, masked, from_link, from_chip, outer, extended):
    blocks, slots, size, _ = stiffness.shape
    rows, wide = masked.shape
    rim = RIM * size
    width = wide // 3
    odd = parity()

    @pl.when(odd == 0)
    def _():
        extended[:rim, : 2 * width] = from_link[...]
        extended[rim + rows :, width:] = from_chip[...]

    @pl.when(odd == 1)
    def _():
        extended[:rim, : 2 * width] = from_chip[...]
        extended[rim + rows :, width:] = from_link[...]

    extended[:rim, 2 * width :] = jnp.zeros((rim, width), BF16)
    extended[rim : rim + rows, :] = masked[...]
    extended[rim + rows :, :width] = jnp.zeros((rim, width), BF16)
    for n, b in enumerate([*range(RIM), *range(blocks - RIM, blocks)]):
        starts = positions(cols, b, blocks, slots, total_blocks)
        outer[n * size : (n + 1) * size, :] = block_image(stiffness, extended, b, size, starts)


def parity():
    return lax.rem(lax.axis_index("blk"), 2)


def store_tile(tile, own, link, chip):
    width = own.shape[0]
    odd = parity()
    own[...] = tile[width : 2 * width].astype(own.dtype)
    down, up = tile[:width].astype(BF16), tile[2 * width :].astype(BF16)

    @pl.when(odd == 0)
    def _():
        link[...] = down
        chip[...] = up

    @pl.when(odd == 1)
    def _():
        link[...] = up
        chip[...] = down


def turn(size, masked, left_inner, left_outer):
    rows = masked.shape[0]
    rim = RIM * size
    left_inner[...] = masked[rim : rows - rim, :].T
    left_outer[:, :rim] = masked[:rim, :].T
    left_outer[:, rim:] = masked[rows - rim :, :].T


def own_tile(size, masked, inner, outer, own, link, chip, left_inner, left_outer):
    turn(size, masked, left_inner, left_outer)
    store_tile(dot(left_inner[...], inner[...]) + dot(left_outer[...], outer[...]), own, link, chip)


def partner_tile(
    size, basis, reach, inner, outer, near_left, inner_r, own, link, chip, far_outer, far, near, masked, far_inner
):
    low, high = reaches(reach)
    blocks = basis.shape[1] // size
    for b in range(blocks):
        mask_block(basis, b, blocks, size, low, high, masked)
    turn(size, masked, far_inner, far_outer)
    store_tile(dot(far_inner[...], inner[...]) + dot(far_outer[...], outer[...]), own, link, chip)
    far[...] = dot(far_inner[...], inner_r[...])
    near[...] = dot(near_left[...], inner_r[...])


def late_tile(base, left_outer, outer, own, link, chip):
    store_tile(base[...] + dot(left_outer[...], outer[...]), own, link, chip)


def add_tiles(steps, *refs):
    count = len(steps)
    terms = refs[: 3 * count]
    coarse, total, sem = refs[-3:]
    width = total.shape[2]
    me = lax.axis_index("col")
    even = parity() == 0
    copies = []
    for n, (even_step, odd_step) in enumerate(steps):
        own, link, chip = (ref[...].astype(F32) for ref in terms[3 * n : 3 * n + 3])
        prev = jnp.where(even, link, chip)
        nxt = jnp.where(even, chip, link)
        for d in range(5):
            value = None
            for offset, term in ((0, prev), (1, own), (2, nxt)):
                if 0 <= d - offset <= 2:
                    part = term[:, (d - offset) * width : (d - offset + 1) * width]
                    value = part if value is None else value + part
            total[n, d] = value
        column = lax.bitwise_xor(me, jnp.where(even, even_step, odd_step))
        start = pl.multiple_of(column * width, width)
        copy = pltpu.make_async_copy(total.at[n], coarse.at[:, :, pl.ds(start, width)], sem.at[n])
        copy.start()
        copies.append(copy)
    for copy in copies:
        copy.wait()


def tile_shapes(width, wide, own):
    return shape((width, wide), own), shape((width, wide), BF16), shape((width, wide), BF16)


def shards(stiffness, block_cols, basis, patch_reach):
    blocks, slots, size, _ = stiffness.shape
    rows, groups, width = basis.shape
    wide = groups * width
    slabs = lax.axis_size("blk")
    total_blocks = blocks * slabs
    pairs = [(i, i ^ 1) for i in range(slabs)]
    cross = [(i, (i - 1 if i % 2 == 0 else i + 1) % slabs) for i in range(slabs)]

    def over_chip(value):
        return lax.ppermute(value, "blk", pairs)

    def over_link(value):
        return lax.ppermute(value, "blk", cross)

    def to(value, slab_of, column_of):
        perm = [(4 * i + q, 4 * (slab_of(i) % slabs) + column_of(i, q)) for i in range(slabs) for q in range(4)]
        return lax.ppermute(value, ("blk", "col"), perm)

    def partner(i, q):
        return q ^ (1 + i % 2)

    def side(i, q):
        return q ^ (2 - i % 2)

    def to_partner(value):
        return to(value, lambda i: i, partner)

    def to_side(value):
        return to(value, lambda i: i, side)

    def spread(own, link, chip):
        own = to_partner(own)
        link = to(link, lambda i: i + 1 if i % 2 else i - 1, partner)
        chip = to(chip, lambda i: i ^ 1, partner)
        return own, link, chip

    basis_p = to_partner(basis).transpose(1, 0, 2)
    reach_p = to_partner(patch_reach).transpose(0, 2, 1)
    cols = block_cols.T
    flat = basis.transpose(1, 0, 2)
    reach = patch_reach.transpose(0, 2, 1)
    inner_rows = (blocks - 2 * RIM) * size
    rim = RIM * size
    row_flops = 2 * slots * size * size * wide
    masked, rim_link, rim_chip, inner = call(
        functools.partial(mask_and_inner, total_blocks),
        (shape((rows, wide), BF16), shape((rim, 2 * width), BF16), shape((rim, 2 * width), BF16), shape((inner_rows, wide), BF16)),
        [HBM] * 4,
        [VMEM] * 4,
        tuple(pltpu.with_memory_space_constraint(x, pltpu.HBM) for x in (cols, flat, reach, stiffness)),
        scratch=[
            pltpu.SMEM(cols.shape, cols.dtype),
            pltpu.VMEM(flat.shape, BF16),
            pltpu.VMEM(reach.shape, reach.dtype),
            pltpu.VMEM(stiffness.shape, BF16),
            pltpu.SemaphoreType.DMA((3 + blocks // RIM,)),
        ],
        flops=row_flops * (blocks - 2 * RIM),
        name="mask_and_inner",
    )
    inner_r = to_side(inner)
    rim_link = over_link(rim_link)
    rim_chip = over_chip(rim_chip)
    rim_link, rim_chip, reach_p = lax.optimization_barrier((rim_link, rim_chip, reach_p))
    outer = call(
        functools.partial(outer_image, total_blocks),
        shape((2 * rim, wide), BF16),
        [SMEM] + [VMEM] * 4,
        VMEM,
        (cols, stiffness, masked, rim_link, rim_chip),
        scratch=[pltpu.VMEM((rows + 2 * rim, wide), BF16)],
        flops=row_flops * 2 * RIM,
        name="outer_image",
    )
    outer_r = to_side(outer)
    tile_flops = 2 * rows * wide * wide
    left_shapes = (shape((wide, inner_rows), BF16), shape((wide, 2 * rim), BF16))
    base_shape = shape((wide, wide), F32)

    own, own_link, own_chip, left_inner, left_outer = call(
        functools.partial(own_tile, size),
        (*tile_shapes(width, wide, F32), *left_shapes),
        [VMEM] * 3,
        [VMEM] * 5,
        (masked, inner, outer),
        flops=tile_flops,
        name="own_tile",
    )
    own_link, own_chip = over_link(own_link), over_chip(own_chip)
    part, part_link, part_chip, far_outer, far_base, near_base = call(
        functools.partial(partner_tile, size),
        (*tile_shapes(width, wide, BF16), left_shapes[1], base_shape, base_shape),
        [VMEM] * 6,
        [VMEM] * 6,
        (basis_p, reach_p, inner, outer, left_inner, inner_r),
        scratch=[pltpu.VMEM((rows, wide), BF16), pltpu.VMEM((wide, inner_rows), BF16)],
        flops=2 * tile_flops,
        name="partner_tile",
    )
    part, part_link, part_chip = spread(part, part_link, part_chip)

    outer_r, own_link, own_chip = lax.optimization_barrier((outer_r, own_link, own_chip))

    def late(base, left, own, name):
        return call(
            late_tile,
            tile_shapes(width, wide, own),
            [VMEM] * 3,
            [VMEM] * 3,
            (base, left, outer_r),
            flops=tile_flops // 2,
            name=name,
        )

    far, far_link, far_chip = spread(*late(far_base, far_outer, BF16, "far_tile"))
    near_base, part, part_link, part_chip = lax.optimization_barrier((near_base, part, part_link, part_chip))
    near, near_link, near_chip = late(near_base, left_outer, F32, "near_tile")
    near_link, near_chip = over_link(near_link), over_chip(near_chip)

    def add(steps, terms, name, base=None):
        extra = () if base is None else (base,)
        return call(
            functools.partial(add_tiles, steps),
            shape((5, width, 4 * width), F32),
            [VMEM] * len(terms) + [HBM] * len(extra),
            HBM,
            (*terms, *extra),
            scratch=[pltpu.VMEM((len(steps), 5, width, width), F32), pltpu.SemaphoreType.DMA((len(steps),))],
            flops=5 * len(steps) * width * width,
            aliases={len(terms): 0} if extra else None,
            name=name,
        )

    coarse = add(((0, 0),), (own, own_link, own_chip), "add_own")
    coarse = add(
        ((2, 1), (1, 2), (3, 3)),
        (near, part_link, part_chip, part, near_link, near_chip, far, far_link, far_chip),
        "add_rest",
        coarse,
    )
    return coarse.transpose(1, 0, 2)


def gathered(stiffness, block_cols, basis, patch_reach):
    blocks, slots, size, _ = stiffness.shape
    rows, groups, width = basis.shape
    slabs = lax.axis_size("blk")
    slab = lax.axis_index("blk")
    total_blocks = blocks * slabs
    ring = [(i, (i + 1) % slabs) for i in range(slabs)]
    back = [(j, i) for i, j in ring]
    low = lax.dynamic_index_in_dim(patch_reach, (slab - 1) % slabs, 0, False)[:, 1]
    high = lax.dynamic_index_in_dim(patch_reach, (slab + 1) % slabs, 0, False)[:, 0]
    block_row = jnp.arange(rows, dtype=jnp.int32) // size
    lower = block_row[:, None] < low[None, :]
    upper = block_row[:, None] >= blocks - high[None, :]
    support = jnp.stack([lower, jnp.ones_like(lower), upper], 1)
    masked = jnp.where(support, basis, jnp.zeros_like(basis))
    rim = RIM * size
    before = lax.ppermute(masked[rows - rim :, 1:], "blk", ring)
    after = lax.ppermute(masked[:rim, :2], "blk", back)
    none = jnp.zeros((rim, 1, width), masked.dtype)
    extended = jnp.concatenate(
        [jnp.concatenate([before, none], 1), masked, jnp.concatenate([none, after], 1)], 0
    ).reshape(blocks + 2 * RIM, size, groups * width)
    position = (block_cols - slab * blocks + RIM) % total_blocks
    picked = jnp.take(extended, position, axis=0)
    image = jnp.einsum("rsij,rsjc->ric", stiffness, picked, preferred_element_type=F32)
    image = image.astype(BF16).reshape(rows, groups, width)
    image = lax.all_gather(image, "col", axis=2, tiled=True)
    tiles = jnp.einsum("rgl,rhc->glhc", masked, image, preferred_element_type=F32)
    from_prev = lax.ppermute(tiles[2], "blk", ring)
    from_next = lax.ppermute(tiles[0], "blk", back)

    def place(tile, offset):
        return jnp.pad(tile, ((0, 0), (offset, 2 - offset), (0, 0)))

    return place(from_prev, 0) + place(tiles[1], 1) + place(from_next, 2)


def solution(mesh):
    in_specs = (
        P("blk", None, None, None),
        P("blk", None),
        P("blk", None, "col"),
        P(None, "col", None),
    )
    out_specs = P(("blk", "col"), None, None)
    body = shards if mesh.shape["col"] == 4 and mesh.shape["blk"] % 2 == 0 else gathered
    return jax.shard_map(body, mesh=mesh, in_specs=in_specs, out_specs=out_specs, check_vma=False)
```

```python
import functools

import jax
import jax.numpy as jnp
from jax import lax
from jax.experimental import pallas as pl
from jax.experimental.pallas import tpu as pltpu
from jax.sharding import PartitionSpec as P

BF16 = jnp.bfloat16
F32 = jnp.float32
VMEM = pl.BlockSpec(memory_space=pltpu.VMEM)
SMEM = pl.BlockSpec(memory_space=pltpu.SMEM)
HBM = pl.BlockSpec(memory_space=pltpu.HBM)
RIM = 2


def shape(dims, dtype):
    return jax.ShapeDtypeStruct(dims, dtype)


def dot(left, right):
    return jnp.dot(left, right, preferred_element_type=F32)


def call(kernel, out_shape, in_specs, out_specs, args, scratch=(), flops=0, aliases=None, name=None):
    outs = jax.tree.leaves(out_shape)
    moved = sum(x.size * x.dtype.itemsize for x in (*args, *outs))
    return pl.pallas_call(
        kernel,
        out_shape=out_shape,
        in_specs=in_specs,
        out_specs=out_specs,
        scratch_shapes=list(scratch),
        input_output_aliases=aliases or {},
        cost_estimate=pl.CostEstimate(flops=flops, bytes_accessed=moved, transcendentals=0),
        compiler_params=pltpu.CompilerParams(vmem_limit_bytes=24 << 20),
        name=name,
    )(*args)


def block_image(stiffness, source, b, block_size, starts):
    blocks = [source[pl.ds(pl.multiple_of(start * block_size, block_size), block_size), :] for start in starts]
    left = jnp.concatenate([stiffness[b, k] for k in range(len(starts))], axis=1)
    return dot(left, jnp.concatenate(blocks, axis=0)).astype(BF16)


def positions(cols, b, blocks, slots, total_blocks):
    first = lax.axis_index("blk") * blocks
    return [
        jnp.clip(lax.rem(cols[k, b] - first + RIM + total_blocks, total_blocks), 0, blocks + 2 * RIM - 1)
        for k in range(slots)
    ]


def reaches(reach):
    slabs = reach.shape[0]
    slab = lax.axis_index("blk")
    low = reach[pl.ds(lax.rem(slab + slabs - 1, slabs), 1), 1, :]
    high = reach[pl.ds(lax.rem(slab + 1, slabs), 1), 0, :]
    return low, high


def mask_block(basis, b, blocks, size, low, high, masked):
    groups, _, width = basis.shape
    rows = slice(b * size, (b + 1) * size)
    keep = {0: (b < low).astype(F32).astype(BF16), 2: (b >= blocks - high).astype(F32).astype(BF16)}
    for g in range(groups):
        value = basis[g, rows, :]
        masked[rows, g * width : (g + 1) * width] = value * keep[g] if g in keep else value


def mask_and_inner(
    total_blocks, cols_hbm, basis_hbm, reach_hbm, stiffness_hbm, masked, to_link, to_chip, inner, cols, basis, reach, stiffness, sem
):
    blocks, slots, size, _ = stiffness.shape
    width = basis.shape[2]
    inner_blocks = pl.ds(RIM, blocks - 2 * RIM)
    moves = [(reach_hbm, reach), (cols_hbm, cols)]
    moves += [
        (basis_hbm.at[:, pl.ds(b * size, RIM * size)], basis.at[:, pl.ds(b * size, RIM * size)])
        for b in range(0, blocks, RIM)
    ]
    moves.append((stiffness_hbm.at[inner_blocks], stiffness.at[inner_blocks]))
    copies = [pltpu.make_async_copy(source, target, sem.at[n]) for n, (source, target) in enumerate(moves)]
    for copy in copies:
        copy.start()
    copies[0].wait()
    low, high = reaches(reach)
    for b in range(blocks):
        if b % RIM == 0:
            copies[2 + b // RIM].wait()
        mask_block(basis, b, blocks, size, low, high, masked)
    odd = parity()

    @pl.when(odd == 0)
    def _():
        to_link[...] = masked[: RIM * size, : 2 * width]
        to_chip[...] = masked[(blocks - RIM) * size :, width:]

    @pl.when(odd == 1)
    def _():
        to_link[...] = masked[(blocks - RIM) * size :, width:]
        to_chip[...] = masked[: RIM * size, : 2 * width]

    copies[1].wait()
    copies[-1].wait()
    for b in range(RIM, blocks - RIM):
        starts = [jnp.clip(p - RIM, 0, blocks - 1) for p in positions(cols, b, blocks, slots, total_blocks)]
        inner[(b - RIM) * size : (b - RIM + 1) * size, :] = block_image(stiffness, masked, b, size, starts)


def outer_image(total_blocks, cols, stiffness, masked, from_link, from_chip, outer, extended):
    blocks, slots, size, _ = stiffness.shape
    rows, wide = masked.shape
    rim = RIM * size
    width = wide // 3
    odd = parity()

    @pl.when(odd == 0)
    def _():
        extended[:rim, : 2 * width] = from_link[...]
        extended[rim + rows :, width:] = from_chip[...]

    @pl.when(odd == 1)
    def _():
        extended[:rim, : 2 * width] = from_chip[...]
        extended[rim + rows :, width:] = from_link[...]

    extended[:rim, 2 * width :] = jnp.zeros((rim, width), BF16)
    extended[rim : rim + rows, :] = masked[...]
    extended[rim + rows :, :width] = jnp.zeros((rim, width), BF16)
    for n, b in enumerate([*range(RIM), *range(blocks - RIM, blocks)]):
        starts = positions(cols, b, blocks, slots, total_blocks)
        outer[n * size : (n + 1) * size, :] = block_image(stiffness, extended, b, size, starts)


def parity():
    return lax.rem(lax.axis_index("blk"), 2)


def store_tile(tile, own, link, chip):
    width = tile.shape[0] // 3
    odd = parity()
    own[...] = tile[width : 2 * width].astype(own.dtype)
    down, up = tile[:width].astype(BF16), tile[2 * width :].astype(BF16)

    @pl.when(odd == 0)
    def _():
        link[...] = down
        chip[...] = up

    @pl.when(odd == 1)
    def _():
        link[...] = up
        chip[...] = down


def turn(size, masked, left_inner, left_outer):
    rows = masked.shape[0]
    rim = RIM * size
    left_inner[...] = masked[rim : rows - rim, :].T
    left_outer[:, :rim] = masked[:rim, :].T
    left_outer[:, rim:] = masked[rows - rim :, :].T


def own_tile(size, masked, inner, outer, own, link, chip, left_inner, left_outer):
    turn(size, masked, left_inner, left_outer)
    store_tile(dot(left_inner[...], inner[...]) + dot(left_outer[...], outer[...]), own, link, chip)


def partner_tile(
    size, basis, reach, inner, outer, near_left, inner_r, own, link, chip, far_outer, far, near, masked, far_inner
):
    low, high = reaches(reach)
    blocks = basis.shape[1] // size
    for b in range(blocks):
        mask_block(basis, b, blocks, size, low, high, masked)
    turn(size, masked, far_inner, far_outer)
    store_tile(dot(far_inner[...], inner[...]) + dot(far_outer[...], outer[...]), own, link, chip)
    far[...] = dot(far_inner[...], inner_r[...])
    near[...] = dot(near_left[...], inner_r[...])


def late_tiles(
    far_base, near_base, far_outer, near_outer, outer_r, near, near_link, near_chip, far, far_link, far_chip
):
    store_tile(far_base[...] + dot(far_outer[...], outer_r[...]), far, far_link, far_chip)
    store_tile(near_base[...] + dot(near_outer[...], outer_r[...]), near, near_link, near_chip)


def add_tiles(steps, *refs):
    count = len(steps)
    terms = refs[: 3 * count]
    coarse, total, sem = refs[-3:]
    width = total.shape[2]
    me = lax.axis_index("col")
    even = parity() == 0
    copies = []
    for n, (even_step, odd_step) in enumerate(steps):
        link, chip, own = (terms[n + m * count][...].astype(F32) for m in range(3))
        prev = jnp.where(even, link, chip)
        nxt = jnp.where(even, chip, link)
        for d in range(5):
            value = None
            for offset, term in ((0, prev), (1, own), (2, nxt)):
                if 0 <= d - offset <= 2:
                    part = term[:, (d - offset) * width : (d - offset + 1) * width]
                    value = part if value is None else value + part
            total[n, d] = value
        column = lax.bitwise_xor(me, jnp.where(even, even_step, odd_step))
        start = pl.multiple_of(column * width, width)
        copy = pltpu.make_async_copy(total.at[n], coarse.at[:, :, pl.ds(start, width)], sem.at[n])
        copy.start()
        copies.append(copy)
    for copy in copies:
        copy.wait()


def tile_shapes(width, wide, own):
    return shape((width, wide), own), shape((width, wide), BF16), shape((width, wide), BF16)


def shards(stiffness, block_cols, basis, patch_reach):
    blocks, slots, size, _ = stiffness.shape
    rows, groups, width = basis.shape
    wide = groups * width
    slabs = lax.axis_size("blk")
    total_blocks = blocks * slabs
    pairs = [(i, i ^ 1) for i in range(slabs)]
    cross = [(i, (i - 1 if i % 2 == 0 else i + 1) % slabs) for i in range(slabs)]

    def over_chip(value):
        return lax.ppermute(value, "blk", pairs)

    def over_link(value):
        return lax.ppermute(value, "blk", cross)

    def to(value, slab_of, column_of):
        perm = [(4 * i + q, 4 * (slab_of(i) % slabs) + column_of(i, q)) for i in range(slabs) for q in range(4)]
        return lax.ppermute(value, ("blk", "col"), perm)

    def partner(i, q):
        return q ^ (1 + i % 2)

    def side(i, q):
        return q ^ (2 - i % 2)

    def to_partner(value):
        return to(value, lambda i: i, partner)

    def to_side(value):
        return to(value, lambda i: i, side)

    def to_partner_chip(value):
        return to(value, lambda i: i ^ 1, partner)

    def to_partner_link(value):
        return to(value, lambda i: i + 1 if i % 2 else i - 1, partner)

    basis_p = to_partner(basis).transpose(1, 0, 2)
    reach_p = to_partner(patch_reach).transpose(0, 2, 1)
    cols = block_cols.T
    flat = basis.transpose(1, 0, 2)
    reach = patch_reach.transpose(0, 2, 1)
    inner_rows = (blocks - 2 * RIM) * size
    rim = RIM * size
    row_flops = 2 * slots * size * size * wide
    masked, rim_link, rim_chip, inner = call(
        functools.partial(mask_and_inner, total_blocks),
        (shape((rows, wide), BF16), shape((rim, 2 * width), BF16), shape((rim, 2 * width), BF16), shape((inner_rows, wide), BF16)),
        [HBM] * 4,
        [VMEM] * 4,
        tuple(pltpu.with_memory_space_constraint(x, pltpu.HBM) for x in (cols, flat, reach, stiffness)),
        scratch=[
            pltpu.SMEM(cols.shape, cols.dtype),
            pltpu.VMEM(flat.shape, BF16),
            pltpu.VMEM(reach.shape, reach.dtype),
            pltpu.VMEM(stiffness.shape, BF16),
            pltpu.SemaphoreType.DMA((3 + blocks // RIM,)),
        ],
        flops=row_flops * (blocks - 2 * RIM),
        name="mask_and_inner",
    )
    inner_r = to_side(inner)
    rim_link = over_link(rim_link)
    rim_chip = over_chip(rim_chip)
    outer = call(
        functools.partial(outer_image, total_blocks),
        shape((2 * rim, wide), BF16),
        [SMEM] + [VMEM] * 4,
        VMEM,
        (cols, stiffness, masked, rim_link, rim_chip),
        scratch=[pltpu.VMEM((rows + 2 * rim, wide), BF16)],
        flops=row_flops * 2 * RIM,
        name="outer_image",
    )
    outer_r = to_side(outer)
    tile_flops = 2 * rows * wide * wide
    left_shapes = (shape((wide, inner_rows), BF16), shape((wide, 2 * rim), BF16))
    base_shape = shape((wide, wide), F32)

    own, own_link, own_chip, left_inner, left_outer = call(
        functools.partial(own_tile, size),
        (*tile_shapes(width, wide, F32), *left_shapes),
        [VMEM] * 3,
        [VMEM] * 5,
        (masked, inner, outer),
        flops=tile_flops,
        name="own_tile",
    )
    own_link, own_chip = over_link(own_link), over_chip(own_chip)
    part, part_link, part_chip, far_outer, far_base, near_base = call(
        functools.partial(partner_tile, size),
        (*tile_shapes(width, wide, BF16), left_shapes[1], base_shape, base_shape),
        [VMEM] * 6,
        [VMEM] * 6,
        (basis_p, reach_p, inner, outer, left_inner, inner_r),
        scratch=[pltpu.VMEM((rows, wide), BF16), pltpu.VMEM((wide, inner_rows), BF16)],
        flops=2 * tile_flops,
        name="partner_tile",
    )
    part, part_link, part_chip = to_partner(part), to_partner_link(part_link), to_partner_chip(part_chip)
    outer_r, own_link, own_chip, far_base = lax.optimization_barrier((outer_r, own_link, own_chip, far_base))
    near, near_link, near_chip, far, far_link, far_chip = call(
        late_tiles,
        (*tile_shapes(width, wide, F32), *tile_shapes(width, wide, BF16)),
        [VMEM] * 5,
        [VMEM] * 6,
        (far_base, near_base, far_outer, left_outer, outer_r),
        flops=tile_flops,
        name="late_tiles",
    )
    far, part, part_link, part_chip = lax.optimization_barrier((far, part, part_link, part_chip))
    far_link = to_partner_link(far_link)
    near_link = over_link(near_link)
    far_chip = to_partner_chip(far_chip)
    far = to_partner(far)
    near_chip = over_chip(near_chip)

    def add(steps, terms, name, base=None):
        extra = () if base is None else (base,)
        return call(
            functools.partial(add_tiles, steps),
            shape((5, width, 4 * width), F32),
            [VMEM] * len(terms) + [HBM] * len(extra),
            HBM,
            (*terms, *extra),
            scratch=[pltpu.VMEM((len(steps), 5, width, width), F32), pltpu.SemaphoreType.DMA((len(steps),))],
            flops=5 * len(steps) * width * width,
            aliases={len(terms): 0} if extra else None,
            name=name,
        )

    coarse = add(((0, 0), (2, 1)), (own_link, part_link, own_chip, part_chip, own, near), "add_first")
    coarse = add(((3, 3), (1, 2)), (far_link, near_link, far_chip, near_chip, far, part), "add_second", coarse)
    return coarse.transpose(1, 0, 2)


def gathered(stiffness, block_cols, basis, patch_reach):
    blocks, slots, size, _ = stiffness.shape
    rows, groups, width = basis.shape
    slabs = lax.axis_size("blk")
    slab = lax.axis_index("blk")
    total_blocks = blocks * slabs
    ring = [(i, (i + 1) % slabs) for i in range(slabs)]
    back = [(j, i) for i, j in ring]
    low = lax.dynamic_index_in_dim(patch_reach, (slab - 1) % slabs, 0, False)[:, 1]
    high = lax.dynamic_index_in_dim(patch_reach, (slab + 1) % slabs, 0, False)[:, 0]
    block_row = jnp.arange(rows, dtype=jnp.int32) // size
    lower = block_row[:, None] < low[None, :]
    upper = block_row[:, None] >= blocks - high[None, :]
    support = jnp.stack([lower, jnp.ones_like(lower), upper], 1)
    masked = jnp.where(support, basis, jnp.zeros_like(basis))
    rim = RIM * size
    before = lax.ppermute(masked[rows - rim :, 1:], "blk", ring)
    after = lax.ppermute(masked[:rim, :2], "blk", back)
    none = jnp.zeros((rim, 1, width), masked.dtype)
    extended = jnp.concatenate(
        [jnp.concatenate([before, none], 1), masked, jnp.concatenate([none, after], 1)], 0
    ).reshape(blocks + 2 * RIM, size, groups * width)
    position = (block_cols - slab * blocks + RIM) % total_blocks
    picked = jnp.take(extended, position, axis=0)
    image = jnp.einsum("rsij,rsjc->ric", stiffness, picked, preferred_element_type=F32)
    image = image.astype(BF16).reshape(rows, groups, width)
    image = lax.all_gather(image, "col", axis=2, tiled=True)
    tiles = jnp.einsum("rgl,rhc->glhc", masked, image, preferred_element_type=F32)
    from_prev = lax.ppermute(tiles[2], "blk", ring)
    from_next = lax.ppermute(tiles[0], "blk", back)

    def place(tile, offset):
        return jnp.pad(tile, ((0, 0), (offset, 2 - offset), (0, 0)))

    return place(from_prev, 0) + place(tiles[1], 1) + place(from_next, 2)


def solution(mesh):
    in_specs = (
        P("blk", None, None, None),
        P("blk", None),
        P("blk", None, "col"),
        P(None, "col", None),
    )
    out_specs = P(("blk", "col"), None, None)
    body = shards if mesh.shape["col"] == 4 and mesh.shape["blk"] % 2 == 0 else gathered
    return jax.shard_map(body, mesh=mesh, in_specs=in_specs, out_specs=out_specs, check_vma=False)
```

```python
import functools

import jax
import jax.numpy as jnp
from jax import lax
from jax.experimental import pallas as pl
from jax.experimental.pallas import tpu as pltpu
from jax.sharding import PartitionSpec as P

BF16 = jnp.bfloat16
F32 = jnp.float32
VMEM = pl.BlockSpec(memory_space=pltpu.VMEM)
SMEM = pl.BlockSpec(memory_space=pltpu.SMEM)
HBM = pl.BlockSpec(memory_space=pltpu.HBM)
RIM = 2


def shape(dims, dtype):
    return jax.ShapeDtypeStruct(dims, dtype)


def dot(left, right):
    return jnp.dot(left, right, preferred_element_type=F32)


def call(kernel, out_shape, in_specs, out_specs, args, scratch=(), flops=0, aliases=None, name=None):
    outs = jax.tree.leaves(out_shape)
    moved = sum(x.size * x.dtype.itemsize for x in (*args, *outs))
    return pl.pallas_call(
        kernel,
        out_shape=out_shape,
        in_specs=in_specs,
        out_specs=out_specs,
        scratch_shapes=list(scratch),
        input_output_aliases=aliases or {},
        cost_estimate=pl.CostEstimate(flops=flops, bytes_accessed=moved, transcendentals=0),
        compiler_params=pltpu.CompilerParams(vmem_limit_bytes=24 << 20),
        name=name,
    )(*args)


def block_image(stiffness, source, b, block_size, starts):
    blocks = [source[pl.ds(pl.multiple_of(start * block_size, block_size), block_size), :] for start in starts]
    left = jnp.concatenate([stiffness[b, k] for k in range(len(starts))], axis=1)
    return dot(left, jnp.concatenate(blocks, axis=0)).astype(BF16)


def positions(cols, b, blocks, slots, total_blocks):
    first = lax.axis_index("blk") * blocks
    return [
        jnp.clip(lax.rem(cols[k, b] - first + RIM + total_blocks, total_blocks), 0, blocks + 2 * RIM - 1)
        for k in range(slots)
    ]


def reaches(reach):
    slabs = reach.shape[0]
    slab = lax.axis_index("blk")
    low = reach[pl.ds(lax.rem(slab + slabs - 1, slabs), 1), 1, :]
    high = reach[pl.ds(lax.rem(slab + 1, slabs), 1), 0, :]
    return low, high


def mask_block(basis, b, blocks, size, low, high, masked):
    groups, _, width = basis.shape
    rows = slice(b * size, (b + 1) * size)
    keep = {0: (b < low).astype(F32).astype(BF16), 2: (b >= blocks - high).astype(F32).astype(BF16)}
    for g in range(groups):
        value = basis[g, rows, :]
        masked[rows, g * width : (g + 1) * width] = value * keep[g] if g in keep else value


def mask_and_inner(
    total_blocks, cols_hbm, basis_hbm, reach_hbm, stiffness_hbm, masked, to_link, to_chip, inner, cols, basis, reach, stiffness, sem
):
    blocks, slots, size, _ = stiffness.shape
    width = basis.shape[2]
    inner_blocks = pl.ds(RIM, blocks - 2 * RIM)
    moves = [(reach_hbm, reach), (cols_hbm, cols)]
    moves += [
        (basis_hbm.at[:, pl.ds(b * size, RIM * size)], basis.at[:, pl.ds(b * size, RIM * size)])
        for b in range(0, blocks, RIM)
    ]
    moves.append((stiffness_hbm.at[inner_blocks], stiffness.at[inner_blocks]))
    copies = [pltpu.make_async_copy(source, target, sem.at[n]) for n, (source, target) in enumerate(moves)]
    for copy in copies:
        copy.start()
    copies[0].wait()
    low, high = reaches(reach)
    for b in range(blocks):
        if b % RIM == 0:
            copies[2 + b // RIM].wait()
        mask_block(basis, b, blocks, size, low, high, masked)
    odd = parity()

    @pl.when(odd == 0)
    def _():
        to_link[...] = masked[: RIM * size, : 2 * width]
        to_chip[...] = masked[(blocks - RIM) * size :, width:]

    @pl.when(odd == 1)
    def _():
        to_link[...] = masked[(blocks - RIM) * size :, width:]
        to_chip[...] = masked[: RIM * size, : 2 * width]

    copies[1].wait()
    copies[-1].wait()
    for b in range(RIM, blocks - RIM):
        starts = [jnp.clip(p - RIM, 0, blocks - 1) for p in positions(cols, b, blocks, slots, total_blocks)]
        inner[(b - RIM) * size : (b - RIM + 1) * size, :] = block_image(stiffness, masked, b, size, starts)


def outer_image(total_blocks, cols, stiffness, masked, from_link, from_chip, outer, extended):
    blocks, slots, size, _ = stiffness.shape
    rows, wide = masked.shape
    rim = RIM * size
    width = wide // 3
    odd = parity()

    @pl.when(odd == 0)
    def _():
        extended[:rim, : 2 * width] = from_link[...]
        extended[rim + rows :, width:] = from_chip[...]

    @pl.when(odd == 1)
    def _():
        extended[:rim, : 2 * width] = from_chip[...]
        extended[rim + rows :, width:] = from_link[...]

    extended[:rim, 2 * width :] = jnp.zeros((rim, width), BF16)
    extended[rim : rim + rows, :] = masked[...]
    extended[rim + rows :, :width] = jnp.zeros((rim, width), BF16)
    for n, b in enumerate([*range(RIM), *range(blocks - RIM, blocks)]):
        starts = positions(cols, b, blocks, slots, total_blocks)
        outer[n * size : (n + 1) * size, :] = block_image(stiffness, extended, b, size, starts)


def parity():
    return lax.rem(lax.axis_index("blk"), 2)


def store_tile(tile, own, link, chip):
    width = tile.shape[0] // 3
    odd = parity()
    own[...] = tile[width : 2 * width].astype(own.dtype)
    down, up = tile[:width].astype(BF16), tile[2 * width :].astype(BF16)

    @pl.when(odd == 0)
    def _():
        link[...] = down
        chip[...] = up

    @pl.when(odd == 1)
    def _():
        link[...] = up
        chip[...] = down


def turn(size, masked, left_inner, left_outer):
    rows = masked.shape[0]
    rim = RIM * size
    left_inner[...] = masked[rim : rows - rim, :].T
    left_outer[:, :rim] = masked[:rim, :].T
    left_outer[:, rim:] = masked[rows - rim :, :].T


def own_tile(size, masked, inner, outer, own, link, chip, left_inner, left_outer):
    turn(size, masked, left_inner, left_outer)
    store_tile(dot(left_inner[...], inner[...]) + dot(left_outer[...], outer[...]), own, link, chip)


def partner_tile(
    size, basis, reach, inner, outer, near_left, inner_r, own, link, chip, far_outer, far, near, masked, far_inner
):
    low, high = reaches(reach)
    blocks = basis.shape[1] // size
    for b in range(blocks):
        mask_block(basis, b, blocks, size, low, high, masked)
    turn(size, masked, far_inner, far_outer)
    store_tile(dot(far_inner[...], inner[...]) + dot(far_outer[...], outer[...]), own, link, chip)
    far[...] = dot(far_inner[...], inner_r[...])
    near[...] = dot(near_left[...], inner_r[...])


def late_tiles(
    part,
    part_link,
    part_chip,
    far_base,
    near_base,
    far_outer,
    near_outer,
    outer_r,
    near,
    near_link,
    near_chip,
    far,
    far_link,
    far_chip,
):
    wide = outer_r.shape[1]
    far[:, :wide] = part[...]
    far_link[:, :wide] = part_link[...]
    far_chip[:, :wide] = part_chip[...]
    tile = far_base[...] + dot(far_outer[...], outer_r[...])
    store_tile(tile, far.at[:, wide:], far_link.at[:, wide:], far_chip.at[:, wide:])
    store_tile(near_base[...] + dot(near_outer[...], outer_r[...]), near, near_link, near_chip)


def add_tiles(steps, *refs):
    count = len(steps)
    terms = refs[: 3 * count]
    coarse, total, sem = refs[-3:]
    width = total.shape[2]
    me = lax.axis_index("col")
    even = parity() == 0
    copies = []
    for n, ((even_step, odd_step), chunks) in enumerate(steps):
        chip, link, own = (
            terms[n + k * count][:, m * 3 * width : (m + 1) * 3 * width].astype(F32) for k, m in enumerate(chunks)
        )
        prev = jnp.where(even, link, chip)
        nxt = jnp.where(even, chip, link)
        for d in range(5):
            value = None
            for offset, term in ((0, prev), (1, own), (2, nxt)):
                if 0 <= d - offset <= 2:
                    part = term[:, (d - offset) * width : (d - offset + 1) * width]
                    value = part if value is None else value + part
            total[n, d] = value
        column = lax.bitwise_xor(me, jnp.where(even, even_step, odd_step))
        start = pl.multiple_of(column * width, width)
        copy = pltpu.make_async_copy(total.at[n], coarse.at[:, :, pl.ds(start, width)], sem.at[n])
        copy.start()
        copies.append(copy)
    for copy in copies:
        copy.wait()


def tile_shapes(width, wide, own):
    return shape((width, wide), own), shape((width, wide), BF16), shape((width, wide), BF16)


def shards(stiffness, block_cols, basis, patch_reach):
    blocks, slots, size, _ = stiffness.shape
    rows, groups, width = basis.shape
    wide = groups * width
    slabs = lax.axis_size("blk")
    total_blocks = blocks * slabs
    pairs = [(i, i ^ 1) for i in range(slabs)]
    cross = [(i, (i - 1 if i % 2 == 0 else i + 1) % slabs) for i in range(slabs)]

    def over_chip(value):
        return lax.ppermute(value, "blk", pairs)

    def over_link(value):
        return lax.ppermute(value, "blk", cross)

    def to(value, slab_of, column_of):
        perm = [(4 * i + q, 4 * (slab_of(i) % slabs) + column_of(i, q)) for i in range(slabs) for q in range(4)]
        return lax.ppermute(value, ("blk", "col"), perm)

    def partner(i, q):
        return q ^ (1 + i % 2)

    def side(i, q):
        return q ^ (2 - i % 2)

    def to_partner(value):
        return to(value, lambda i: i, partner)

    def to_side(value):
        return to(value, lambda i: i, side)

    def to_partner_link(value):
        return to(value, lambda i: i + 1 if i % 2 else i - 1, partner)

    basis_p = to_partner(basis).transpose(1, 0, 2)
    reach_p = to_partner(patch_reach).transpose(0, 2, 1)
    cols = block_cols.T
    flat = basis.transpose(1, 0, 2)
    reach = patch_reach.transpose(0, 2, 1)
    inner_rows = (blocks - 2 * RIM) * size
    rim = RIM * size
    row_flops = 2 * slots * size * size * wide
    masked, rim_link, rim_chip, inner = call(
        functools.partial(mask_and_inner, total_blocks),
        (shape((rows, wide), BF16), shape((rim, 2 * width), BF16), shape((rim, 2 * width), BF16), shape((inner_rows, wide), BF16)),
        [HBM] * 4,
        [VMEM] * 4,
        tuple(pltpu.with_memory_space_constraint(x, pltpu.HBM) for x in (cols, flat, reach, stiffness)),
        scratch=[
            pltpu.SMEM(cols.shape, cols.dtype),
            pltpu.VMEM(flat.shape, BF16),
            pltpu.VMEM(reach.shape, reach.dtype),
            pltpu.VMEM(stiffness.shape, BF16),
            pltpu.SemaphoreType.DMA((3 + blocks // RIM,)),
        ],
        flops=row_flops * (blocks - 2 * RIM),
        name="mask_and_inner",
    )
    inner_r = to_side(inner)
    rim_link = over_link(rim_link)
    rim_chip = over_chip(rim_chip)
    outer = call(
        functools.partial(outer_image, total_blocks),
        shape((2 * rim, wide), BF16),
        [SMEM] + [VMEM] * 4,
        VMEM,
        (cols, stiffness, masked, rim_link, rim_chip),
        scratch=[pltpu.VMEM((rows + 2 * rim, wide), BF16)],
        flops=row_flops * 2 * RIM,
        name="outer_image",
    )
    outer_r = to_side(outer)
    tile_flops = 2 * rows * wide * wide
    left_shapes = (shape((wide, inner_rows), BF16), shape((wide, 2 * rim), BF16))
    base_shape = shape((wide, wide), F32)

    own, own_link, own_chip, left_inner, left_outer = call(
        functools.partial(own_tile, size),
        (*tile_shapes(width, wide, F32), *left_shapes),
        [VMEM] * 3,
        [VMEM] * 5,
        (masked, inner, outer),
        flops=tile_flops,
        name="own_tile",
    )
    own_link, own_chip = over_link(own_link), over_chip(own_chip)
    part, part_link, part_chip, far_outer, far_base, near_base = call(
        functools.partial(partner_tile, size),
        (*tile_shapes(width, wide, BF16), left_shapes[1], base_shape, base_shape),
        [VMEM] * 6,
        [VMEM] * 6,
        (basis_p, reach_p, inner, outer, left_inner, inner_r),
        scratch=[pltpu.VMEM((rows, wide), BF16), pltpu.VMEM((wide, inner_rows), BF16)],
        flops=2 * tile_flops,
        name="partner_tile",
    )
    outer_r, own_link, own_chip, far_base = lax.optimization_barrier((outer_r, own_link, own_chip, far_base))
    near, near_link, near_chip, far, far_link, far_chip = call(
        late_tiles,
        (*tile_shapes(width, wide, F32), *(shape((width, 2 * wide), BF16),) * 3),
        [VMEM] * 8,
        [VMEM] * 6,
        (part, part_link, part_chip, far_base, near_base, far_outer, left_outer, outer_r),
        flops=tile_flops,
        name="late_tiles",
    )
    far_link = to_partner_link(far_link)
    near_link = over_link(near_link)
    far_chip = to(far_chip, lambda i: i ^ 1, partner)
    far = to_partner(far)
    near_chip = over_chip(near_chip)

    def add(steps, terms, name, base=None):
        extra = () if base is None else (base,)
        return call(
            functools.partial(add_tiles, steps),
            shape((5, width, 4 * width), F32),
            [VMEM] * len(terms) + [HBM] * len(extra),
            HBM,
            (*terms, *extra),
            scratch=[pltpu.VMEM((len(steps), 5, width, width), F32), pltpu.SemaphoreType.DMA((len(steps),))],
            flops=5 * len(steps) * width * width,
            aliases={len(terms): 0} if extra else None,
            name=name,
        )

    coarse = add((((0, 0), (0, 0, 0)),), (own_chip, own_link, own), "add_own")
    coarse = add(
        (((3, 3), (1, 1, 1)), ((1, 2), (0, 0, 0)), ((2, 1), (0, 0, 0))),
        (far_chip, near_chip, far_chip, far_link, near_link, far_link, far, far, near),
        "add_rest",
        coarse,
    )
    return coarse.transpose(1, 0, 2)


def gathered(stiffness, block_cols, basis, patch_reach):
    blocks, slots, size, _ = stiffness.shape
    rows, groups, width = basis.shape
    slabs = lax.axis_size("blk")
    slab = lax.axis_index("blk")
    total_blocks = blocks * slabs
    ring = [(i, (i + 1) % slabs) for i in range(slabs)]
    back = [(j, i) for i, j in ring]
    low = lax.dynamic_index_in_dim(patch_reach, (slab - 1) % slabs, 0, False)[:, 1]
    high = lax.dynamic_index_in_dim(patch_reach, (slab + 1) % slabs, 0, False)[:, 0]
    block_row = jnp.arange(rows, dtype=jnp.int32) // size
    lower = block_row[:, None] < low[None, :]
    upper = block_row[:, None] >= blocks - high[None, :]
    support = jnp.stack([lower, jnp.ones_like(lower), upper], 1)
    masked = jnp.where(support, basis, jnp.zeros_like(basis))
    rim = RIM * size
    before = lax.ppermute(masked[rows - rim :, 1:], "blk", ring)
    after = lax.ppermute(masked[:rim, :2], "blk", back)
    none = jnp.zeros((rim, 1, width), masked.dtype)
    extended = jnp.concatenate(
        [jnp.concatenate([before, none], 1), masked, jnp.concatenate([none, after], 1)], 0
    ).reshape(blocks + 2 * RIM, size, groups * width)
    position = (block_cols - slab * blocks + RIM) % total_blocks
    picked = jnp.take(extended, position, axis=0)
    image = jnp.einsum("rsij,rsjc->ric", stiffness, picked, preferred_element_type=F32)
    image = image.astype(BF16).reshape(rows, groups, width)
    image = lax.all_gather(image, "col", axis=2, tiled=True)
    tiles = jnp.einsum("rgl,rhc->glhc", masked, image, preferred_element_type=F32)
    from_prev = lax.ppermute(tiles[2], "blk", ring)
    from_next = lax.ppermute(tiles[0], "blk", back)

    def place(tile, offset):
        return jnp.pad(tile, ((0, 0), (offset, 2 - offset), (0, 0)))

    return place(from_prev, 0) + place(tiles[1], 1) + place(from_next, 2)


def solution(mesh):
    in_specs = (
        P("blk", None, None, None),
        P("blk", None),
        P("blk", None, "col"),
        P(None, "col", None),
    )
    out_specs = P(("blk", "col"), None, None)
    body = shards if mesh.shape["col"] == 4 and mesh.shape["blk"] % 2 == 0 else gathered
    return jax.shard_map(body, mesh=mesh, in_specs=in_specs, out_specs=out_specs, check_vma=False)
```

```python
import functools

import jax
import jax.numpy as jnp
from jax import lax
from jax.experimental import pallas as pl
from jax.experimental.pallas import tpu as pltpu
from jax.sharding import PartitionSpec as P

BF16 = jnp.bfloat16
F32 = jnp.float32
VMEM = pl.BlockSpec(memory_space=pltpu.VMEM)
SMEM = pl.BlockSpec(memory_space=pltpu.SMEM)
HBM = pl.BlockSpec(memory_space=pltpu.HBM)
RIM = 2


def shape(dims, dtype):
    return jax.ShapeDtypeStruct(dims, dtype)


def dot(left, right):
    return jnp.dot(left, right, preferred_element_type=F32)


def call(kernel, out_shape, in_specs, out_specs, args, scratch=(), flops=0, aliases=None, name=None):
    outs = jax.tree.leaves(out_shape)
    moved = sum(x.size * x.dtype.itemsize for x in (*args, *outs))
    return pl.pallas_call(
        kernel,
        out_shape=out_shape,
        in_specs=in_specs,
        out_specs=out_specs,
        scratch_shapes=list(scratch),
        input_output_aliases=aliases or {},
        cost_estimate=pl.CostEstimate(flops=flops, bytes_accessed=moved, transcendentals=0),
        compiler_params=pltpu.CompilerParams(vmem_limit_bytes=24 << 20),
        name=name,
    )(*args)


def block_image(stiffness, source, b, block_size, starts):
    blocks = [source[pl.ds(pl.multiple_of(start * block_size, block_size), block_size), :] for start in starts]
    left = jnp.concatenate([stiffness[b, k] for k in range(len(starts))], axis=1)
    return dot(left, jnp.concatenate(blocks, axis=0)).astype(BF16)


def positions(cols, b, blocks, slots, total_blocks):
    first = lax.axis_index("blk") * blocks
    return [
        jnp.clip(lax.rem(cols[k, b] - first + RIM + total_blocks, total_blocks), 0, blocks + 2 * RIM - 1)
        for k in range(slots)
    ]


def reaches(reach):
    slabs = reach.shape[0]
    slab = lax.axis_index("blk")
    low = reach[pl.ds(lax.rem(slab + slabs - 1, slabs), 1), 1, :]
    high = reach[pl.ds(lax.rem(slab + 1, slabs), 1), 0, :]
    return low, high


def mask_block(basis, b, blocks, size, low, high, masked):
    groups, _, width = basis.shape
    rows = slice(b * size, (b + 1) * size)
    keep = {0: (b < low).astype(F32).astype(BF16), 2: (b >= blocks - high).astype(F32).astype(BF16)}
    for g in range(groups):
        value = basis[g, rows, :]
        masked[rows, g * width : (g + 1) * width] = value * keep[g] if g in keep else value


def mask_and_inner(
    total_blocks, cols_hbm, basis_hbm, reach_hbm, stiffness_hbm, masked, to_link, to_chip, inner, cols, basis, reach, stiffness, sem
):
    blocks, slots, size, _ = stiffness.shape
    width = basis.shape[2]
    inner_blocks = pl.ds(RIM, blocks - 2 * RIM)
    moves = [(reach_hbm, reach), (cols_hbm, cols)]
    moves += [
        (basis_hbm.at[:, pl.ds(b * size, RIM * size)], basis.at[:, pl.ds(b * size, RIM * size)])
        for b in range(0, blocks, RIM)
    ]
    moves.append((stiffness_hbm.at[inner_blocks], stiffness.at[inner_blocks]))
    copies = [pltpu.make_async_copy(source, target, sem.at[n]) for n, (source, target) in enumerate(moves)]
    for copy in copies:
        copy.start()
    copies[0].wait()
    low, high = reaches(reach)
    for b in range(blocks):
        if b % RIM == 0:
            copies[2 + b // RIM].wait()
        mask_block(basis, b, blocks, size, low, high, masked)
    odd = parity()

    @pl.when(odd == 0)
    def _():
        to_link[...] = masked[: RIM * size, : 2 * width]
        to_chip[...] = masked[(blocks - RIM) * size :, width:]

    @pl.when(odd == 1)
    def _():
        to_link[...] = masked[(blocks - RIM) * size :, width:]
        to_chip[...] = masked[: RIM * size, : 2 * width]

    copies[1].wait()
    copies[-1].wait()
    for b in range(RIM, blocks - RIM):
        starts = [jnp.clip(p - RIM, 0, blocks - 1) for p in positions(cols, b, blocks, slots, total_blocks)]
        inner[(b - RIM) * size : (b - RIM + 1) * size, :] = block_image(stiffness, masked, b, size, starts)


def outer_image(total_blocks, cols, stiffness, masked, from_link, from_chip, outer, extended):
    blocks, slots, size, _ = stiffness.shape
    rows, wide = masked.shape
    rim = RIM * size
    width = wide // 3
    odd = parity()

    @pl.when(odd == 0)
    def _():
        extended[:rim, : 2 * width] = from_link[...]
        extended[rim + rows :, width:] = from_chip[...]

    @pl.when(odd == 1)
    def _():
        extended[:rim, : 2 * width] = from_chip[...]
        extended[rim + rows :, width:] = from_link[...]

    extended[:rim, 2 * width :] = jnp.zeros((rim, width), BF16)
    extended[rim : rim + rows, :] = masked[...]
    extended[rim + rows :, :width] = jnp.zeros((rim, width), BF16)
    for n, b in enumerate([*range(RIM), *range(blocks - RIM, blocks)]):
        starts = positions(cols, b, blocks, slots, total_blocks)
        outer[n * size : (n + 1) * size, :] = block_image(stiffness, extended, b, size, starts)


def parity():
    return lax.rem(lax.axis_index("blk"), 2)


def store_tile(tile, own, link, chip):
    width = tile.shape[0] // 3
    odd = parity()
    own[...] = tile[width : 2 * width].astype(own.dtype)
    down, up = tile[:width].astype(BF16), tile[2 * width :].astype(BF16)

    @pl.when(odd == 0)
    def _():
        link[...] = down
        chip[...] = up

    @pl.when(odd == 1)
    def _():
        link[...] = up
        chip[...] = down


def turn(size, masked, left_inner, left_outer):
    rows = masked.shape[0]
    rim = RIM * size
    left_inner[...] = masked[rim : rows - rim, :].T
    left_outer[:, :rim] = masked[:rim, :].T
    left_outer[:, rim:] = masked[rows - rim :, :].T


def own_tile(size, masked, inner, outer, own, link, chip, left_inner, left_outer):
    turn(size, masked, left_inner, left_outer)
    store_tile(dot(left_inner[...], inner[...]) + dot(left_outer[...], outer[...]), own, link, chip)


def partner_tile(
    size, basis, reach, inner, outer, near_left, inner_r, own, link, chip, far_outer, far, near, masked, far_inner
):
    low, high = reaches(reach)
    blocks = basis.shape[1] // size
    for b in range(blocks):
        mask_block(basis, b, blocks, size, low, high, masked)
    turn(size, masked, far_inner, far_outer)
    store_tile(dot(far_inner[...], inner[...]) + dot(far_outer[...], outer[...]), own, link, chip)
    far[...] = dot(far_inner[...], inner_r[...])
    near[...] = dot(near_left[...], inner_r[...])


def late_tiles(
    part,
    part_chip,
    far_base,
    near_base,
    far_outer,
    near_outer,
    outer_r,
    near,
    near_link,
    near_chip,
    far,
    far_link,
    far_chip,
):
    wide = outer_r.shape[1]
    far[:, :wide] = part[...]
    far_chip[:, :wide] = part_chip[...]
    tile = far_base[...] + dot(far_outer[...], outer_r[...])
    store_tile(tile, far.at[:, wide:], far_link, far_chip.at[:, wide:])
    store_tile(near_base[...] + dot(near_outer[...], outer_r[...]), near, near_link, near_chip)


def add_tiles(steps, *refs):
    count = len(steps)
    terms = refs[: 3 * count]
    coarse, total, sem = refs[-3:]
    width = total.shape[2]
    me = lax.axis_index("col")
    even = parity() == 0
    copies = []
    for n, ((even_step, odd_step), chunks) in enumerate(steps):
        chip, link, own = (
            terms[n + k * count][:, m * 3 * width : (m + 1) * 3 * width].astype(F32) for k, m in enumerate(chunks)
        )
        prev = jnp.where(even, link, chip)
        nxt = jnp.where(even, chip, link)
        for d in range(5):
            value = None
            for offset, term in ((0, prev), (1, own), (2, nxt)):
                if 0 <= d - offset <= 2:
                    part = term[:, (d - offset) * width : (d - offset + 1) * width]
                    value = part if value is None else value + part
            total[n, d] = value
        column = lax.bitwise_xor(me, jnp.where(even, even_step, odd_step))
        start = pl.multiple_of(column * width, width)
        copy = pltpu.make_async_copy(total.at[n], coarse.at[:, :, pl.ds(start, width)], sem.at[n])
        copy.start()
        copies.append(copy)
    for copy in copies:
        copy.wait()


def tile_shapes(width, wide, own):
    return shape((width, wide), own), shape((width, wide), BF16), shape((width, wide), BF16)


def shards(stiffness, block_cols, basis, patch_reach):
    blocks, slots, size, _ = stiffness.shape
    rows, groups, width = basis.shape
    wide = groups * width
    slabs = lax.axis_size("blk")
    total_blocks = blocks * slabs
    pairs = [(i, i ^ 1) for i in range(slabs)]
    cross = [(i, (i - 1 if i % 2 == 0 else i + 1) % slabs) for i in range(slabs)]

    def over_chip(value):
        return lax.ppermute(value, "blk", pairs)

    def over_link(value):
        return lax.ppermute(value, "blk", cross)

    def to(value, slab_of, column_of):
        perm = [(4 * i + q, 4 * (slab_of(i) % slabs) + column_of(i, q)) for i in range(slabs) for q in range(4)]
        return lax.ppermute(value, ("blk", "col"), perm)

    def partner(i, q):
        return q ^ (1 + i % 2)

    def side(i, q):
        return q ^ (2 - i % 2)

    def to_partner(value):
        return to(value, lambda i: i, partner)

    def to_side(value):
        return to(value, lambda i: i, side)

    def to_partner_link(value):
        return to(value, lambda i: i + 1 if i % 2 else i - 1, partner)

    basis_p = to_partner(basis).transpose(1, 0, 2)
    reach_p = to_partner(patch_reach).transpose(0, 2, 1)
    cols = block_cols.T
    flat = basis.transpose(1, 0, 2)
    reach = patch_reach.transpose(0, 2, 1)
    inner_rows = (blocks - 2 * RIM) * size
    rim = RIM * size
    row_flops = 2 * slots * size * size * wide
    masked, rim_link, rim_chip, inner = call(
        functools.partial(mask_and_inner, total_blocks),
        (shape((rows, wide), BF16), shape((rim, 2 * width), BF16), shape((rim, 2 * width), BF16), shape((inner_rows, wide), BF16)),
        [HBM] * 4,
        [VMEM] * 4,
        tuple(pltpu.with_memory_space_constraint(x, pltpu.HBM) for x in (cols, flat, reach, stiffness)),
        scratch=[
            pltpu.SMEM(cols.shape, cols.dtype),
            pltpu.VMEM(flat.shape, BF16),
            pltpu.VMEM(reach.shape, reach.dtype),
            pltpu.VMEM(stiffness.shape, BF16),
            pltpu.SemaphoreType.DMA((3 + blocks // RIM,)),
        ],
        flops=row_flops * (blocks - 2 * RIM),
        name="mask_and_inner",
    )
    inner_r = to_side(inner)
    rim_link = over_link(rim_link)
    rim_chip = over_chip(rim_chip)
    outer = call(
        functools.partial(outer_image, total_blocks),
        shape((2 * rim, wide), BF16),
        [SMEM] + [VMEM] * 4,
        VMEM,
        (cols, stiffness, masked, rim_link, rim_chip),
        scratch=[pltpu.VMEM((rows + 2 * rim, wide), BF16)],
        flops=row_flops * 2 * RIM,
        name="outer_image",
    )
    outer_r = to_side(outer)
    tile_flops = 2 * rows * wide * wide
    left_shapes = (shape((wide, inner_rows), BF16), shape((wide, 2 * rim), BF16))
    base_shape = shape((wide, wide), F32)

    own, own_link, own_chip, left_inner, left_outer = call(
        functools.partial(own_tile, size),
        (*tile_shapes(width, wide, F32), *left_shapes),
        [VMEM] * 3,
        [VMEM] * 5,
        (masked, inner, outer),
        flops=tile_flops,
        name="own_tile",
    )
    own_link, own_chip = over_link(own_link), over_chip(own_chip)
    part, part_link, part_chip, far_outer, far_base, near_base = call(
        functools.partial(partner_tile, size),
        (*tile_shapes(width, wide, BF16), left_shapes[1], base_shape, base_shape),
        [VMEM] * 6,
        [VMEM] * 6,
        (basis_p, reach_p, inner, outer, left_inner, inner_r),
        scratch=[pltpu.VMEM((rows, wide), BF16), pltpu.VMEM((wide, inner_rows), BF16)],
        flops=2 * tile_flops,
        name="partner_tile",
    )
    part_link = to_partner_link(part_link)
    outer_r, own_link, own_chip, far_base = lax.optimization_barrier((outer_r, own_link, own_chip, far_base))
    near, near_link, near_chip, far, far_link, far_chip = call(
        late_tiles,
        (
            *tile_shapes(width, wide, F32),
            shape((width, 2 * wide), BF16),
            shape((width, wide), BF16),
            shape((width, 2 * wide), BF16),
        ),
        [VMEM] * 7,
        [VMEM] * 6,
        (part, part_chip, far_base, near_base, far_outer, left_outer, outer_r),
        flops=tile_flops,
        name="late_tiles",
    )
    far, part_link = lax.optimization_barrier((far, part_link))
    far_link = to_partner_link(far_link)
    near_link = over_link(near_link)
    far_chip = to(far_chip, lambda i: i ^ 1, partner)
    far = to_partner(far)
    near_chip = over_chip(near_chip)

    def add(steps, terms, name, base=None):
        extra = () if base is None else (base,)
        return call(
            functools.partial(add_tiles, steps),
            shape((5, width, 4 * width), F32),
            [VMEM] * len(terms) + [HBM] * len(extra),
            HBM,
            (*terms, *extra),
            scratch=[pltpu.VMEM((len(steps), 5, width, width), F32), pltpu.SemaphoreType.DMA((len(steps),))],
            flops=5 * len(steps) * width * width,
            aliases={len(terms): 0} if extra else None,
            name=name,
        )

    coarse = add((((0, 0), (0, 0, 0)),), (own_chip, own_link, own), "add_own")
    coarse = add(
        (((3, 3), (1, 0, 1)), ((1, 2), (0, 0, 0)), ((2, 1), (0, 0, 0))),
        (far_chip, near_chip, far_chip, far_link, near_link, part_link, far, far, near),
        "add_rest",
        coarse,
    )
    return coarse.transpose(1, 0, 2)


def gathered(stiffness, block_cols, basis, patch_reach):
    blocks, slots, size, _ = stiffness.shape
    rows, groups, width = basis.shape
    slabs = lax.axis_size("blk")
    slab = lax.axis_index("blk")
    total_blocks = blocks * slabs
    ring = [(i, (i + 1) % slabs) for i in range(slabs)]
    back = [(j, i) for i, j in ring]
    low = lax.dynamic_index_in_dim(patch_reach, (slab - 1) % slabs, 0, False)[:, 1]
    high = lax.dynamic_index_in_dim(patch_reach, (slab + 1) % slabs, 0, False)[:, 0]
    block_row = jnp.arange(rows, dtype=jnp.int32) // size
    lower = block_row[:, None] < low[None, :]
    upper = block_row[:, None] >= blocks - high[None, :]
    support = jnp.stack([lower, jnp.ones_like(lower), upper], 1)
    masked = jnp.where(support, basis, jnp.zeros_like(basis))
    rim = RIM * size
    before = lax.ppermute(masked[rows - rim :, 1:], "blk", ring)
    after = lax.ppermute(masked[:rim, :2], "blk", back)
    none = jnp.zeros((rim, 1, width), masked.dtype)
    extended = jnp.concatenate(
        [jnp.concatenate([before, none], 1), masked, jnp.concatenate([none, after], 1)], 0
    ).reshape(blocks + 2 * RIM, size, groups * width)
    position = (block_cols - slab * blocks + RIM) % total_blocks
    picked = jnp.take(extended, position, axis=0)
    image = jnp.einsum("rsij,rsjc->ric", stiffness, picked, preferred_element_type=F32)
    image = image.astype(BF16).reshape(rows, groups, width)
    image = lax.all_gather(image, "col", axis=2, tiled=True)
    tiles = jnp.einsum("rgl,rhc->glhc", masked, image, preferred_element_type=F32)
    from_prev = lax.ppermute(tiles[2], "blk", ring)
    from_next = lax.ppermute(tiles[0], "blk", back)

    def place(tile, offset):
        return jnp.pad(tile, ((0, 0), (offset, 2 - offset), (0, 0)))

    return place(from_prev, 0) + place(tiles[1], 1) + place(from_next, 2)


def solution(mesh):
    in_specs = (
        P("blk", None, None, None),
        P("blk", None),
        P("blk", None, "col"),
        P(None, "col", None),
    )
    out_specs = P(("blk", "col"), None, None)
    body = shards if mesh.shape["col"] == 4 and mesh.shape["blk"] % 2 == 0 else gathered
    return jax.shard_map(body, mesh=mesh, in_specs=in_specs, out_specs=out_specs, check_vma=False)
```

```python
import functools

import jax
import jax.numpy as jnp
from jax import lax
from jax.experimental import pallas as pl
from jax.experimental.pallas import tpu as pltpu
from jax.sharding import PartitionSpec as P

BF16 = jnp.bfloat16
F32 = jnp.float32
VMEM = pl.BlockSpec(memory_space=pltpu.VMEM)
SMEM = pl.BlockSpec(memory_space=pltpu.SMEM)
HBM = pl.BlockSpec(memory_space=pltpu.HBM)
RIM = 2


def shape(dims, dtype):
    return jax.ShapeDtypeStruct(dims, dtype)


def dot(left, right):
    return jnp.dot(left, right, preferred_element_type=F32)


def call(kernel, out_shape, in_specs, out_specs, args, scratch=(), flops=0, aliases=None, name=None):
    outs = jax.tree.leaves(out_shape)
    moved = sum(x.size * x.dtype.itemsize for x in (*args, *outs))
    return pl.pallas_call(
        kernel,
        out_shape=out_shape,
        in_specs=in_specs,
        out_specs=out_specs,
        scratch_shapes=list(scratch),
        input_output_aliases=aliases or {},
        cost_estimate=pl.CostEstimate(flops=flops, bytes_accessed=moved, transcendentals=0),
        compiler_params=pltpu.CompilerParams(vmem_limit_bytes=24 << 20),
        name=name,
    )(*args)


def block_image(stiffness, source, b, block_size, starts):
    blocks = [source[pl.ds(pl.multiple_of(start * block_size, block_size), block_size), :] for start in starts]
    left = jnp.concatenate([stiffness[b, k] for k in range(len(starts))], axis=1)
    return dot(left, jnp.concatenate(blocks, axis=0)).astype(BF16)


def positions(cols, b, blocks, slots, total_blocks):
    first = lax.axis_index("blk") * blocks
    return [
        jnp.clip(lax.rem(cols[k, b] - first + RIM + total_blocks, total_blocks), 0, blocks + 2 * RIM - 1)
        for k in range(slots)
    ]


def reaches(reach):
    slabs = reach.shape[0]
    slab = lax.axis_index("blk")
    low = reach[pl.ds(lax.rem(slab + slabs - 1, slabs), 1), 1, :]
    high = reach[pl.ds(lax.rem(slab + 1, slabs), 1), 0, :]
    return low, high


def mask_block(basis, b, blocks, size, low, high, masked):
    groups, _, width = basis.shape
    rows = slice(b * size, (b + 1) * size)
    keep = {0: (b < low).astype(F32).astype(BF16), 2: (b >= blocks - high).astype(F32).astype(BF16)}
    for g in range(groups):
        value = basis[g, rows, :]
        masked[rows, g * width : (g + 1) * width] = value * keep[g] if g in keep else value


def mask_and_inner(
    total_blocks, cols_hbm, basis_hbm, reach_hbm, stiffness_hbm, masked, to_link, to_chip, inner, cols, basis, reach, stiffness, sem
):
    blocks, slots, size, _ = stiffness.shape
    width = basis.shape[2]
    inner_blocks = pl.ds(RIM, blocks - 2 * RIM)
    moves = [(reach_hbm, reach), (cols_hbm, cols)]
    moves += [
        (basis_hbm.at[:, pl.ds(b * size, RIM * size)], basis.at[:, pl.ds(b * size, RIM * size)])
        for b in range(0, blocks, RIM)
    ]
    moves.append((stiffness_hbm.at[inner_blocks], stiffness.at[inner_blocks]))
    copies = [pltpu.make_async_copy(source, target, sem.at[n]) for n, (source, target) in enumerate(moves)]
    for copy in copies:
        copy.start()
    copies[0].wait()
    low, high = reaches(reach)
    for b in range(blocks):
        if b % RIM == 0:
            copies[2 + b // RIM].wait()
        mask_block(basis, b, blocks, size, low, high, masked)
    odd = parity()

    @pl.when(odd == 0)
    def _():
        to_link[...] = masked[: RIM * size, : 2 * width]
        to_chip[...] = masked[(blocks - RIM) * size :, width:]

    @pl.when(odd == 1)
    def _():
        to_link[...] = masked[(blocks - RIM) * size :, width:]
        to_chip[...] = masked[: RIM * size, : 2 * width]

    copies[1].wait()
    copies[-1].wait()
    for b in range(RIM, blocks - RIM):
        starts = [jnp.clip(p - RIM, 0, blocks - 1) for p in positions(cols, b, blocks, slots, total_blocks)]
        inner[(b - RIM) * size : (b - RIM + 1) * size, :] = block_image(stiffness, masked, b, size, starts)


def outer_image(total_blocks, cols, stiffness, masked, from_link, from_chip, outer, extended):
    blocks, slots, size, _ = stiffness.shape
    rows, wide = masked.shape
    rim = RIM * size
    width = wide // 3
    odd = parity()

    @pl.when(odd == 0)
    def _():
        extended[:rim, : 2 * width] = from_link[...]
        extended[rim + rows :, width:] = from_chip[...]

    @pl.when(odd == 1)
    def _():
        extended[:rim, : 2 * width] = from_chip[...]
        extended[rim + rows :, width:] = from_link[...]

    extended[:rim, 2 * width :] = jnp.zeros((rim, width), BF16)
    extended[rim : rim + rows, :] = masked[...]
    extended[rim + rows :, :width] = jnp.zeros((rim, width), BF16)
    for n, b in enumerate([*range(RIM), *range(blocks - RIM, blocks)]):
        starts = positions(cols, b, blocks, slots, total_blocks)
        outer[n * size : (n + 1) * size, :] = block_image(stiffness, extended, b, size, starts)


def parity():
    return lax.rem(lax.axis_index("blk"), 2)


def store_tile(tile, own, link, chip):
    width = tile.shape[0] // 3
    odd = parity()
    own[...] = tile[width : 2 * width].astype(own.dtype)
    down, up = tile[:width].astype(BF16), tile[2 * width :].astype(BF16)

    @pl.when(odd == 0)
    def _():
        link[...] = down
        chip[...] = up

    @pl.when(odd == 1)
    def _():
        link[...] = up
        chip[...] = down


def turn(size, masked, left_inner, left_outer):
    rows = masked.shape[0]
    rim = RIM * size
    left_inner[...] = masked[rim : rows - rim, :].T
    left_outer[:, :rim] = masked[:rim, :].T
    left_outer[:, rim:] = masked[rows - rim :, :].T


def own_tile(size, masked, inner, outer, own, link, chip, left_inner, left_outer):
    turn(size, masked, left_inner, left_outer)
    store_tile(dot(left_inner[...], inner[...]) + dot(left_outer[...], outer[...]), own, link, chip)


def partner_tile(
    size, basis, reach, inner, outer, near_left, inner_r, own, link, chip, far_outer, far, near, masked, far_inner
):
    low, high = reaches(reach)
    blocks = basis.shape[1] // size
    for b in range(blocks):
        mask_block(basis, b, blocks, size, low, high, masked)
    turn(size, masked, far_inner, far_outer)
    store_tile(dot(far_inner[...], inner[...]) + dot(far_outer[...], outer[...]), own, link, chip)
    far[...] = dot(far_inner[...], inner_r[...])
    near[...] = dot(near_left[...], inner_r[...])


def late_tiles(
    part,
    part_link,
    part_chip,
    far_base,
    near_base,
    far_outer,
    near_outer,
    outer_r,
    near,
    near_link,
    near_chip,
    far,
    far_link,
    far_chip,
):
    wide = outer_r.shape[1]
    far[:, :wide] = part[...]
    far_link[:, :wide] = part_link[...]
    far_chip[:, :wide] = part_chip[...]
    tile = far_base[...] + dot(far_outer[...], outer_r[...])
    store_tile(tile, far.at[:, wide:], far_link.at[:, wide:], far_chip.at[:, wide:])
    store_tile(near_base[...] + dot(near_outer[...], outer_r[...]), near, near_link, near_chip)


def add_tiles(steps, *refs):
    count = len(steps)
    terms = refs[: 3 * count]
    coarse, total, sem = refs[-3:]
    width = total.shape[2]
    me = lax.axis_index("col")
    even = parity() == 0
    copies = []
    for n, ((even_step, odd_step), chunks) in enumerate(steps):
        link, own, chip = (
            terms[n + k * count][:, m * 3 * width : (m + 1) * 3 * width].astype(F32) for k, m in enumerate(chunks)
        )
        prev = jnp.where(even, link, chip)
        nxt = jnp.where(even, chip, link)
        for d in range(5):
            value = None
            for offset, term in ((0, prev), (1, own), (2, nxt)):
                if 0 <= d - offset <= 2:
                    part = term[:, (d - offset) * width : (d - offset + 1) * width]
                    value = part if value is None else value + part
            total[n, d] = value
        column = lax.bitwise_xor(me, jnp.where(even, even_step, odd_step))
        start = pl.multiple_of(column * width, width)
        copy = pltpu.make_async_copy(total.at[n], coarse.at[:, :, pl.ds(start, width)], sem.at[n])
        copy.start()
        copies.append(copy)
    for copy in copies:
        copy.wait()


def tile_shapes(width, wide, own):
    return shape((width, wide), own), shape((width, wide), BF16), shape((width, wide), BF16)


def shards(stiffness, block_cols, basis, patch_reach):
    blocks, slots, size, _ = stiffness.shape
    rows, groups, width = basis.shape
    wide = groups * width
    slabs = lax.axis_size("blk")
    total_blocks = blocks * slabs
    pairs = [(i, i ^ 1) for i in range(slabs)]
    cross = [(i, (i - 1 if i % 2 == 0 else i + 1) % slabs) for i in range(slabs)]

    def over_chip(value):
        return lax.ppermute(value, "blk", pairs)

    def over_link(value):
        return lax.ppermute(value, "blk", cross)

    def to(value, slab_of, column_of):
        perm = [(4 * i + q, 4 * (slab_of(i) % slabs) + column_of(i, q)) for i in range(slabs) for q in range(4)]
        return lax.ppermute(value, ("blk", "col"), perm)

    def partner(i, q):
        return q ^ (1 + i % 2)

    def side(i, q):
        return q ^ (2 - i % 2)

    def to_partner(value):
        return to(value, lambda i: i, partner)

    def to_side(value):
        return to(value, lambda i: i, side)

    def to_partner_link(value):
        return to(value, lambda i: i + 1 if i % 2 else i - 1, partner)

    basis_p = to_partner(basis).transpose(1, 0, 2)
    reach_p = to_partner(patch_reach).transpose(0, 2, 1)
    cols = block_cols.T
    flat = basis.transpose(1, 0, 2)
    reach = patch_reach.transpose(0, 2, 1)
    inner_rows = (blocks - 2 * RIM) * size
    rim = RIM * size
    row_flops = 2 * slots * size * size * wide
    masked, rim_link, rim_chip, inner = call(
        functools.partial(mask_and_inner, total_blocks),
        (shape((rows, wide), BF16), shape((rim, 2 * width), BF16), shape((rim, 2 * width), BF16), shape((inner_rows, wide), BF16)),
        [HBM] * 4,
        [VMEM] * 4,
        tuple(pltpu.with_memory_space_constraint(x, pltpu.HBM) for x in (cols, flat, reach, stiffness)),
        scratch=[
            pltpu.SMEM(cols.shape, cols.dtype),
            pltpu.VMEM(flat.shape, BF16),
            pltpu.VMEM(reach.shape, reach.dtype),
            pltpu.VMEM(stiffness.shape, BF16),
            pltpu.SemaphoreType.DMA((3 + blocks // RIM,)),
        ],
        flops=row_flops * (blocks - 2 * RIM),
        name="mask_and_inner",
    )
    inner_r = to_side(inner)
    rim_link = over_link(rim_link)
    rim_chip = over_chip(rim_chip)
    outer = call(
        functools.partial(outer_image, total_blocks),
        shape((2 * rim, wide), BF16),
        [SMEM] + [VMEM] * 4,
        VMEM,
        (cols, stiffness, masked, rim_link, rim_chip),
        scratch=[pltpu.VMEM((rows + 2 * rim, wide), BF16)],
        flops=row_flops * 2 * RIM,
        name="outer_image",
    )
    outer_r = to_side(outer)
    tile_flops = 2 * rows * wide * wide
    left_shapes = (shape((wide, inner_rows), BF16), shape((wide, 2 * rim), BF16))
    base_shape = shape((wide, wide), F32)

    own, own_link, own_chip, left_inner, left_outer = call(
        functools.partial(own_tile, size),
        (*tile_shapes(width, wide, F32), *left_shapes),
        [VMEM] * 3,
        [VMEM] * 5,
        (masked, inner, outer),
        flops=tile_flops,
        name="own_tile",
    )
    own_link, own_chip = over_link(own_link), over_chip(own_chip)
    part, part_link, part_chip, far_outer, far_base, near_base = call(
        functools.partial(partner_tile, size),
        (*tile_shapes(width, wide, BF16), left_shapes[1], base_shape, base_shape),
        [VMEM] * 6,
        [VMEM] * 6,
        (basis_p, reach_p, inner, outer, left_inner, inner_r),
        scratch=[pltpu.VMEM((rows, wide), BF16), pltpu.VMEM((wide, inner_rows), BF16)],
        flops=2 * tile_flops,
        name="partner_tile",
    )
    outer_r, own_link, own_chip, far_base = lax.optimization_barrier((outer_r, own_link, own_chip, far_base))
    near, near_link, near_chip, far, far_link, far_chip = call(
        late_tiles,
        (*tile_shapes(width, wide, F32), *(shape((width, 2 * wide), BF16),) * 3),
        [VMEM] * 8,
        [VMEM] * 6,
        (part, part_link, part_chip, far_base, near_base, far_outer, left_outer, outer_r),
        flops=tile_flops,
        name="late_tiles",
    )
    far_link = to_partner_link(far_link)
    near_link = over_link(near_link)
    far_chip = to(far_chip, lambda i: i ^ 1, partner)
    far = to_partner(far)
    near_chip = over_chip(near_chip)

    def add(steps, terms, name, base=None):
        extra = () if base is None else (base,)
        return call(
            functools.partial(add_tiles, steps),
            shape((5, width, 4 * width), F32),
            [VMEM] * len(terms) + [HBM] * len(extra),
            HBM,
            (*terms, *extra),
            scratch=[pltpu.VMEM((len(steps), 5, width, width), F32), pltpu.SemaphoreType.DMA((len(steps),))],
            flops=5 * len(steps) * width * width,
            aliases={len(terms): 0} if extra else None,
            name=name,
        )

    coarse = add((((0, 0), (0, 0, 0)),), (own_link, own, own_chip), "add_own")
    coarse = add(
        (((3, 3), (1, 1, 1)), ((1, 2), (0, 0, 0)), ((2, 1), (0, 0, 0))),
        (far_link, near_link, far_link, far, far, near, far_chip, near_chip, far_chip),
        "add_rest",
        coarse,
    )
    return coarse.transpose(1, 0, 2)


def gathered(stiffness, block_cols, basis, patch_reach):
    blocks, slots, size, _ = stiffness.shape
    rows, groups, width = basis.shape
    slabs = lax.axis_size("blk")
    slab = lax.axis_index("blk")
    total_blocks = blocks * slabs
    ring = [(i, (i + 1) % slabs) for i in range(slabs)]
    back = [(j, i) for i, j in ring]
    low = lax.dynamic_index_in_dim(patch_reach, (slab - 1) % slabs, 0, False)[:, 1]
    high = lax.dynamic_index_in_dim(patch_reach, (slab + 1) % slabs, 0, False)[:, 0]
    block_row = jnp.arange(rows, dtype=jnp.int32) // size
    lower = block_row[:, None] < low[None, :]
    upper = block_row[:, None] >= blocks - high[None, :]
    support = jnp.stack([lower, jnp.ones_like(lower), upper], 1)
    masked = jnp.where(support, basis, jnp.zeros_like(basis))
    rim = RIM * size
    before = lax.ppermute(masked[rows - rim :, 1:], "blk", ring)
    after = lax.ppermute(masked[:rim, :2], "blk", back)
    none = jnp.zeros((rim, 1, width), masked.dtype)
    extended = jnp.concatenate(
        [jnp.concatenate([before, none], 1), masked, jnp.concatenate([none, after], 1)], 0
    ).reshape(blocks + 2 * RIM, size, groups * width)
    position = (block_cols - slab * blocks + RIM) % total_blocks
    picked = jnp.take(extended, position, axis=0)
    image = jnp.einsum("rsij,rsjc->ric", stiffness, picked, preferred_element_type=F32)
    image = image.astype(BF16).reshape(rows, groups, width)
    image = lax.all_gather(image, "col", axis=2, tiled=True)
    tiles = jnp.einsum("rgl,rhc->glhc", masked, image, preferred_element_type=F32)
    from_prev = lax.ppermute(tiles[2], "blk", ring)
    from_next = lax.ppermute(tiles[0], "blk", back)

    def place(tile, offset):
        return jnp.pad(tile, ((0, 0), (offset, 2 - offset), (0, 0)))

    return place(from_prev, 0) + place(tiles[1], 1) + place(from_next, 2)


def solution(mesh):
    in_specs = (
        P("blk", None, None, None),
        P("blk", None),
        P("blk", None, "col"),
        P(None, "col", None),
    )
    out_specs = P(("blk", "col"), None, None)
    body = shards if mesh.shape["col"] == 4 and mesh.shape["blk"] % 2 == 0 else gathered
    return jax.shard_map(body, mesh=mesh, in_specs=in_specs, out_specs=out_specs, check_vma=False)
```

```python
import functools

import jax
import jax.numpy as jnp
from jax import lax
from jax.experimental import pallas as pl
from jax.experimental.pallas import tpu as pltpu
from jax.sharding import PartitionSpec as P

BF16 = jnp.bfloat16
F32 = jnp.float32
VMEM = pl.BlockSpec(memory_space=pltpu.VMEM)
SMEM = pl.BlockSpec(memory_space=pltpu.SMEM)
HBM = pl.BlockSpec(memory_space=pltpu.HBM)
RIM = 2


def shape(dims, dtype):
    return jax.ShapeDtypeStruct(dims, dtype)


def dot(left, right):
    return jnp.dot(left, right, preferred_element_type=F32)


def call(kernel, out_shape, in_specs, out_specs, args, scratch=(), flops=0, aliases=None, name=None):
    outs = jax.tree.leaves(out_shape)
    moved = sum(x.size * x.dtype.itemsize for x in (*args, *outs))
    return pl.pallas_call(
        kernel,
        out_shape=out_shape,
        in_specs=in_specs,
        out_specs=out_specs,
        scratch_shapes=list(scratch),
        input_output_aliases=aliases or {},
        cost_estimate=pl.CostEstimate(flops=flops, bytes_accessed=moved, transcendentals=0),
        compiler_params=pltpu.CompilerParams(vmem_limit_bytes=24 << 20),
        name=name,
    )(*args)


def block_image(stiffness, source, b, block_size, starts):
    blocks = [source[pl.ds(pl.multiple_of(start * block_size, block_size), block_size), :] for start in starts]
    left = jnp.concatenate([stiffness[b, k] for k in range(len(starts))], axis=1)
    return dot(left, jnp.concatenate(blocks, axis=0)).astype(BF16)


def positions(cols, b, blocks, slots, total_blocks):
    first = lax.axis_index("blk") * blocks
    return [
        jnp.clip(lax.rem(cols[k, b] - first + RIM + total_blocks, total_blocks), 0, blocks + 2 * RIM - 1)
        for k in range(slots)
    ]


def reaches(reach):
    slabs = reach.shape[0]
    slab = lax.axis_index("blk")
    low = reach[pl.ds(lax.rem(slab + slabs - 1, slabs), 1), 1, :]
    high = reach[pl.ds(lax.rem(slab + 1, slabs), 1), 0, :]
    return low, high


def mask_block(basis, b, blocks, size, low, high, masked):
    groups, _, width = basis.shape
    rows = slice(b * size, (b + 1) * size)
    keep = {0: (b < low).astype(F32).astype(BF16), 2: (b >= blocks - high).astype(F32).astype(BF16)}
    for g in range(groups):
        value = basis[g, rows, :]
        masked[rows, g * width : (g + 1) * width] = value * keep[g] if g in keep else value


def mask_and_inner(
    total_blocks, cols_hbm, basis_hbm, reach_hbm, stiffness_hbm, masked, to_link, to_chip, inner, cols, basis, reach, stiffness, sem
):
    blocks, slots, size, _ = stiffness.shape
    width = basis.shape[2]
    inner_blocks = pl.ds(RIM, blocks - 2 * RIM)
    moves = [(reach_hbm, reach), (cols_hbm, cols)]
    moves += [
        (basis_hbm.at[:, pl.ds(b * size, RIM * size)], basis.at[:, pl.ds(b * size, RIM * size)])
        for b in range(0, blocks, RIM)
    ]
    moves.append((stiffness_hbm.at[inner_blocks], stiffness.at[inner_blocks]))
    copies = [pltpu.make_async_copy(source, target, sem.at[n]) for n, (source, target) in enumerate(moves)]
    for copy in copies:
        copy.start()
    copies[0].wait()
    low, high = reaches(reach)
    for b in range(blocks):
        if b % RIM == 0:
            copies[2 + b // RIM].wait()
        mask_block(basis, b, blocks, size, low, high, masked)
    odd = parity()

    @pl.when(odd == 0)
    def _():
        to_link[...] = masked[: RIM * size, : 2 * width]
        to_chip[...] = masked[(blocks - RIM) * size :, width:]

    @pl.when(odd == 1)
    def _():
        to_link[...] = masked[(blocks - RIM) * size :, width:]
        to_chip[...] = masked[: RIM * size, : 2 * width]

    copies[1].wait()
    copies[-1].wait()
    for b in range(RIM, blocks - RIM):
        starts = [jnp.clip(p - RIM, 0, blocks - 1) for p in positions(cols, b, blocks, slots, total_blocks)]
        inner[(b - RIM) * size : (b - RIM + 1) * size, :] = block_image(stiffness, masked, b, size, starts)


def outer_image(total_blocks, cols, stiffness, masked, from_link, from_chip, outer, extended):
    blocks, slots, size, _ = stiffness.shape
    rows, wide = masked.shape
    rim = RIM * size
    width = wide // 3
    odd = parity()

    @pl.when(odd == 0)
    def _():
        extended[:rim, : 2 * width] = from_link[...]
        extended[rim + rows :, width:] = from_chip[...]

    @pl.when(odd == 1)
    def _():
        extended[:rim, : 2 * width] = from_chip[...]
        extended[rim + rows :, width:] = from_link[...]

    extended[:rim, 2 * width :] = jnp.zeros((rim, width), BF16)
    extended[rim : rim + rows, :] = masked[...]
    extended[rim + rows :, :width] = jnp.zeros((rim, width), BF16)
    for n, b in enumerate([*range(RIM), *range(blocks - RIM, blocks)]):
        starts = positions(cols, b, blocks, slots, total_blocks)
        outer[n * size : (n + 1) * size, :] = block_image(stiffness, extended, b, size, starts)


def parity():
    return lax.rem(lax.axis_index("blk"), 2)


def store_tile(tile, own, link, chip):
    width = tile.shape[0] // 3
    odd = parity()
    own[...] = tile[width : 2 * width].astype(own.dtype)
    down, up = tile[:width].astype(BF16), tile[2 * width :].astype(BF16)

    @pl.when(odd == 0)
    def _():
        link[...] = down
        chip[...] = up

    @pl.when(odd == 1)
    def _():
        link[...] = up
        chip[...] = down


def turn(size, masked, left_inner, left_outer):
    rows = masked.shape[0]
    rim = RIM * size
    left_inner[...] = masked[rim : rows - rim, :].T
    left_outer[:, :rim] = masked[:rim, :].T
    left_outer[:, rim:] = masked[rows - rim :, :].T


def own_tile(size, masked, inner, outer, own, link, chip, left_inner, left_outer):
    turn(size, masked, left_inner, left_outer)
    store_tile(dot(left_inner[...], inner[...]) + dot(left_outer[...], outer[...]), own, link, chip)


def partner_tile(
    size, basis, reach, inner, outer, near_left, inner_r, own, link, chip, far_outer, far, near, masked, far_inner
):
    low, high = reaches(reach)
    blocks = basis.shape[1] // size
    for b in range(blocks):
        mask_block(basis, b, blocks, size, low, high, masked)
    turn(size, masked, far_inner, far_outer)
    store_tile(dot(far_inner[...], inner[...]) + dot(far_outer[...], outer[...]), own, link, chip)
    far[...] = dot(far_inner[...], inner_r[...])
    near[...] = dot(near_left[...], inner_r[...])


def late_tiles(
    part,
    part_link,
    part_chip,
    far_base,
    near_base,
    far_outer,
    near_outer,
    outer_r,
    near,
    near_link,
    near_chip,
    far,
    far_link,
    far_chip,
):
    wide = outer_r.shape[1]
    far[:, :wide] = part[...]
    far_link[:, :wide] = part_link[...]
    far_chip[:, :wide] = part_chip[...]
    tile = far_base[...] + dot(far_outer[...], outer_r[...])
    store_tile(tile, far.at[:, wide:], far_link.at[:, wide:], far_chip.at[:, wide:])
    store_tile(near_base[...] + dot(near_outer[...], outer_r[...]), near, near_link, near_chip)


def add_tiles(steps, *refs):
    coarse, total, sem = refs[-3:]
    width = total.shape[2]
    me = lax.axis_index("col")
    even = parity() == 0
    copies = []
    for n, ((even_step, odd_step), terms, chunks) in enumerate(steps):
        own, *others = (refs[k][:, m * 3 * width : (m + 1) * 3 * width].astype(F32) for k, m in zip(terms, chunks))
        if others:
            chip, link = others
            placed = ((0, jnp.where(even, link, chip)), (1, own), (2, jnp.where(even, chip, link)))
        else:
            placed = ((1, own),)
        for d in range(5):
            value = None if others else refs[terms[1]][:, d * width : (d + 1) * width]
            for offset, term in placed:
                if 0 <= d - offset <= 2:
                    part = term[:, (d - offset) * width : (d - offset + 1) * width]
                    value = part if value is None else value + part
            total[n, d] = value
        column = lax.bitwise_xor(me, jnp.where(even, even_step, odd_step))
        start = pl.multiple_of(column * width, width)
        copy = pltpu.make_async_copy(total.at[n], coarse.at[:, :, pl.ds(start, width)], sem.at[n])
        copy.start()
        copies.append(copy)
    for copy in copies:
        copy.wait()


def join_terms(link, chip, joined):
    even = parity() == 0
    width = chip.shape[0]
    prev = jnp.where(even, link[...], chip[...]).astype(F32)
    nxt = jnp.where(even, chip[...], link[...]).astype(F32)
    joined[:, : 2 * width] = prev[:, : 2 * width]
    joined[:, 2 * width : 3 * width] = prev[:, 2 * width :] + nxt[:, :width]
    joined[:, 3 * width :] = nxt[:, width:]


def tile_shapes(width, wide, own):
    return shape((width, wide), own), shape((width, wide), BF16), shape((width, wide), BF16)


def shards(stiffness, block_cols, basis, patch_reach):
    blocks, slots, size, _ = stiffness.shape
    rows, groups, width = basis.shape
    wide = groups * width
    slabs = lax.axis_size("blk")
    total_blocks = blocks * slabs
    pairs = [(i, i ^ 1) for i in range(slabs)]
    cross = [(i, (i - 1 if i % 2 == 0 else i + 1) % slabs) for i in range(slabs)]

    def over_chip(value):
        return lax.ppermute(value, "blk", pairs)

    def over_link(value):
        return lax.ppermute(value, "blk", cross)

    def to(value, slab_of, column_of):
        perm = [(4 * i + q, 4 * (slab_of(i) % slabs) + column_of(i, q)) for i in range(slabs) for q in range(4)]
        return lax.ppermute(value, ("blk", "col"), perm)

    def partner(i, q):
        return q ^ (1 + i % 2)

    def side(i, q):
        return q ^ (2 - i % 2)

    def to_partner(value):
        return to(value, lambda i: i, partner)

    def to_side(value):
        return to(value, lambda i: i, side)

    def to_partner_link(value):
        return to(value, lambda i: i + 1 if i % 2 else i - 1, partner)

    basis_p = to_partner(basis).transpose(1, 0, 2)
    reach_p = to_partner(patch_reach).transpose(0, 2, 1)
    cols = block_cols.T
    flat = basis.transpose(1, 0, 2)
    reach = patch_reach.transpose(0, 2, 1)
    inner_rows = (blocks - 2 * RIM) * size
    rim = RIM * size
    row_flops = 2 * slots * size * size * wide
    masked, rim_link, rim_chip, inner = call(
        functools.partial(mask_and_inner, total_blocks),
        (shape((rows, wide), BF16), shape((rim, 2 * width), BF16), shape((rim, 2 * width), BF16), shape((inner_rows, wide), BF16)),
        [HBM] * 4,
        [VMEM] * 4,
        tuple(pltpu.with_memory_space_constraint(x, pltpu.HBM) for x in (cols, flat, reach, stiffness)),
        scratch=[
            pltpu.SMEM(cols.shape, cols.dtype),
            pltpu.VMEM(flat.shape, BF16),
            pltpu.VMEM(reach.shape, reach.dtype),
            pltpu.VMEM(stiffness.shape, BF16),
            pltpu.SemaphoreType.DMA((3 + blocks // RIM,)),
        ],
        flops=row_flops * (blocks - 2 * RIM),
        name="mask_and_inner",
    )
    inner_r = to_side(inner)
    rim_link = over_link(rim_link)
    rim_chip = over_chip(rim_chip)
    outer = call(
        functools.partial(outer_image, total_blocks),
        shape((2 * rim, wide), BF16),
        [SMEM] + [VMEM] * 4,
        VMEM,
        (cols, stiffness, masked, rim_link, rim_chip),
        scratch=[pltpu.VMEM((rows + 2 * rim, wide), BF16)],
        flops=row_flops * 2 * RIM,
        name="outer_image",
    )
    outer_r = to_side(outer)
    tile_flops = 2 * rows * wide * wide
    left_shapes = (shape((wide, inner_rows), BF16), shape((wide, 2 * rim), BF16))
    base_shape = shape((wide, wide), F32)

    own, own_link, own_chip, left_inner, left_outer = call(
        functools.partial(own_tile, size),
        (*tile_shapes(width, wide, F32), *left_shapes),
        [VMEM] * 3,
        [VMEM] * 5,
        (masked, inner, outer),
        flops=tile_flops,
        name="own_tile",
    )
    own_link, own_chip = over_link(own_link), over_chip(own_chip)
    part, part_link, part_chip, far_outer, far_base, near_base = call(
        functools.partial(partner_tile, size),
        (*tile_shapes(width, wide, BF16), left_shapes[1], base_shape, base_shape),
        [VMEM] * 6,
        [VMEM] * 6,
        (basis_p, reach_p, inner, outer, left_inner, inner_r),
        scratch=[pltpu.VMEM((rows, wide), BF16), pltpu.VMEM((wide, inner_rows), BF16)],
        flops=2 * tile_flops,
        name="partner_tile",
    )
    outer_r, own_link, own_chip, far_base = lax.optimization_barrier((outer_r, own_link, own_chip, far_base))
    near, near_link, near_chip, far, far_link, far_chip = call(
        late_tiles,
        (*tile_shapes(width, wide, F32), *(shape((width, 2 * wide), BF16),) * 3),
        [VMEM] * 8,
        [VMEM] * 6,
        (part, part_link, part_chip, far_base, near_base, far_outer, left_outer, outer_r),
        flops=tile_flops,
        name="late_tiles",
    )
    far_link = to_partner_link(far_link)
    near_link = over_link(near_link)
    far_chip = to(far_chip, lambda i: i ^ 1, partner)
    far = to_partner(far)
    near_chip = over_chip(near_chip)

    def add(steps, terms, name, base=None):
        extra = () if base is None else (base,)
        return call(
            functools.partial(add_tiles, steps),
            shape((5, width, 4 * width), F32),
            [VMEM] * len(terms) + [HBM] * len(extra),
            HBM,
            (*terms, *extra),
            scratch=[pltpu.VMEM((len(steps), 5, width, width), F32), pltpu.SemaphoreType.DMA((len(steps),))],
            flops=5 * len(steps) * width * width,
            aliases={len(terms): 0} if extra else None,
            name=name,
        )

    joined = call(
        join_terms,
        shape((width, 5 * width), F32),
        [VMEM] * 2,
        VMEM,
        (near_link, near_chip),
        flops=int(3e9),
        name="join_terms",
    )
    coarse = add((((0, 0), (2, 0, 1), (0, 0, 0)),), (own_chip, own_link, own), "add_own")
    coarse = add(
        (((3, 3), (0, 1, 2), (1, 1, 1)), ((1, 2), (0, 4), (0,)), ((2, 1), (3, 1, 2), (0, 0, 0))),
        (far, far_chip, far_link, near, joined),
        "add_rest",
        coarse,
    )
    return coarse.transpose(1, 0, 2)


def gathered(stiffness, block_cols, basis, patch_reach):
    blocks, slots, size, _ = stiffness.shape
    rows, groups, width = basis.shape
    slabs = lax.axis_size("blk")
    slab = lax.axis_index("blk")
    total_blocks = blocks * slabs
    ring = [(i, (i + 1) % slabs) for i in range(slabs)]
    back = [(j, i) for i, j in ring]
    low = lax.dynamic_index_in_dim(patch_reach, (slab - 1) % slabs, 0, False)[:, 1]
    high = lax.dynamic_index_in_dim(patch_reach, (slab + 1) % slabs, 0, False)[:, 0]
    block_row = jnp.arange(rows, dtype=jnp.int32) // size
    lower = block_row[:, None] < low[None, :]
    upper = block_row[:, None] >= blocks - high[None, :]
    support = jnp.stack([lower, jnp.ones_like(lower), upper], 1)
    masked = jnp.where(support, basis, jnp.zeros_like(basis))
    rim = RIM * size
    before = lax.ppermute(masked[rows - rim :, 1:], "blk", ring)
    after = lax.ppermute(masked[:rim, :2], "blk", back)
    none = jnp.zeros((rim, 1, width), masked.dtype)
    extended = jnp.concatenate(
        [jnp.concatenate([before, none], 1), masked, jnp.concatenate([none, after], 1)], 0
    ).reshape(blocks + 2 * RIM, size, groups * width)
    position = (block_cols - slab * blocks + RIM) % total_blocks
    picked = jnp.take(extended, position, axis=0)
    image = jnp.einsum("rsij,rsjc->ric", stiffness, picked, preferred_element_type=F32)
    image = image.astype(BF16).reshape(rows, groups, width)
    image = lax.all_gather(image, "col", axis=2, tiled=True)
    tiles = jnp.einsum("rgl,rhc->glhc", masked, image, preferred_element_type=F32)
    from_prev = lax.ppermute(tiles[2], "blk", ring)
    from_next = lax.ppermute(tiles[0], "blk", back)

    def place(tile, offset):
        return jnp.pad(tile, ((0, 0), (offset, 2 - offset), (0, 0)))

    return place(from_prev, 0) + place(tiles[1], 1) + place(from_next, 2)


def solution(mesh):
    in_specs = (
        P("blk", None, None, None),
        P("blk", None),
        P("blk", None, "col"),
        P(None, "col", None),
    )
    out_specs = P(("blk", "col"), None, None)
    body = shards if mesh.shape["col"] == 4 and mesh.shape["blk"] % 2 == 0 else gathered
    return jax.shard_map(body, mesh=mesh, in_specs=in_specs, out_specs=out_specs, check_vma=False)
```

```python
import functools

import jax
import jax.numpy as jnp
from jax import lax
from jax.experimental import pallas as pl
from jax.experimental.pallas import tpu as pltpu
from jax.sharding import PartitionSpec as P

BF16 = jnp.bfloat16
F32 = jnp.float32
VMEM = pl.BlockSpec(memory_space=pltpu.VMEM)
SMEM = pl.BlockSpec(memory_space=pltpu.SMEM)
HBM = pl.BlockSpec(memory_space=pltpu.HBM)
RIM = 2


def shape(dims, dtype):
    return jax.ShapeDtypeStruct(dims, dtype)


def dot(left, right):
    return jnp.dot(left, right, preferred_element_type=F32)


def call(kernel, out_shape, in_specs, out_specs, args, scratch=(), flops=0, aliases=None, name=None):
    outs = jax.tree.leaves(out_shape)
    moved = sum(x.size * x.dtype.itemsize for x in (*args, *outs))
    return pl.pallas_call(
        kernel,
        out_shape=out_shape,
        in_specs=in_specs,
        out_specs=out_specs,
        scratch_shapes=list(scratch),
        input_output_aliases=aliases or {},
        cost_estimate=pl.CostEstimate(flops=flops, bytes_accessed=moved, transcendentals=0),
        compiler_params=pltpu.CompilerParams(vmem_limit_bytes=24 << 20),
        name=name,
    )(*args)


def block_image(stiffness, source, b, block_size, starts):
    blocks = [source[pl.ds(pl.multiple_of(start * block_size, block_size), block_size), :] for start in starts]
    left = jnp.concatenate([stiffness[b, k] for k in range(len(starts))], axis=1)
    return dot(left, jnp.concatenate(blocks, axis=0)).astype(BF16)


def positions(cols, b, blocks, slots, total_blocks):
    first = lax.axis_index("blk") * blocks
    return [
        jnp.clip(lax.rem(cols[k, b] - first + RIM + total_blocks, total_blocks), 0, blocks + 2 * RIM - 1)
        for k in range(slots)
    ]


def reaches(reach):
    slabs = reach.shape[0]
    slab = lax.axis_index("blk")
    low = reach[pl.ds(lax.rem(slab + slabs - 1, slabs), 1), 1, :]
    high = reach[pl.ds(lax.rem(slab + 1, slabs), 1), 0, :]
    return low, high


def mask_block(basis, b, blocks, size, low, high, masked):
    groups, _, width = basis.shape
    rows = slice(b * size, (b + 1) * size)
    keep = {0: (b < low).astype(F32).astype(BF16), 2: (b >= blocks - high).astype(F32).astype(BF16)}
    for g in range(groups):
        value = basis[g, rows, :]
        masked[rows, g * width : (g + 1) * width] = value * keep[g] if g in keep else value


def mask_and_inner(
    total_blocks, cols_hbm, basis_hbm, reach_hbm, stiffness_hbm, masked, to_link, to_chip, inner, cols, basis, reach, stiffness, sem
):
    blocks, slots, size, _ = stiffness.shape
    width = basis.shape[2]
    inner_blocks = pl.ds(RIM, blocks - 2 * RIM)
    moves = [(reach_hbm, reach), (cols_hbm, cols)]
    moves += [
        (basis_hbm.at[:, pl.ds(b * size, RIM * size)], basis.at[:, pl.ds(b * size, RIM * size)])
        for b in range(0, blocks, RIM)
    ]
    moves.append((stiffness_hbm.at[inner_blocks], stiffness.at[inner_blocks]))
    copies = [pltpu.make_async_copy(source, target, sem.at[n]) for n, (source, target) in enumerate(moves)]
    for copy in copies:
        copy.start()
    copies[0].wait()
    low, high = reaches(reach)
    for b in range(blocks):
        if b % RIM == 0:
            copies[2 + b // RIM].wait()
        mask_block(basis, b, blocks, size, low, high, masked)
    odd = parity()

    @pl.when(odd == 0)
    def _():
        to_link[...] = masked[: RIM * size, : 2 * width]
        to_chip[...] = masked[(blocks - RIM) * size :, width:]

    @pl.when(odd == 1)
    def _():
        to_link[...] = masked[(blocks - RIM) * size :, width:]
        to_chip[...] = masked[: RIM * size, : 2 * width]

    copies[1].wait()
    copies[-1].wait()
    for b in range(RIM, blocks - RIM):
        starts = [jnp.clip(p - RIM, 0, blocks - 1) for p in positions(cols, b, blocks, slots, total_blocks)]
        inner[(b - RIM) * size : (b - RIM + 1) * size, :] = block_image(stiffness, masked, b, size, starts)


def outer_image(total_blocks, cols, stiffness, masked, from_link, from_chip, outer, extended):
    blocks, slots, size, _ = stiffness.shape
    rows, wide = masked.shape
    rim = RIM * size
    width = wide // 3
    odd = parity()

    @pl.when(odd == 0)
    def _():
        extended[:rim, : 2 * width] = from_link[...]
        extended[rim + rows :, width:] = from_chip[...]

    @pl.when(odd == 1)
    def _():
        extended[:rim, : 2 * width] = from_chip[...]
        extended[rim + rows :, width:] = from_link[...]

    extended[:rim, 2 * width :] = jnp.zeros((rim, width), BF16)
    extended[rim : rim + rows, :] = masked[...]
    extended[rim + rows :, :width] = jnp.zeros((rim, width), BF16)
    for n, b in enumerate([*range(RIM), *range(blocks - RIM, blocks)]):
        starts = positions(cols, b, blocks, slots, total_blocks)
        outer[n * size : (n + 1) * size, :] = block_image(stiffness, extended, b, size, starts)


def parity():
    return lax.rem(lax.axis_index("blk"), 2)


def store_tile(tile, own, link, chip):
    width = tile.shape[0] // 3
    odd = parity()
    own[...] = tile[width : 2 * width].astype(own.dtype)
    down, up = tile[:width].astype(BF16), tile[2 * width :].astype(BF16)

    @pl.when(odd == 0)
    def _():
        link[...] = down
        chip[...] = up

    @pl.when(odd == 1)
    def _():
        link[...] = up
        chip[...] = down


def turn(size, masked, left_inner, left_outer):
    rows = masked.shape[0]
    rim = RIM * size
    left_inner[...] = masked[rim : rows - rim, :].T
    left_outer[:, :rim] = masked[:rim, :].T
    left_outer[:, rim:] = masked[rows - rim :, :].T


def own_tile(size, masked, inner, outer, own, link, chip, left_inner, left_outer):
    turn(size, masked, left_inner, left_outer)
    store_tile(dot(left_inner[...], inner[...]) + dot(left_outer[...], outer[...]), own, link, chip)


def partner_tile(
    size, basis, reach, inner, outer, near_left, inner_r, own, link, chip, far_outer, far, near, masked, far_inner
):
    low, high = reaches(reach)
    blocks = basis.shape[1] // size
    for b in range(blocks):
        mask_block(basis, b, blocks, size, low, high, masked)
    turn(size, masked, far_inner, far_outer)
    store_tile(dot(far_inner[...], inner[...]) + dot(far_outer[...], outer[...]), own, link, chip)
    far[...] = dot(far_inner[...], inner_r[...])
    near[...] = dot(near_left[...], inner_r[...])


def late_tiles(
    part,
    part_link,
    part_chip,
    far_base,
    near_base,
    far_outer,
    near_outer,
    outer_r,
    near,
    near_link,
    near_chip,
    far,
    far_link,
    far_chip,
):
    wide = outer_r.shape[1]
    far[:, :wide] = part[...]
    far_link[:, :wide] = part_link[...]
    far_chip[:, :wide] = part_chip[...]
    tile = far_base[...] + dot(far_outer[...], outer_r[...])
    store_tile(tile, far.at[:, wide:], far_link.at[:, wide:], far_chip.at[:, wide:])
    store_tile(near_base[...] + dot(near_outer[...], outer_r[...]), near, near_link, near_chip)


def add_tiles(steps, *refs):
    count = len(steps)
    terms = refs[: 3 * count]
    coarse, total, sem = refs[-3:]
    width = total.shape[2]
    me = lax.axis_index("col")
    even = parity() == 0
    copies = []
    for n, ((even_step, odd_step), chunks) in enumerate(steps):
        own, link, chip = (
            ref[:, m * 3 * width : (m + 1) * 3 * width].astype(F32) for ref, m in zip(terms[3 * n : 3 * n + 3], chunks)
        )
        prev = jnp.where(even, link, chip)
        nxt = jnp.where(even, chip, link)
        for d in range(5):
            value = None
            for offset, term in ((0, prev), (1, own), (2, nxt)):
                if 0 <= d - offset <= 2:
                    part = term[:, (d - offset) * width : (d - offset + 1) * width]
                    value = part if value is None else value + part
            total[n, d] = value
        column = lax.bitwise_xor(me, jnp.where(even, even_step, odd_step))
        start = pl.multiple_of(column * width, width)
        copy = pltpu.make_async_copy(total.at[n], coarse.at[:, :, pl.ds(start, width)], sem.at[n])
        copy.start()
        copies.append(copy)
    for copy in copies:
        copy.wait()


def tile_shapes(width, wide, own):
    return shape((width, wide), own), shape((width, wide), BF16), shape((width, wide), BF16)


def shards(stiffness, block_cols, basis, patch_reach):
    blocks, slots, size, _ = stiffness.shape
    rows, groups, width = basis.shape
    wide = groups * width
    slabs = lax.axis_size("blk")
    total_blocks = blocks * slabs
    pairs = [(i, i ^ 1) for i in range(slabs)]
    cross = [(i, (i - 1 if i % 2 == 0 else i + 1) % slabs) for i in range(slabs)]

    def over_chip(value):
        return lax.ppermute(value, "blk", pairs)

    def over_link(value):
        return lax.ppermute(value, "blk", cross)

    def to(value, slab_of, column_of):
        perm = [(4 * i + q, 4 * (slab_of(i) % slabs) + column_of(i, q)) for i in range(slabs) for q in range(4)]
        return lax.ppermute(value, ("blk", "col"), perm)

    def partner(i, q):
        return q ^ (1 + i % 2)

    def side(i, q):
        return q ^ (2 - i % 2)

    def to_partner(value):
        return to(value, lambda i: i, partner)

    def to_side(value):
        return to(value, lambda i: i, side)

    def to_partner_link(value):
        return to(value, lambda i: i + 1 if i % 2 else i - 1, partner)

    basis_p = to_partner(basis).transpose(1, 0, 2)
    reach_p = to_partner(patch_reach).transpose(0, 2, 1)
    cols = block_cols.T
    flat = basis.transpose(1, 0, 2)
    reach = patch_reach.transpose(0, 2, 1)
    inner_rows = (blocks - 2 * RIM) * size
    rim = RIM * size
    row_flops = 2 * slots * size * size * wide
    masked, rim_link, rim_chip, inner = call(
        functools.partial(mask_and_inner, total_blocks),
        (shape((rows, wide), BF16), shape((rim, 2 * width), BF16), shape((rim, 2 * width), BF16), shape((inner_rows, wide), BF16)),
        [HBM] * 4,
        [VMEM] * 4,
        tuple(pltpu.with_memory_space_constraint(x, pltpu.HBM) for x in (cols, flat, reach, stiffness)),
        scratch=[
            pltpu.SMEM(cols.shape, cols.dtype),
            pltpu.VMEM(flat.shape, BF16),
            pltpu.VMEM(reach.shape, reach.dtype),
            pltpu.VMEM(stiffness.shape, BF16),
            pltpu.SemaphoreType.DMA((3 + blocks // RIM,)),
        ],
        flops=row_flops * (blocks - 2 * RIM),
        name="mask_and_inner",
    )
    inner_r = to_side(inner)
    rim_link = over_link(rim_link)
    rim_chip = over_chip(rim_chip)
    outer = call(
        functools.partial(outer_image, total_blocks),
        shape((2 * rim, wide), BF16),
        [SMEM] + [VMEM] * 4,
        VMEM,
        (cols, stiffness, masked, rim_link, rim_chip),
        scratch=[pltpu.VMEM((rows + 2 * rim, wide), BF16)],
        flops=row_flops * 2 * RIM,
        name="outer_image",
    )
    outer_r = to_side(outer)
    tile_flops = 2 * rows * wide * wide
    left_shapes = (shape((wide, inner_rows), BF16), shape((wide, 2 * rim), BF16))
    base_shape = shape((wide, wide), F32)

    own, own_link, own_chip, left_inner, left_outer = call(
        functools.partial(own_tile, size),
        (*tile_shapes(width, wide, F32), *left_shapes),
        [VMEM] * 3,
        [VMEM] * 5,
        (masked, inner, outer),
        flops=tile_flops,
        name="own_tile",
    )
    own_link, own_chip = over_link(own_link), over_chip(own_chip)
    part, part_link, part_chip, far_outer, far_base, near_base = call(
        functools.partial(partner_tile, size),
        (*tile_shapes(width, wide, BF16), left_shapes[1], base_shape, base_shape),
        [VMEM] * 6,
        [VMEM] * 6,
        (basis_p, reach_p, inner, outer, left_inner, inner_r),
        scratch=[pltpu.VMEM((rows, wide), BF16), pltpu.VMEM((wide, inner_rows), BF16)],
        flops=2 * tile_flops,
        name="partner_tile",
    )
    outer_r, own_link, own_chip, far_base = lax.optimization_barrier((outer_r, own_link, own_chip, far_base))
    near, near_link, near_chip, far, far_link, far_chip = call(
        late_tiles,
        (*tile_shapes(width, wide, F32), *(shape((width, 2 * wide), BF16),) * 3),
        [VMEM] * 8,
        [VMEM] * 6,
        (part, part_link, part_chip, far_base, near_base, far_outer, left_outer, outer_r),
        flops=tile_flops,
        name="late_tiles",
    )
    far_link = to_partner_link(far_link)
    near_link = over_link(near_link)
    far_chip = to(far_chip, lambda i: i ^ 1, partner)
    far = to_partner(far)
    near_chip = over_chip(near_chip)

    def add(steps, terms, name, base=None):
        extra = () if base is None else (base,)
        return call(
            functools.partial(add_tiles, steps),
            shape((5, width, 4 * width), F32),
            [VMEM] * len(terms) + [HBM] * len(extra),
            HBM,
            (*terms, *extra),
            scratch=[pltpu.VMEM((len(steps), 5, width, width), F32), pltpu.SemaphoreType.DMA((len(steps),))],
            flops=5 * len(steps) * width * width,
            aliases={len(terms): 0} if extra else None,
            name=name,
        )

    coarse = add((((0, 0), (0, 0, 0)),), (own, own_link, own_chip), "add_own")
    coarse = add(
        (((2, 1), (0, 0, 0)), ((1, 2), (0, 0, 0)), ((3, 3), (1, 1, 1))),
        (near, far_link, far_chip, far, near_link, near_chip, far, far_link, far_chip),
        "add_rest",
        coarse,
    )
    return coarse.transpose(1, 0, 2)


def gathered(stiffness, block_cols, basis, patch_reach):
    blocks, slots, size, _ = stiffness.shape
    rows, groups, width = basis.shape
    slabs = lax.axis_size("blk")
    slab = lax.axis_index("blk")
    total_blocks = blocks * slabs
    ring = [(i, (i + 1) % slabs) for i in range(slabs)]
    back = [(j, i) for i, j in ring]
    low = lax.dynamic_index_in_dim(patch_reach, (slab - 1) % slabs, 0, False)[:, 1]
    high = lax.dynamic_index_in_dim(patch_reach, (slab + 1) % slabs, 0, False)[:, 0]
    block_row = jnp.arange(rows, dtype=jnp.int32) // size
    lower = block_row[:, None] < low[None, :]
    upper = block_row[:, None] >= blocks - high[None, :]
    support = jnp.stack([lower, jnp.ones_like(lower), upper], 1)
    masked = jnp.where(support, basis, jnp.zeros_like(basis))
    rim = RIM * size
    before = lax.ppermute(masked[rows - rim :, 1:], "blk", ring)
    after = lax.ppermute(masked[:rim, :2], "blk", back)
    none = jnp.zeros((rim, 1, width), masked.dtype)
    extended = jnp.concatenate(
        [jnp.concatenate([before, none], 1), masked, jnp.concatenate([none, after], 1)], 0
    ).reshape(blocks + 2 * RIM, size, groups * width)
    position = (block_cols - slab * blocks + RIM) % total_blocks
    picked = jnp.take(extended, position, axis=0)
    image = jnp.einsum("rsij,rsjc->ric", stiffness, picked, preferred_element_type=F32)
    image = image.astype(BF16).reshape(rows, groups, width)
    image = lax.all_gather(image, "col", axis=2, tiled=True)
    tiles = jnp.einsum("rgl,rhc->glhc", masked, image, preferred_element_type=F32)
    from_prev = lax.ppermute(tiles[2], "blk", ring)
    from_next = lax.ppermute(tiles[0], "blk", back)

    def place(tile, offset):
        return jnp.pad(tile, ((0, 0), (offset, 2 - offset), (0, 0)))

    return place(from_prev, 0) + place(tiles[1], 1) + place(from_next, 2)


def solution(mesh):
    in_specs = (
        P("blk", None, None, None),
        P("blk", None),
        P("blk", None, "col"),
        P(None, "col", None),
    )
    out_specs = P(("blk", "col"), None, None)
    body = shards if mesh.shape["col"] == 4 and mesh.shape["blk"] % 2 == 0 else gathered
    return jax.shard_map(body, mesh=mesh, in_specs=in_specs, out_specs=out_specs, check_vma=False)
```

```python
import functools

import jax
import jax.numpy as jnp
from jax import lax
from jax.experimental import pallas as pl
from jax.experimental.pallas import tpu as pltpu
from jax.sharding import PartitionSpec as P

BF16 = jnp.bfloat16
F32 = jnp.float32
VMEM = pl.BlockSpec(memory_space=pltpu.VMEM)
SMEM = pl.BlockSpec(memory_space=pltpu.SMEM)
HBM = pl.BlockSpec(memory_space=pltpu.HBM)
RIM = 2


def shape(dims, dtype):
    return jax.ShapeDtypeStruct(dims, dtype)


def dot(left, right):
    return jnp.dot(left, right, preferred_element_type=F32)


def call(kernel, out_shape, in_specs, out_specs, args, scratch=(), flops=0, aliases=None, name=None):
    outs = jax.tree.leaves(out_shape)
    moved = sum(x.size * x.dtype.itemsize for x in (*args, *outs))
    return pl.pallas_call(
        kernel,
        out_shape=out_shape,
        in_specs=in_specs,
        out_specs=out_specs,
        scratch_shapes=list(scratch),
        input_output_aliases=aliases or {},
        cost_estimate=pl.CostEstimate(flops=flops, bytes_accessed=moved, transcendentals=0),
        compiler_params=pltpu.CompilerParams(vmem_limit_bytes=24 << 20),
        name=name,
    )(*args)


def block_image(stiffness, source, b, block_size, starts):
    blocks = [source[pl.ds(pl.multiple_of(start * block_size, block_size), block_size), :] for start in starts]
    left = jnp.concatenate([stiffness[b, k] for k in range(len(starts))], axis=1)
    return dot(left, jnp.concatenate(blocks, axis=0)).astype(BF16)


def positions(cols, b, blocks, slots, total_blocks):
    first = lax.axis_index("blk") * blocks
    return [
        jnp.clip(lax.rem(cols[k, b] - first + RIM + total_blocks, total_blocks), 0, blocks + 2 * RIM - 1)
        for k in range(slots)
    ]


def reaches(reach):
    slabs = reach.shape[0]
    slab = lax.axis_index("blk")
    low = reach[pl.ds(lax.rem(slab + slabs - 1, slabs), 1), 1, :]
    high = reach[pl.ds(lax.rem(slab + 1, slabs), 1), 0, :]
    return low, high


def mask_block(basis, b, blocks, size, low, high, masked):
    groups, _, width = basis.shape
    rows = slice(b * size, (b + 1) * size)
    keep = {0: (b < low).astype(F32).astype(BF16), 2: (b >= blocks - high).astype(F32).astype(BF16)}
    for g in range(groups):
        value = basis[g, rows, :]
        masked[rows, g * width : (g + 1) * width] = value * keep[g] if g in keep else value


def mask_and_inner(
    total_blocks, cols_hbm, basis_hbm, reach_hbm, stiffness_hbm, masked, to_link, to_chip, inner, cols, basis, reach, stiffness, sem
):
    blocks, slots, size, _ = stiffness.shape
    width = basis.shape[2]
    inner_blocks = pl.ds(RIM, blocks - 2 * RIM)
    moves = [(reach_hbm, reach), (cols_hbm, cols)]
    moves += [
        (basis_hbm.at[:, pl.ds(b * size, RIM * size)], basis.at[:, pl.ds(b * size, RIM * size)])
        for b in range(0, blocks, RIM)
    ]
    moves.append((stiffness_hbm.at[inner_blocks], stiffness.at[inner_blocks]))
    copies = [pltpu.make_async_copy(source, target, sem.at[n]) for n, (source, target) in enumerate(moves)]
    for copy in copies:
        copy.start()
    copies[0].wait()
    low, high = reaches(reach)
    for b in range(blocks):
        if b % RIM == 0:
            copies[2 + b // RIM].wait()
        mask_block(basis, b, blocks, size, low, high, masked)
    odd = parity()

    @pl.when(odd == 0)
    def _():
        to_link[...] = masked[: RIM * size, : 2 * width]
        to_chip[...] = masked[(blocks - RIM) * size :, width:]

    @pl.when(odd == 1)
    def _():
        to_link[...] = masked[(blocks - RIM) * size :, width:]
        to_chip[...] = masked[: RIM * size, : 2 * width]

    copies[1].wait()
    copies[-1].wait()
    for b in range(RIM, blocks - RIM):
        starts = [jnp.clip(p - RIM, 0, blocks - 1) for p in positions(cols, b, blocks, slots, total_blocks)]
        inner[(b - RIM) * size : (b - RIM + 1) * size, :] = block_image(stiffness, masked, b, size, starts)


def outer_image(total_blocks, cols, stiffness, masked, from_link, from_chip, outer, extended):
    blocks, slots, size, _ = stiffness.shape
    rows, wide = masked.shape
    rim = RIM * size
    width = wide // 3
    odd = parity()

    @pl.when(odd == 0)
    def _():
        extended[:rim, : 2 * width] = from_link[...]
        extended[rim + rows :, width:] = from_chip[...]

    @pl.when(odd == 1)
    def _():
        extended[:rim, : 2 * width] = from_chip[...]
        extended[rim + rows :, width:] = from_link[...]

    extended[:rim, 2 * width :] = jnp.zeros((rim, width), BF16)
    extended[rim : rim + rows, :] = masked[...]
    extended[rim + rows :, :width] = jnp.zeros((rim, width), BF16)
    for n, b in enumerate([*range(RIM), *range(blocks - RIM, blocks)]):
        starts = positions(cols, b, blocks, slots, total_blocks)
        outer[n * size : (n + 1) * size, :] = block_image(stiffness, extended, b, size, starts)


def parity():
    return lax.rem(lax.axis_index("blk"), 2)


def store_tile(tile, own, link, chip):
    width = tile.shape[0] // 3
    odd = parity()
    own[...] = tile[width : 2 * width].astype(own.dtype)
    down, up = tile[:width].astype(BF16), tile[2 * width :].astype(BF16)

    @pl.when(odd == 0)
    def _():
        link[...] = down
        chip[...] = up

    @pl.when(odd == 1)
    def _():
        link[...] = up
        chip[...] = down


def turn(size, masked, left_inner, left_outer):
    rows = masked.shape[0]
    rim = RIM * size
    left_inner[...] = masked[rim : rows - rim, :].T
    left_outer[:, :rim] = masked[:rim, :].T
    left_outer[:, rim:] = masked[rows - rim :, :].T


def own_tile(size, masked, inner, outer, own, link, chip, left_inner, left_outer):
    turn(size, masked, left_inner, left_outer)
    store_tile(dot(left_inner[...], inner[...]) + dot(left_outer[...], outer[...]), own, link, chip)


def partner_tile(
    size, basis, reach, inner, outer, near_left, inner_r, own, link, chip, far_outer, far, near, masked, far_inner
):
    low, high = reaches(reach)
    blocks = basis.shape[1] // size
    for b in range(blocks):
        mask_block(basis, b, blocks, size, low, high, masked)
    turn(size, masked, far_inner, far_outer)
    store_tile(dot(far_inner[...], inner[...]) + dot(far_outer[...], outer[...]), own, link, chip)
    far[...] = dot(far_inner[...], inner_r[...])
    near[...] = dot(near_left[...], inner_r[...])


def far_tile(part, part_link, part_chip, base, left_outer, outer_r, far, far_link, far_chip):
    wide = outer_r.shape[1]
    far[:, :wide] = part[...]
    far_link[:, :wide] = part_link[...]
    far_chip[:, :wide] = part_chip[...]
    tile = base[...] + dot(left_outer[...], outer_r[...])
    store_tile(tile, far.at[:, wide:], far_link.at[:, wide:], far_chip.at[:, wide:])


def near_tile(base, left_outer, outer_r, near, near_link, near_chip):
    store_tile(base[...] + dot(left_outer[...], outer_r[...]), near, near_link, near_chip)


def add_tiles(steps, *refs):
    count = len(steps)
    terms = refs[: 3 * count]
    coarse, total, sem = refs[-3:]
    width = total.shape[2]
    me = lax.axis_index("col")
    even = parity() == 0
    copies = []
    for n, ((even_step, odd_step), chunks) in enumerate(steps):
        chip, link, own = (
            terms[n + k * count][:, m * 3 * width : (m + 1) * 3 * width].astype(F32) for k, m in enumerate(chunks)
        )
        prev = jnp.where(even, link, chip)
        nxt = jnp.where(even, chip, link)
        for d in range(5):
            value = None
            for offset, term in ((0, prev), (1, own), (2, nxt)):
                if 0 <= d - offset <= 2:
                    part = term[:, (d - offset) * width : (d - offset + 1) * width]
                    value = part if value is None else value + part
            total[n, d] = value
        column = lax.bitwise_xor(me, jnp.where(even, even_step, odd_step))
        start = pl.multiple_of(column * width, width)
        copy = pltpu.make_async_copy(total.at[n], coarse.at[:, :, pl.ds(start, width)], sem.at[n])
        copy.start()
        copies.append(copy)
    for copy in copies:
        copy.wait()


def tile_shapes(width, wide, own):
    return shape((width, wide), own), shape((width, wide), BF16), shape((width, wide), BF16)


def shards(stiffness, block_cols, basis, patch_reach):
    blocks, slots, size, _ = stiffness.shape
    rows, groups, width = basis.shape
    wide = groups * width
    slabs = lax.axis_size("blk")
    total_blocks = blocks * slabs
    pairs = [(i, i ^ 1) for i in range(slabs)]
    cross = [(i, (i - 1 if i % 2 == 0 else i + 1) % slabs) for i in range(slabs)]

    def over_chip(value):
        return lax.ppermute(value, "blk", pairs)

    def over_link(value):
        return lax.ppermute(value, "blk", cross)

    def to(value, slab_of, column_of):
        perm = [(4 * i + q, 4 * (slab_of(i) % slabs) + column_of(i, q)) for i in range(slabs) for q in range(4)]
        return lax.ppermute(value, ("blk", "col"), perm)

    def partner(i, q):
        return q ^ (1 + i % 2)

    def side(i, q):
        return q ^ (2 - i % 2)

    def to_partner(value):
        return to(value, lambda i: i, partner)

    def to_side(value):
        return to(value, lambda i: i, side)

    def to_partner_link(value):
        return to(value, lambda i: i + 1 if i % 2 else i - 1, partner)

    basis_p = to_partner(basis).transpose(1, 0, 2)
    reach_p = to_partner(patch_reach).transpose(0, 2, 1)
    cols = block_cols.T
    flat = basis.transpose(1, 0, 2)
    reach = patch_reach.transpose(0, 2, 1)
    inner_rows = (blocks - 2 * RIM) * size
    rim = RIM * size
    row_flops = 2 * slots * size * size * wide
    masked, rim_link, rim_chip, inner = call(
        functools.partial(mask_and_inner, total_blocks),
        (shape((rows, wide), BF16), shape((rim, 2 * width), BF16), shape((rim, 2 * width), BF16), shape((inner_rows, wide), BF16)),
        [HBM] * 4,
        [VMEM] * 4,
        tuple(pltpu.with_memory_space_constraint(x, pltpu.HBM) for x in (cols, flat, reach, stiffness)),
        scratch=[
            pltpu.SMEM(cols.shape, cols.dtype),
            pltpu.VMEM(flat.shape, BF16),
            pltpu.VMEM(reach.shape, reach.dtype),
            pltpu.VMEM(stiffness.shape, BF16),
            pltpu.SemaphoreType.DMA((3 + blocks // RIM,)),
        ],
        flops=row_flops * (blocks - 2 * RIM),
        name="mask_and_inner",
    )
    inner_r = to_side(inner)
    rim_link = over_link(rim_link)
    rim_chip = over_chip(rim_chip)
    outer = call(
        functools.partial(outer_image, total_blocks),
        shape((2 * rim, wide), BF16),
        [SMEM] + [VMEM] * 4,
        VMEM,
        (cols, stiffness, masked, rim_link, rim_chip),
        scratch=[pltpu.VMEM((rows + 2 * rim, wide), BF16)],
        flops=row_flops * 2 * RIM,
        name="outer_image",
    )
    outer_r = to_side(outer)
    tile_flops = 2 * rows * wide * wide
    left_shapes = (shape((wide, inner_rows), BF16), shape((wide, 2 * rim), BF16))
    base_shape = shape((wide, wide), F32)

    own, own_link, own_chip, left_inner, left_outer = call(
        functools.partial(own_tile, size),
        (*tile_shapes(width, wide, F32), *left_shapes),
        [VMEM] * 3,
        [VMEM] * 5,
        (masked, inner, outer),
        flops=tile_flops,
        name="own_tile",
    )
    own_link, own_chip = over_link(own_link), over_chip(own_chip)
    part, part_link, part_chip, far_outer, far_base, near_base = call(
        functools.partial(partner_tile, size),
        (*tile_shapes(width, wide, BF16), left_shapes[1], base_shape, base_shape),
        [VMEM] * 6,
        [VMEM] * 6,
        (basis_p, reach_p, inner, outer, left_inner, inner_r),
        scratch=[pltpu.VMEM((rows, wide), BF16), pltpu.VMEM((wide, inner_rows), BF16)],
        flops=2 * tile_flops,
        name="partner_tile",
    )
    outer_r, own_link, own_chip, far_base = lax.optimization_barrier((outer_r, own_link, own_chip, far_base))
    far, far_link, far_chip = call(
        far_tile,
        (shape((width, 2 * wide), BF16),) * 3,
        [VMEM] * 6,
        [VMEM] * 3,
        (part, part_link, part_chip, far_base, far_outer, outer_r),
        flops=tile_flops // 2,
        name="far_tile",
    )
    near, near_link, near_chip = call(
        near_tile,
        tile_shapes(width, wide, F32),
        [VMEM] * 3,
        [VMEM] * 3,
        (near_base, left_outer, outer_r),
        flops=tile_flops // 2,
        name="near_tile",
    )
    far_link = to_partner_link(far_link)
    near_link = over_link(near_link)
    far_chip = to(far_chip, lambda i: i ^ 1, partner)
    far = to_partner(far)
    near_chip = over_chip(near_chip)

    def add(steps, terms, name, base=None):
        extra = () if base is None else (base,)
        return call(
            functools.partial(add_tiles, steps),
            shape((5, width, 4 * width), F32),
            [VMEM] * len(terms) + [HBM] * len(extra),
            HBM,
            (*terms, *extra),
            scratch=[pltpu.VMEM((len(steps), 5, width, width), F32), pltpu.SemaphoreType.DMA((len(steps),))],
            flops=5 * len(steps) * width * width,
            aliases={len(terms): 0} if extra else None,
            name=name,
        )

    coarse = add((((0, 0), (0, 0, 0)),), (own_chip, own_link, own), "add_own")
    coarse = add(
        (((3, 3), (1, 1, 1)), ((1, 2), (0, 0, 0)), ((2, 1), (0, 0, 0))),
        (far_chip, near_chip, far_chip, far_link, near_link, far_link, far, far, near),
        "add_rest",
        coarse,
    )
    return coarse.transpose(1, 0, 2)


def gathered(stiffness, block_cols, basis, patch_reach):
    blocks, slots, size, _ = stiffness.shape
    rows, groups, width = basis.shape
    slabs = lax.axis_size("blk")
    slab = lax.axis_index("blk")
    total_blocks = blocks * slabs
    ring = [(i, (i + 1) % slabs) for i in range(slabs)]
    back = [(j, i) for i, j in ring]
    low = lax.dynamic_index_in_dim(patch_reach, (slab - 1) % slabs, 0, False)[:, 1]
    high = lax.dynamic_index_in_dim(patch_reach, (slab + 1) % slabs, 0, False)[:, 0]
    block_row = jnp.arange(rows, dtype=jnp.int32) // size
    lower = block_row[:, None] < low[None, :]
    upper = block_row[:, None] >= blocks - high[None, :]
    support = jnp.stack([lower, jnp.ones_like(lower), upper], 1)
    masked = jnp.where(support, basis, jnp.zeros_like(basis))
    rim = RIM * size
    before = lax.ppermute(masked[rows - rim :, 1:], "blk", ring)
    after = lax.ppermute(masked[:rim, :2], "blk", back)
    none = jnp.zeros((rim, 1, width), masked.dtype)
    extended = jnp.concatenate(
        [jnp.concatenate([before, none], 1), masked, jnp.concatenate([none, after], 1)], 0
    ).reshape(blocks + 2 * RIM, size, groups * width)
    position = (block_cols - slab * blocks + RIM) % total_blocks
    picked = jnp.take(extended, position, axis=0)
    image = jnp.einsum("rsij,rsjc->ric", stiffness, picked, preferred_element_type=F32)
    image = image.astype(BF16).reshape(rows, groups, width)
    image = lax.all_gather(image, "col", axis=2, tiled=True)
    tiles = jnp.einsum("rgl,rhc->glhc", masked, image, preferred_element_type=F32)
    from_prev = lax.ppermute(tiles[2], "blk", ring)
    from_next = lax.ppermute(tiles[0], "blk", back)

    def place(tile, offset):
        return jnp.pad(tile, ((0, 0), (offset, 2 - offset), (0, 0)))

    return place(from_prev, 0) + place(tiles[1], 1) + place(from_next, 2)


def solution(mesh):
    in_specs = (
        P("blk", None, None, None),
        P("blk", None),
        P("blk", None, "col"),
        P(None, "col", None),
    )
    out_specs = P(("blk", "col"), None, None)
    body = shards if mesh.shape["col"] == 4 and mesh.shape["blk"] % 2 == 0 else gathered
    return jax.shard_map(body, mesh=mesh, in_specs=in_specs, out_specs=out_specs, check_vma=False)
```

```python
import functools

import jax
import jax.numpy as jnp
from jax import lax
from jax.experimental import pallas as pl
from jax.experimental.pallas import tpu as pltpu
from jax.sharding import PartitionSpec as P

BF16 = jnp.bfloat16
F32 = jnp.float32
VMEM = pl.BlockSpec(memory_space=pltpu.VMEM)
SMEM = pl.BlockSpec(memory_space=pltpu.SMEM)
HBM = pl.BlockSpec(memory_space=pltpu.HBM)
RIM = 2


def shape(dims, dtype):
    return jax.ShapeDtypeStruct(dims, dtype)


def dot(left, right):
    return jnp.dot(left, right, preferred_element_type=F32)


def call(kernel, out_shape, in_specs, out_specs, args, scratch=(), flops=0, aliases=None, name=None):
    outs = jax.tree.leaves(out_shape)
    moved = sum(x.size * x.dtype.itemsize for x in (*args, *outs))
    return pl.pallas_call(
        kernel,
        out_shape=out_shape,
        in_specs=in_specs,
        out_specs=out_specs,
        scratch_shapes=list(scratch),
        input_output_aliases=aliases or {},
        cost_estimate=pl.CostEstimate(flops=flops, bytes_accessed=moved, transcendentals=0),
        compiler_params=pltpu.CompilerParams(vmem_limit_bytes=24 << 20),
        name=name,
    )(*args)


def block_image(stiffness, source, b, block_size, starts):
    blocks = [source[pl.ds(pl.multiple_of(start * block_size, block_size), block_size), :] for start in starts]
    left = jnp.concatenate([stiffness[b, k] for k in range(len(starts))], axis=1)
    return dot(left, jnp.concatenate(blocks, axis=0)).astype(BF16)


def positions(cols, b, blocks, slots, total_blocks):
    first = lax.axis_index("blk") * blocks
    return [
        jnp.clip(lax.rem(cols[k, b] - first + RIM + total_blocks, total_blocks), 0, blocks + 2 * RIM - 1)
        for k in range(slots)
    ]


def reaches(reach):
    slabs = reach.shape[0]
    slab = lax.axis_index("blk")
    low = reach[pl.ds(lax.rem(slab + slabs - 1, slabs), 1), 1, :]
    high = reach[pl.ds(lax.rem(slab + 1, slabs), 1), 0, :]
    return low, high


def mask_block(basis, b, blocks, size, low, high, masked):
    groups, _, width = basis.shape
    rows = slice(b * size, (b + 1) * size)
    keep = {0: (b < low).astype(F32).astype(BF16), 2: (b >= blocks - high).astype(F32).astype(BF16)}
    for g in range(groups):
        value = basis[g, rows, :]
        masked[rows, g * width : (g + 1) * width] = value * keep[g] if g in keep else value


def mask_and_inner(
    total_blocks, cols_hbm, basis_hbm, reach_hbm, stiffness_hbm, masked, to_link, to_chip, inner, cols, basis, reach, stiffness, sem
):
    blocks, slots, size, _ = stiffness.shape
    width = basis.shape[2]
    inner_blocks = pl.ds(RIM, blocks - 2 * RIM)
    moves = [(reach_hbm, reach), (cols_hbm, cols)]
    moves += [
        (basis_hbm.at[:, pl.ds(b * size, RIM * size)], basis.at[:, pl.ds(b * size, RIM * size)])
        for b in range(0, blocks, RIM)
    ]
    moves.append((stiffness_hbm.at[inner_blocks], stiffness.at[inner_blocks]))
    copies = [pltpu.make_async_copy(source, target, sem.at[n]) for n, (source, target) in enumerate(moves)]
    for copy in copies:
        copy.start()
    copies[0].wait()
    low, high = reaches(reach)
    for b in range(blocks):
        if b % RIM == 0:
            copies[2 + b // RIM].wait()
        mask_block(basis, b, blocks, size, low, high, masked)
    odd = parity()

    @pl.when(odd == 0)
    def _():
        to_link[...] = masked[: RIM * size, : 2 * width]
        to_chip[...] = masked[(blocks - RIM) * size :, width:]

    @pl.when(odd == 1)
    def _():
        to_link[...] = masked[(blocks - RIM) * size :, width:]
        to_chip[...] = masked[: RIM * size, : 2 * width]

    copies[1].wait()
    copies[-1].wait()
    for b in range(RIM, blocks - RIM):
        starts = [jnp.clip(p - RIM, 0, blocks - 1) for p in positions(cols, b, blocks, slots, total_blocks)]
        inner[(b - RIM) * size : (b - RIM + 1) * size, :] = block_image(stiffness, masked, b, size, starts)


def outer_image(total_blocks, cols, stiffness, masked, from_link, from_chip, outer, extended):
    blocks, slots, size, _ = stiffness.shape
    rows, wide = masked.shape
    rim = RIM * size
    width = wide // 3
    odd = parity()

    @pl.when(odd == 0)
    def _():
        extended[:rim, : 2 * width] = from_link[...]
        extended[rim + rows :, width:] = from_chip[...]

    @pl.when(odd == 1)
    def _():
        extended[:rim, : 2 * width] = from_chip[...]
        extended[rim + rows :, width:] = from_link[...]

    extended[:rim, 2 * width :] = jnp.zeros((rim, width), BF16)
    extended[rim : rim + rows, :] = masked[...]
    extended[rim + rows :, :width] = jnp.zeros((rim, width), BF16)
    for n, b in enumerate([*range(RIM), *range(blocks - RIM, blocks)]):
        starts = positions(cols, b, blocks, slots, total_blocks)
        outer[n * size : (n + 1) * size, :] = block_image(stiffness, extended, b, size, starts)


def parity():
    return lax.rem(lax.axis_index("blk"), 2)


def store_tile(tile, own, link, chip):
    width = tile.shape[0] // 3
    odd = parity()
    own[...] = tile[width : 2 * width].astype(own.dtype)
    down, up = tile[:width].astype(BF16), tile[2 * width :].astype(BF16)

    @pl.when(odd == 0)
    def _():
        link[...] = down
        chip[...] = up

    @pl.when(odd == 1)
    def _():
        link[...] = up
        chip[...] = down


def turn(size, masked, left_inner, left_outer):
    rows = masked.shape[0]
    rim = RIM * size
    left_inner[...] = masked[rim : rows - rim, :].T
    left_outer[:, :rim] = masked[:rim, :].T
    left_outer[:, rim:] = masked[rows - rim :, :].T


def own_tile(size, masked, inner, outer, own, link, chip, left_inner, left_outer):
    turn(size, masked, left_inner, left_outer)
    store_tile(dot(left_inner[...], inner[...]) + dot(left_outer[...], outer[...]), own, link, chip)


def partner_tile(
    size, basis, reach, inner, outer, near_left, inner_r, own, link, chip, far_outer, far, near, masked, far_inner
):
    low, high = reaches(reach)
    blocks = basis.shape[1] // size
    for b in range(blocks):
        mask_block(basis, b, blocks, size, low, high, masked)
    turn(size, masked, far_inner, far_outer)
    store_tile(dot(far_inner[...], inner[...]) + dot(far_outer[...], outer[...]), own, link, chip)
    far[...] = dot(far_inner[...], inner_r[...])
    near[...] = dot(near_left[...], inner_r[...])


def far_tile(part, part_link, part_chip, base, left_outer, outer_r, far, far_link, far_chip):
    wide = outer_r.shape[1]
    far[:, :wide] = part[...]
    far_link[:, :wide] = part_link[...]
    far_chip[:, :wide] = part_chip[...]
    tile = base[...] + dot(left_outer[...], outer_r[...])
    store_tile(tile, far.at[:, wide:], far_link.at[:, wide:], far_chip.at[:, wide:])


def near_tile(own_chip, base, left_outer, outer_r, near, near_link, near_chip):
    wide = outer_r.shape[1]
    near_chip[:, :wide] = own_chip[...]
    store_tile(base[...] + dot(left_outer[...], outer_r[...]), near, near_link, near_chip.at[:, wide:])


def add_tiles(steps, *refs):
    count = len(steps)
    terms = refs[: 3 * count]
    coarse, total, sem = refs[-3:]
    width = total.shape[2]
    me = lax.axis_index("col")
    even = parity() == 0
    copies = []
    for n, ((even_step, odd_step), chunks) in enumerate(steps):
        own, chip, link = (
            terms[n + k * count][:, m * 3 * width : (m + 1) * 3 * width].astype(F32) for k, m in enumerate(chunks)
        )
        prev = jnp.where(even, link, chip)
        nxt = jnp.where(even, chip, link)
        for d in range(5):
            value = None
            for offset, term in ((0, prev), (1, own), (2, nxt)):
                if 0 <= d - offset <= 2:
                    part = term[:, (d - offset) * width : (d - offset + 1) * width]
                    value = part if value is None else value + part
            total[n, d] = value
        column = lax.bitwise_xor(me, jnp.where(even, even_step, odd_step))
        start = pl.multiple_of(column * width, width)
        copy = pltpu.make_async_copy(total.at[n], coarse.at[:, :, pl.ds(start, width)], sem.at[n])
        copy.start()
        copies.append(copy)
    for copy in copies:
        copy.wait()


def tile_shapes(width, wide, own):
    return shape((width, wide), own), shape((width, wide), BF16), shape((width, wide), BF16)


def shards(stiffness, block_cols, basis, patch_reach):
    blocks, slots, size, _ = stiffness.shape
    rows, groups, width = basis.shape
    wide = groups * width
    slabs = lax.axis_size("blk")
    total_blocks = blocks * slabs
    pairs = [(i, i ^ 1) for i in range(slabs)]
    cross = [(i, (i - 1 if i % 2 == 0 else i + 1) % slabs) for i in range(slabs)]

    def over_chip(value):
        return lax.ppermute(value, "blk", pairs)

    def over_link(value):
        return lax.ppermute(value, "blk", cross)

    def to(value, slab_of, column_of):
        perm = [(4 * i + q, 4 * (slab_of(i) % slabs) + column_of(i, q)) for i in range(slabs) for q in range(4)]
        return lax.ppermute(value, ("blk", "col"), perm)

    def partner(i, q):
        return q ^ (1 + i % 2)

    def side(i, q):
        return q ^ (2 - i % 2)

    def to_partner(value):
        return to(value, lambda i: i, partner)

    def to_side(value):
        return to(value, lambda i: i, side)

    def to_partner_link(value):
        return to(value, lambda i: i + 1 if i % 2 else i - 1, partner)

    basis_p = to_partner(basis).transpose(1, 0, 2)
    reach_p = to_partner(patch_reach).transpose(0, 2, 1)
    cols = block_cols.T
    flat = basis.transpose(1, 0, 2)
    reach = patch_reach.transpose(0, 2, 1)
    inner_rows = (blocks - 2 * RIM) * size
    rim = RIM * size
    row_flops = 2 * slots * size * size * wide
    masked, rim_link, rim_chip, inner = call(
        functools.partial(mask_and_inner, total_blocks),
        (shape((rows, wide), BF16), shape((rim, 2 * width), BF16), shape((rim, 2 * width), BF16), shape((inner_rows, wide), BF16)),
        [HBM] * 4,
        [VMEM] * 4,
        tuple(pltpu.with_memory_space_constraint(x, pltpu.HBM) for x in (cols, flat, reach, stiffness)),
        scratch=[
            pltpu.SMEM(cols.shape, cols.dtype),
            pltpu.VMEM(flat.shape, BF16),
            pltpu.VMEM(reach.shape, reach.dtype),
            pltpu.VMEM(stiffness.shape, BF16),
            pltpu.SemaphoreType.DMA((3 + blocks // RIM,)),
        ],
        flops=row_flops * (blocks - 2 * RIM),
        name="mask_and_inner",
    )
    inner_r = to_side(inner)
    rim_link = over_link(rim_link)
    rim_chip = over_chip(rim_chip)
    outer = call(
        functools.partial(outer_image, total_blocks),
        shape((2 * rim, wide), BF16),
        [SMEM] + [VMEM] * 4,
        VMEM,
        (cols, stiffness, masked, rim_link, rim_chip),
        scratch=[pltpu.VMEM((rows + 2 * rim, wide), BF16)],
        flops=row_flops * 2 * RIM,
        name="outer_image",
    )
    outer_r = to_side(outer)
    tile_flops = 2 * rows * wide * wide
    left_shapes = (shape((wide, inner_rows), BF16), shape((wide, 2 * rim), BF16))
    base_shape = shape((wide, wide), F32)

    own, own_link, own_chip, left_inner, left_outer = call(
        functools.partial(own_tile, size),
        (*tile_shapes(width, wide, F32), *left_shapes),
        [VMEM] * 3,
        [VMEM] * 5,
        (masked, inner, outer),
        flops=tile_flops,
        name="own_tile",
    )
    own_link = over_link(own_link)
    part, part_link, part_chip, far_outer, far_base, near_base = call(
        functools.partial(partner_tile, size),
        (*tile_shapes(width, wide, BF16), left_shapes[1], base_shape, base_shape),
        [VMEM] * 6,
        [VMEM] * 6,
        (basis_p, reach_p, inner, outer, left_inner, inner_r),
        scratch=[pltpu.VMEM((rows, wide), BF16), pltpu.VMEM((wide, inner_rows), BF16)],
        flops=2 * tile_flops,
        name="partner_tile",
    )
    outer_r, own_link, far_base = lax.optimization_barrier((outer_r, own_link, far_base))
    far, far_link, far_chip = call(
        far_tile,
        (shape((width, 2 * wide), BF16),) * 3,
        [VMEM] * 6,
        [VMEM] * 3,
        (part, part_link, part_chip, far_base, far_outer, outer_r),
        flops=tile_flops // 2,
        name="far_tile",
    )
    near, near_link, near_chip = call(
        near_tile,
        (shape((width, wide), F32), shape((width, wide), BF16), shape((width, 2 * wide), BF16)),
        [VMEM] * 4,
        [VMEM] * 3,
        (own_chip, near_base, left_outer, outer_r),
        flops=tile_flops // 2,
        name="near_tile",
    )
    far_link = to_partner_link(far_link)
    near_link = over_link(near_link)
    far_chip = to(far_chip, lambda i: i ^ 1, partner)
    far = to_partner(far)
    near_chip = over_chip(near_chip)

    def add(steps, terms, name, base=None):
        extra = () if base is None else (base,)
        return call(
            functools.partial(add_tiles, steps),
            shape((5, width, 4 * width), F32),
            [VMEM] * len(terms) + [HBM] * len(extra),
            HBM,
            (*terms, *extra),
            scratch=[pltpu.VMEM((len(steps), 5, width, width), F32), pltpu.SemaphoreType.DMA((len(steps),))],
            flops=5 * len(steps) * width * width,
            aliases={len(terms): 0} if extra else None,
            name=name,
        )

    coarse = add((((0, 0), (0, 0, 0)),), (own, near_chip, own_link), "add_own")
    coarse = add(
        (((3, 3), (1, 1, 1)), ((1, 2), (0, 1, 0)), ((2, 1), (0, 0, 0))),
        (far, far, near, far_chip, near_chip, far_chip, far_link, near_link, far_link),
        "add_rest",
        coarse,
    )
    return coarse.transpose(1, 0, 2)


def gathered(stiffness, block_cols, basis, patch_reach):
    blocks, slots, size, _ = stiffness.shape
    rows, groups, width = basis.shape
    slabs = lax.axis_size("blk")
    slab = lax.axis_index("blk")
    total_blocks = blocks * slabs
    ring = [(i, (i + 1) % slabs) for i in range(slabs)]
    back = [(j, i) for i, j in ring]
    low = lax.dynamic_index_in_dim(patch_reach, (slab - 1) % slabs, 0, False)[:, 1]
    high = lax.dynamic_index_in_dim(patch_reach, (slab + 1) % slabs, 0, False)[:, 0]
    block_row = jnp.arange(rows, dtype=jnp.int32) // size
    lower = block_row[:, None] < low[None, :]
    upper = block_row[:, None] >= blocks - high[None, :]
    support = jnp.stack([lower, jnp.ones_like(lower), upper], 1)
    masked = jnp.where(support, basis, jnp.zeros_like(basis))
    rim = RIM * size
    before = lax.ppermute(masked[rows - rim :, 1:], "blk", ring)
    after = lax.ppermute(masked[:rim, :2], "blk", back)
    none = jnp.zeros((rim, 1, width), masked.dtype)
    extended = jnp.concatenate(
        [jnp.concatenate([before, none], 1), masked, jnp.concatenate([none, after], 1)], 0
    ).reshape(blocks + 2 * RIM, size, groups * width)
    position = (block_cols - slab * blocks + RIM) % total_blocks
    picked = jnp.take(extended, position, axis=0)
    image = jnp.einsum("rsij,rsjc->ric", stiffness, picked, preferred_element_type=F32)
    image = image.astype(BF16).reshape(rows, groups, width)
    image = lax.all_gather(image, "col", axis=2, tiled=True)
    tiles = jnp.einsum("rgl,rhc->glhc", masked, image, preferred_element_type=F32)
    from_prev = lax.ppermute(tiles[2], "blk", ring)
    from_next = lax.ppermute(tiles[0], "blk", back)

    def place(tile, offset):
        return jnp.pad(tile, ((0, 0), (offset, 2 - offset), (0, 0)))

    return place(from_prev, 0) + place(tiles[1], 1) + place(from_next, 2)


def solution(mesh):
    in_specs = (
        P("blk", None, None, None),
        P("blk", None),
        P("blk", None, "col"),
        P(None, "col", None),
    )
    out_specs = P(("blk", "col"), None, None)
    body = shards if mesh.shape["col"] == 4 and mesh.shape["blk"] % 2 == 0 else gathered
    return jax.shard_map(body, mesh=mesh, in_specs=in_specs, out_specs=out_specs, check_vma=False)
```

```python
import functools

import jax
import jax.numpy as jnp
from jax import lax
from jax.experimental import pallas as pl
from jax.experimental.pallas import tpu as pltpu
from jax.sharding import PartitionSpec as P

BF16 = jnp.bfloat16
F32 = jnp.float32
VMEM = pl.BlockSpec(memory_space=pltpu.VMEM)
SMEM = pl.BlockSpec(memory_space=pltpu.SMEM)
HBM = pl.BlockSpec(memory_space=pltpu.HBM)
RIM = 2


def shape(dims, dtype):
    return jax.ShapeDtypeStruct(dims, dtype)


def dot(left, right):
    return jnp.dot(left, right, preferred_element_type=F32)


def call(kernel, out_shape, in_specs, out_specs, args, scratch=(), flops=0, aliases=None, name=None):
    outs = jax.tree.leaves(out_shape)
    moved = sum(x.size * x.dtype.itemsize for x in (*args, *outs))
    return pl.pallas_call(
        kernel,
        out_shape=out_shape,
        in_specs=in_specs,
        out_specs=out_specs,
        scratch_shapes=list(scratch),
        input_output_aliases=aliases or {},
        cost_estimate=pl.CostEstimate(flops=flops, bytes_accessed=moved, transcendentals=0),
        compiler_params=pltpu.CompilerParams(vmem_limit_bytes=24 << 20),
        name=name,
    )(*args)


def block_image(stiffness, source, b, block_size, starts):
    blocks = [source[pl.ds(pl.multiple_of(start * block_size, block_size), block_size), :] for start in starts]
    left = jnp.concatenate([stiffness[b, k] for k in range(len(starts))], axis=1)
    return dot(left, jnp.concatenate(blocks, axis=0)).astype(BF16)


def positions(cols, b, blocks, slots, total_blocks):
    first = lax.axis_index("blk") * blocks
    return [
        jnp.clip(lax.rem(cols[k, b] - first + RIM + total_blocks, total_blocks), 0, blocks + 2 * RIM - 1)
        for k in range(slots)
    ]


def reaches(reach):
    slabs = reach.shape[0]
    slab = lax.axis_index("blk")
    low = reach[pl.ds(lax.rem(slab + slabs - 1, slabs), 1), 1, :]
    high = reach[pl.ds(lax.rem(slab + 1, slabs), 1), 0, :]
    return low, high


def mask_block(basis, b, blocks, size, low, high, masked):
    groups, _, width = basis.shape
    rows = slice(b * size, (b + 1) * size)
    keep = {0: (b < low).astype(F32).astype(BF16), 2: (b >= blocks - high).astype(F32).astype(BF16)}
    for g in range(groups):
        value = basis[g, rows, :]
        masked[rows, g * width : (g + 1) * width] = value * keep[g] if g in keep else value


def mask_and_inner(
    total_blocks, cols_hbm, basis_hbm, reach_hbm, stiffness_hbm, masked, to_link, to_chip, inner, cols, basis, reach, stiffness, sem
):
    blocks, slots, size, _ = stiffness.shape
    width = basis.shape[2]
    inner_blocks = pl.ds(RIM, blocks - 2 * RIM)
    moves = [(reach_hbm, reach), (cols_hbm, cols)]
    moves += [
        (basis_hbm.at[:, pl.ds(b * size, RIM * size)], basis.at[:, pl.ds(b * size, RIM * size)])
        for b in range(0, blocks, RIM)
    ]
    moves.append((stiffness_hbm.at[inner_blocks], stiffness.at[inner_blocks]))
    copies = [pltpu.make_async_copy(source, target, sem.at[n]) for n, (source, target) in enumerate(moves)]
    for copy in copies:
        copy.start()
    copies[0].wait()
    low, high = reaches(reach)
    for b in range(blocks):
        if b % RIM == 0:
            copies[2 + b // RIM].wait()
        mask_block(basis, b, blocks, size, low, high, masked)
    odd = parity()

    @pl.when(odd == 0)
    def _():
        to_link[...] = masked[: RIM * size, : 2 * width]
        to_chip[...] = masked[(blocks - RIM) * size :, width:]

    @pl.when(odd == 1)
    def _():
        to_link[...] = masked[(blocks - RIM) * size :, width:]
        to_chip[...] = masked[: RIM * size, : 2 * width]

    copies[1].wait()
    copies[-1].wait()
    for b in range(RIM, blocks - RIM):
        starts = [jnp.clip(p - RIM, 0, blocks - 1) for p in positions(cols, b, blocks, slots, total_blocks)]
        inner[(b - RIM) * size : (b - RIM + 1) * size, :] = block_image(stiffness, masked, b, size, starts)


def outer_image(total_blocks, cols, stiffness, masked, from_link, from_chip, outer, extended):
    blocks, slots, size, _ = stiffness.shape
    rows, wide = masked.shape
    rim = RIM * size
    width = wide // 3
    odd = parity()

    @pl.when(odd == 0)
    def _():
        extended[:rim, : 2 * width] = from_link[...]
        extended[rim + rows :, width:] = from_chip[...]

    @pl.when(odd == 1)
    def _():
        extended[:rim, : 2 * width] = from_chip[...]
        extended[rim + rows :, width:] = from_link[...]

    extended[:rim, 2 * width :] = jnp.zeros((rim, width), BF16)
    extended[rim : rim + rows, :] = masked[...]
    extended[rim + rows :, :width] = jnp.zeros((rim, width), BF16)
    for n, b in enumerate([*range(RIM), *range(blocks - RIM, blocks)]):
        starts = positions(cols, b, blocks, slots, total_blocks)
        outer[n * size : (n + 1) * size, :] = block_image(stiffness, extended, b, size, starts)


def parity():
    return lax.rem(lax.axis_index("blk"), 2)


def store_tile(tile, own, link, chip):
    width = tile.shape[0] // 3
    odd = parity()
    own[...] = tile[width : 2 * width].astype(own.dtype)
    down, up = tile[:width].astype(BF16), tile[2 * width :].astype(BF16)

    @pl.when(odd == 0)
    def _():
        link[...] = down
        chip[...] = up

    @pl.when(odd == 1)
    def _():
        link[...] = up
        chip[...] = down


def turn(size, masked, left_inner, left_outer):
    rows = masked.shape[0]
    rim = RIM * size
    left_inner[...] = masked[rim : rows - rim, :].T
    left_outer[:, :rim] = masked[:rim, :].T
    left_outer[:, rim:] = masked[rows - rim :, :].T


def own_tile(size, masked, inner, outer, own, link, chip, left_inner, left_outer):
    turn(size, masked, left_inner, left_outer)
    store_tile(dot(left_inner[...], inner[...]) + dot(left_outer[...], outer[...]), own, link, chip)


def partner_tile(
    size, basis, reach, inner, outer, near_left, inner_r, own, link, chip, far_outer, far, near, masked, far_inner
):
    low, high = reaches(reach)
    blocks = basis.shape[1] // size
    for b in range(blocks):
        mask_block(basis, b, blocks, size, low, high, masked)
    turn(size, masked, far_inner, far_outer)
    store_tile(dot(far_inner[...], inner[...]) + dot(far_outer[...], outer[...]), own, link, chip)
    far[...] = dot(far_inner[...], inner_r[...])
    near[...] = dot(near_left[...], inner_r[...])


def far_tile(part, part_link, part_chip, base, left_outer, outer_r, far, far_link, far_chip):
    wide = outer_r.shape[1]
    far[:, :wide] = part[...]
    far_link[:, :wide] = part_link[...]
    far_chip[:, :wide] = part_chip[...]
    tile = base[...] + dot(left_outer[...], outer_r[...])
    store_tile(tile, far.at[:, wide:], far_link.at[:, wide:], far_chip.at[:, wide:])


def near_tile(base, left_outer, outer_r, near, near_link, near_chip):
    store_tile(base[...] + dot(left_outer[...], outer_r[...]), near, near_link, near_chip)


def add_tiles(steps, *refs):
    count = len(steps)
    terms = refs[: 3 * count]
    coarse, total, sem = refs[-3:]
    width = total.shape[2]
    me = lax.axis_index("col")
    even = parity() == 0
    copies = []
    for n, ((even_step, odd_step), chunks) in enumerate(steps):
        chip, link, own = (
            terms[n + k * count][:, m * 3 * width : (m + 1) * 3 * width].astype(F32) for k, m in enumerate(chunks)
        )
        prev = jnp.where(even, link, chip)
        nxt = jnp.where(even, chip, link)
        for d in range(5):
            value = None
            for offset, term in ((0, prev), (1, own), (2, nxt)):
                if 0 <= d - offset <= 2:
                    part = term[:, (d - offset) * width : (d - offset + 1) * width]
                    value = part if value is None else value + part
            total[n, d] = value
        column = lax.bitwise_xor(me, jnp.where(even, even_step, odd_step))
        start = pl.multiple_of(column * width, width)
        copy = pltpu.make_async_copy(total.at[n], coarse.at[:, :, pl.ds(start, width)], sem.at[n])
        copy.start()
        copies.append(copy)
    for copy in copies:
        copy.wait()


def tile_shapes(width, wide, own):
    return shape((width, wide), own), shape((width, wide), BF16), shape((width, wide), BF16)


def shards(stiffness, block_cols, basis, patch_reach):
    blocks, slots, size, _ = stiffness.shape
    rows, groups, width = basis.shape
    wide = groups * width
    slabs = lax.axis_size("blk")
    total_blocks = blocks * slabs
    pairs = [(i, i ^ 1) for i in range(slabs)]
    cross = [(i, (i - 1 if i % 2 == 0 else i + 1) % slabs) for i in range(slabs)]

    def over_chip(value):
        return lax.ppermute(value, "blk", pairs)

    def over_link(value):
        return lax.ppermute(value, "blk", cross)

    def to(value, slab_of, column_of):
        perm = [(4 * i + q, 4 * (slab_of(i) % slabs) + column_of(i, q)) for i in range(slabs) for q in range(4)]
        return lax.ppermute(value, ("blk", "col"), perm)

    def partner(i, q):
        return q ^ (1 + i % 2)

    def side(i, q):
        return q ^ (2 - i % 2)

    def to_partner(value):
        return to(value, lambda i: i, partner)

    def to_side(value):
        return to(value, lambda i: i, side)

    def to_partner_link(value):
        return to(value, lambda i: i + 1 if i % 2 else i - 1, partner)

    basis_p = to_partner(basis).transpose(1, 0, 2)
    reach_p = to_partner(patch_reach).transpose(0, 2, 1)
    cols = block_cols.T
    flat = basis.transpose(1, 0, 2)
    reach = patch_reach.transpose(0, 2, 1)
    inner_rows = (blocks - 2 * RIM) * size
    rim = RIM * size
    row_flops = 2 * slots * size * size * wide
    masked, rim_link, rim_chip, inner = call(
        functools.partial(mask_and_inner, total_blocks),
        (shape((rows, wide), BF16), shape((rim, 2 * width), BF16), shape((rim, 2 * width), BF16), shape((inner_rows, wide), BF16)),
        [HBM] * 4,
        [VMEM] * 4,
        tuple(pltpu.with_memory_space_constraint(x, pltpu.HBM) for x in (cols, flat, reach, stiffness)),
        scratch=[
            pltpu.SMEM(cols.shape, cols.dtype),
            pltpu.VMEM(flat.shape, BF16),
            pltpu.VMEM(reach.shape, reach.dtype),
            pltpu.VMEM(stiffness.shape, BF16),
            pltpu.SemaphoreType.DMA((3 + blocks // RIM,)),
        ],
        flops=row_flops * (blocks - 2 * RIM),
        name="mask_and_inner",
    )
    inner_r = to_side(inner)
    rim_link = over_link(rim_link)
    rim_chip = over_chip(rim_chip)
    outer = call(
        functools.partial(outer_image, total_blocks),
        shape((2 * rim, wide), BF16),
        [SMEM] + [VMEM] * 4,
        VMEM,
        (cols, stiffness, masked, rim_link, rim_chip),
        scratch=[pltpu.VMEM((rows + 2 * rim, wide), BF16)],
        flops=row_flops * 2 * RIM,
        name="outer_image",
    )
    outer_r = to_side(outer)
    tile_flops = 2 * rows * wide * wide
    left_shapes = (shape((wide, inner_rows), BF16), shape((wide, 2 * rim), BF16))
    base_shape = shape((wide, wide), F32)

    own, own_link, own_chip, left_inner, left_outer = call(
        functools.partial(own_tile, size),
        (*tile_shapes(width, wide, F32), *left_shapes),
        [VMEM] * 3,
        [VMEM] * 5,
        (masked, inner, outer),
        flops=tile_flops,
        name="own_tile",
    )
    own_link, own_chip = over_link(own_link), over_chip(own_chip)
    inner_r, own_chip = lax.optimization_barrier((inner_r, own_chip))
    part, part_link, part_chip, far_outer, far_base, near_base = call(
        functools.partial(partner_tile, size),
        (*tile_shapes(width, wide, BF16), left_shapes[1], base_shape, base_shape),
        [VMEM] * 6,
        [VMEM] * 6,
        (basis_p, reach_p, inner, outer, left_inner, inner_r),
        scratch=[pltpu.VMEM((rows, wide), BF16), pltpu.VMEM((wide, inner_rows), BF16)],
        flops=2 * tile_flops,
        name="partner_tile",
    )
    outer_r, own_link, own_chip, far_base = lax.optimization_barrier((outer_r, own_link, own_chip, far_base))
    far, far_link, far_chip = call(
        far_tile,
        (shape((width, 2 * wide), BF16),) * 3,
        [VMEM] * 6,
        [VMEM] * 3,
        (part, part_link, part_chip, far_base, far_outer, outer_r),
        flops=tile_flops // 2,
        name="far_tile",
    )
    near, near_link, near_chip = call(
        near_tile,
        tile_shapes(width, wide, F32),
        [VMEM] * 3,
        [VMEM] * 3,
        (near_base, left_outer, outer_r),
        flops=tile_flops // 2,
        name="near_tile",
    )
    far_link = to_partner_link(far_link)
    near_link = over_link(near_link)
    far_chip = to(far_chip, lambda i: i ^ 1, partner)
    far = to_partner(far)
    near_chip = over_chip(near_chip)

    def add(steps, terms, name, base=None):
        extra = () if base is None else (base,)
        return call(
            functools.partial(add_tiles, steps),
            shape((5, width, 4 * width), F32),
            [VMEM] * len(terms) + [HBM] * len(extra),
            HBM,
            (*terms, *extra),
            scratch=[pltpu.VMEM((len(steps), 5, width, width), F32), pltpu.SemaphoreType.DMA((len(steps),))],
            flops=5 * len(steps) * width * width,
            aliases={len(terms): 0} if extra else None,
            name=name,
        )

    coarse = add((((0, 0), (0, 0, 0)),), (own_chip, own_link, own), "add_own")
    coarse = add(
        (((3, 3), (1, 1, 1)), ((1, 2), (0, 0, 0)), ((2, 1), (0, 0, 0))),
        (far_chip, near_chip, far_chip, far_link, near_link, far_link, far, far, near),
        "add_rest",
        coarse,
    )
    return coarse.transpose(1, 0, 2)


def gathered(stiffness, block_cols, basis, patch_reach):
    blocks, slots, size, _ = stiffness.shape
    rows, groups, width = basis.shape
    slabs = lax.axis_size("blk")
    slab = lax.axis_index("blk")
    total_blocks = blocks * slabs
    ring = [(i, (i + 1) % slabs) for i in range(slabs)]
    back = [(j, i) for i, j in ring]
    low = lax.dynamic_index_in_dim(patch_reach, (slab - 1) % slabs, 0, False)[:, 1]
    high = lax.dynamic_index_in_dim(patch_reach, (slab + 1) % slabs, 0, False)[:, 0]
    block_row = jnp.arange(rows, dtype=jnp.int32) // size
    lower = block_row[:, None] < low[None, :]
    upper = block_row[:, None] >= blocks - high[None, :]
    support = jnp.stack([lower, jnp.ones_like(lower), upper], 1)
    masked = jnp.where(support, basis, jnp.zeros_like(basis))
    rim = RIM * size
    before = lax.ppermute(masked[rows - rim :, 1:], "blk", ring)
    after = lax.ppermute(masked[:rim, :2], "blk", back)
    none = jnp.zeros((rim, 1, width), masked.dtype)
    extended = jnp.concatenate(
        [jnp.concatenate([before, none], 1), masked, jnp.concatenate([none, after], 1)], 0
    ).reshape(blocks + 2 * RIM, size, groups * width)
    position = (block_cols - slab * blocks + RIM) % total_blocks
    picked = jnp.take(extended, position, axis=0)
    image = jnp.einsum("rsij,rsjc->ric", stiffness, picked, preferred_element_type=F32)
    image = image.astype(BF16).reshape(rows, groups, width)
    image = lax.all_gather(image, "col", axis=2, tiled=True)
    tiles = jnp.einsum("rgl,rhc->glhc", masked, image, preferred_element_type=F32)
    from_prev = lax.ppermute(tiles[2], "blk", ring)
    from_next = lax.ppermute(tiles[0], "blk", back)

    def place(tile, offset):
        return jnp.pad(tile, ((0, 0), (offset, 2 - offset), (0, 0)))

    return place(from_prev, 0) + place(tiles[1], 1) + place(from_next, 2)


def solution(mesh):
    in_specs = (
        P("blk", None, None, None),
        P("blk", None),
        P("blk", None, "col"),
        P(None, "col", None),
    )
    out_specs = P(("blk", "col"), None, None)
    body = shards if mesh.shape["col"] == 4 and mesh.shape["blk"] % 2 == 0 else gathered
    return jax.shard_map(body, mesh=mesh, in_specs=in_specs, out_specs=out_specs, check_vma=False)
```

```python
import functools

import jax
import jax.numpy as jnp
from jax import lax
from jax.experimental import pallas as pl
from jax.experimental.pallas import tpu as pltpu
from jax.sharding import PartitionSpec as P

BF16 = jnp.bfloat16
F32 = jnp.float32
VMEM = pl.BlockSpec(memory_space=pltpu.VMEM)
SMEM = pl.BlockSpec(memory_space=pltpu.SMEM)
HBM = pl.BlockSpec(memory_space=pltpu.HBM)
RIM = 2


def shape(dims, dtype):
    return jax.ShapeDtypeStruct(dims, dtype)


def dot(left, right):
    return jnp.dot(left, right, preferred_element_type=F32)


def call(kernel, out_shape, in_specs, out_specs, args, scratch=(), flops=0, aliases=None, name=None):
    outs = jax.tree.leaves(out_shape)
    moved = sum(x.size * x.dtype.itemsize for x in (*args, *outs))
    return pl.pallas_call(
        kernel,
        out_shape=out_shape,
        in_specs=in_specs,
        out_specs=out_specs,
        scratch_shapes=list(scratch),
        input_output_aliases=aliases or {},
        cost_estimate=pl.CostEstimate(flops=flops, bytes_accessed=moved, transcendentals=0),
        compiler_params=pltpu.CompilerParams(vmem_limit_bytes=24 << 20),
        name=name,
    )(*args)


def block_image(stiffness, source, b, block_size, starts):
    blocks = [source[pl.ds(pl.multiple_of(start * block_size, block_size), block_size), :] for start in starts]
    left = jnp.concatenate([stiffness[b, k] for k in range(len(starts))], axis=1)
    return dot(left, jnp.concatenate(blocks, axis=0)).astype(BF16)


def positions(cols, b, blocks, slots, total_blocks):
    first = lax.axis_index("blk") * blocks
    return [
        jnp.clip(lax.rem(cols[k, b] - first + RIM + total_blocks, total_blocks), 0, blocks + 2 * RIM - 1)
        for k in range(slots)
    ]


def reaches(reach):
    slabs = reach.shape[0]
    slab = lax.axis_index("blk")
    low = reach[pl.ds(lax.rem(slab + slabs - 1, slabs), 1), 1, :]
    high = reach[pl.ds(lax.rem(slab + 1, slabs), 1), 0, :]
    return low, high


def mask_block(basis, b, blocks, size, low, high, masked):
    groups, _, width = basis.shape
    rows = slice(b * size, (b + 1) * size)
    keep = {0: (b < low).astype(F32).astype(BF16), 2: (b >= blocks - high).astype(F32).astype(BF16)}
    for g in range(groups):
        value = basis[g, rows, :]
        masked[rows, g * width : (g + 1) * width] = value * keep[g] if g in keep else value


def mask_and_inner(
    total_blocks, cols_hbm, basis_hbm, reach_hbm, stiffness_hbm, masked, to_link, to_chip, inner, cols, basis, reach, stiffness, sem
):
    blocks, slots, size, _ = stiffness.shape
    width = basis.shape[2]
    inner_blocks = pl.ds(RIM, blocks - 2 * RIM)
    moves = [(reach_hbm, reach), (cols_hbm, cols)]
    moves += [
        (basis_hbm.at[:, pl.ds(b * size, RIM * size)], basis.at[:, pl.ds(b * size, RIM * size)])
        for b in range(0, blocks, RIM)
    ]
    moves.append((stiffness_hbm.at[inner_blocks], stiffness.at[inner_blocks]))
    copies = [pltpu.make_async_copy(source, target, sem.at[n]) for n, (source, target) in enumerate(moves)]
    for copy in copies:
        copy.start()
    copies[0].wait()
    low, high = reaches(reach)
    for b in range(blocks):
        if b % RIM == 0:
            copies[2 + b // RIM].wait()
        mask_block(basis, b, blocks, size, low, high, masked)
    odd = parity()

    @pl.when(odd == 0)
    def _():
        to_link[...] = masked[: RIM * size, : 2 * width]
        to_chip[...] = masked[(blocks - RIM) * size :, width:]

    @pl.when(odd == 1)
    def _():
        to_link[...] = masked[(blocks - RIM) * size :, width:]
        to_chip[...] = masked[: RIM * size, : 2 * width]

    copies[1].wait()
    copies[-1].wait()
    for b in range(RIM, blocks - RIM):
        starts = [jnp.clip(p - RIM, 0, blocks - 1) for p in positions(cols, b, blocks, slots, total_blocks)]
        inner[(b - RIM) * size : (b - RIM + 1) * size, :] = block_image(stiffness, masked, b, size, starts)


def outer_image(total_blocks, cols, stiffness, masked, from_link, from_chip, outer, extended):
    blocks, slots, size, _ = stiffness.shape
    rows, wide = masked.shape
    rim = RIM * size
    width = wide // 3
    odd = parity()

    @pl.when(odd == 0)
    def _():
        extended[:rim, : 2 * width] = from_link[...]
        extended[rim + rows :, width:] = from_chip[...]

    @pl.when(odd == 1)
    def _():
        extended[:rim, : 2 * width] = from_chip[...]
        extended[rim + rows :, width:] = from_link[...]

    extended[:rim, 2 * width :] = jnp.zeros((rim, width), BF16)
    extended[rim : rim + rows, :] = masked[...]
    extended[rim + rows :, :width] = jnp.zeros((rim, width), BF16)
    for n, b in enumerate([*range(RIM), *range(blocks - RIM, blocks)]):
        starts = positions(cols, b, blocks, slots, total_blocks)
        outer[n * size : (n + 1) * size, :] = block_image(stiffness, extended, b, size, starts)


def parity():
    return lax.rem(lax.axis_index("blk"), 2)


def store_tile(tile, own, link, chip):
    width = tile.shape[0] // 3
    odd = parity()
    own[...] = tile[width : 2 * width].astype(own.dtype)
    down, up = tile[:width].astype(BF16), tile[2 * width :].astype(BF16)

    @pl.when(odd == 0)
    def _():
        link[...] = down
        chip[...] = up

    @pl.when(odd == 1)
    def _():
        link[...] = up
        chip[...] = down


def turn(size, masked, left_inner, left_outer):
    rows = masked.shape[0]
    rim = RIM * size
    left_inner[...] = masked[rim : rows - rim, :].T
    left_outer[:, :rim] = masked[:rim, :].T
    left_outer[:, rim:] = masked[rows - rim :, :].T


def own_tile(size, masked, inner, outer, own, link, chip, left_inner, left_outer):
    turn(size, masked, left_inner, left_outer)
    store_tile(dot(left_inner[...], inner[...]) + dot(left_outer[...], outer[...]), own, link, chip)


def partner_tile(
    size, basis, reach, inner, outer, near_left, inner_r, own, link, chip, far_outer, far, near, masked, far_inner
):
    low, high = reaches(reach)
    blocks = basis.shape[1] // size
    for b in range(blocks):
        mask_block(basis, b, blocks, size, low, high, masked)
    turn(size, masked, far_inner, far_outer)
    store_tile(dot(far_inner[...], inner[...]) + dot(far_outer[...], outer[...]), own, link, chip)
    far[...] = dot(far_inner[...], inner_r[...])
    near[...] = dot(near_left[...], inner_r[...])


def far_tile(part, part_link, part_chip, base, left_outer, outer_r, far, far_link, far_chip):
    wide = outer_r.shape[1]
    far[:, :wide] = part[...]
    far_link[:, :wide] = part_link[...]
    far_chip[:, :wide] = part_chip[...]
    tile = base[...] + dot(left_outer[...], outer_r[...])
    store_tile(tile, far.at[:, wide:], far_link.at[:, wide:], far_chip.at[:, wide:])


def near_tile(base, left_outer, outer_r, near, near_link, near_chip):
    store_tile(base[...] + dot(left_outer[...], outer_r[...]), near, near_link, near_chip)


def add_tiles(steps, *refs):
    count = len(steps)
    terms = refs[: 3 * count]
    coarse, total, sem = refs[-3:]
    width = total.shape[2]
    me = lax.axis_index("col")
    even = parity() == 0
    copies = []
    for n, ((even_step, odd_step), chunks) in enumerate(steps):
        own, chip, link = (
            terms[n + k * count][:, m * 3 * width : (m + 1) * 3 * width].astype(F32) for k, m in enumerate(chunks)
        )
        prev = jnp.where(even, link, chip)
        nxt = jnp.where(even, chip, link)
        for d in range(5):
            value = None
            for offset, term in ((0, prev), (1, own), (2, nxt)):
                if 0 <= d - offset <= 2:
                    part = term[:, (d - offset) * width : (d - offset + 1) * width]
                    value = part if value is None else value + part
            total[n, d] = value
        column = lax.bitwise_xor(me, jnp.where(even, even_step, odd_step))
        start = pl.multiple_of(column * width, width)
        copy = pltpu.make_async_copy(total.at[n], coarse.at[:, :, pl.ds(start, width)], sem.at[n])
        copy.start()
        copies.append(copy)
    for copy in copies:
        copy.wait()


def tile_shapes(width, wide, own):
    return shape((width, wide), own), shape((width, wide), BF16), shape((width, wide), BF16)


def shards(stiffness, block_cols, basis, patch_reach):
    blocks, slots, size, _ = stiffness.shape
    rows, groups, width = basis.shape
    wide = groups * width
    slabs = lax.axis_size("blk")
    total_blocks = blocks * slabs
    pairs = [(i, i ^ 1) for i in range(slabs)]
    cross = [(i, (i - 1 if i % 2 == 0 else i + 1) % slabs) for i in range(slabs)]

    def over_chip(value):
        return lax.ppermute(value, "blk", pairs)

    def over_link(value):
        return lax.ppermute(value, "blk", cross)

    def to(value, slab_of, column_of):
        perm = [(4 * i + q, 4 * (slab_of(i) % slabs) + column_of(i, q)) for i in range(slabs) for q in range(4)]
        return lax.ppermute(value, ("blk", "col"), perm)

    def partner(i, q):
        return q ^ (1 + i % 2)

    def side(i, q):
        return q ^ (2 - i % 2)

    def to_partner(value):
        return to(value, lambda i: i, partner)

    def to_side(value):
        return to(value, lambda i: i, side)

    def to_partner_link(value):
        return to(value, lambda i: i + 1 if i % 2 else i - 1, partner)

    basis_p = to_partner(basis).transpose(1, 0, 2)
    reach_p = to_partner(patch_reach).transpose(0, 2, 1)
    cols = block_cols.T
    flat = basis.transpose(1, 0, 2)
    reach = patch_reach.transpose(0, 2, 1)
    inner_rows = (blocks - 2 * RIM) * size
    rim = RIM * size
    row_flops = 2 * slots * size * size * wide
    masked, rim_link, rim_chip, inner = call(
        functools.partial(mask_and_inner, total_blocks),
        (shape((rows, wide), BF16), shape((rim, 2 * width), BF16), shape((rim, 2 * width), BF16), shape((inner_rows, wide), BF16)),
        [HBM] * 4,
        [VMEM] * 4,
        tuple(pltpu.with_memory_space_constraint(x, pltpu.HBM) for x in (cols, flat, reach, stiffness)),
        scratch=[
            pltpu.SMEM(cols.shape, cols.dtype),
            pltpu.VMEM(flat.shape, BF16),
            pltpu.VMEM(reach.shape, reach.dtype),
            pltpu.VMEM(stiffness.shape, BF16),
            pltpu.SemaphoreType.DMA((3 + blocks // RIM,)),
        ],
        flops=row_flops * (blocks - 2 * RIM),
        name="mask_and_inner",
    )
    inner_r = to_side(inner)
    rim_link = over_link(rim_link)
    rim_chip = over_chip(rim_chip)
    outer = call(
        functools.partial(outer_image, total_blocks),
        shape((2 * rim, wide), BF16),
        [SMEM] + [VMEM] * 4,
        VMEM,
        (cols, stiffness, masked, rim_link, rim_chip),
        scratch=[pltpu.VMEM((rows + 2 * rim, wide), BF16)],
        flops=row_flops * 2 * RIM,
        name="outer_image",
    )
    outer_r = to_side(outer)
    tile_flops = 2 * rows * wide * wide
    left_shapes = (shape((wide, inner_rows), BF16), shape((wide, 2 * rim), BF16))
    base_shape = shape((wide, wide), F32)

    own, own_link, own_chip, left_inner, left_outer = call(
        functools.partial(own_tile, size),
        (*tile_shapes(width, wide, F32), *left_shapes),
        [VMEM] * 3,
        [VMEM] * 5,
        (masked, inner, outer),
        flops=tile_flops,
        name="own_tile",
    )
    own_link, own_chip = over_link(own_link), over_chip(own_chip)
    part, part_link, part_chip, far_outer, far_base, near_base = call(
        functools.partial(partner_tile, size),
        (*tile_shapes(width, wide, BF16), left_shapes[1], base_shape, base_shape),
        [VMEM] * 6,
        [VMEM] * 6,
        (basis_p, reach_p, inner, outer, left_inner, inner_r),
        scratch=[pltpu.VMEM((rows, wide), BF16), pltpu.VMEM((wide, inner_rows), BF16)],
        flops=2 * tile_flops,
        name="partner_tile",
    )
    outer_r, own_link, own_chip, far_base = lax.optimization_barrier((outer_r, own_link, own_chip, far_base))
    far, far_link, far_chip = call(
        far_tile,
        (shape((width, 2 * wide), BF16),) * 3,
        [VMEM] * 6,
        [VMEM] * 3,
        (part, part_link, part_chip, far_base, far_outer, outer_r),
        flops=tile_flops // 2,
        name="far_tile",
    )
    near, near_link, near_chip = call(
        near_tile,
        tile_shapes(width, wide, F32),
        [VMEM] * 3,
        [VMEM] * 3,
        (near_base, left_outer, outer_r),
        flops=tile_flops // 2,
        name="near_tile",
    )
    far_link = to_partner_link(far_link)
    near_link = over_link(near_link)
    far_chip = to(far_chip, lambda i: i ^ 1, partner)
    far = to_partner(far)
    near_chip = over_chip(near_chip)

    def add(steps, terms, name, base=None):
        extra = () if base is None else (base,)
        return call(
            functools.partial(add_tiles, steps),
            shape((5, width, 4 * width), F32),
            [VMEM] * len(terms) + [HBM] * len(extra),
            HBM,
            (*terms, *extra),
            scratch=[pltpu.VMEM((len(steps), 5, width, width), F32), pltpu.SemaphoreType.DMA((len(steps),))],
            flops=5 * len(steps) * width * width,
            aliases={len(terms): 0} if extra else None,
            name=name,
        )

    coarse = add((((0, 0), (0, 0, 0)),), (own, own_chip, own_link), "add_own")
    coarse = add(
        (((3, 3), (1, 1, 1)), ((1, 2), (0, 0, 0)), ((2, 1), (0, 0, 0))),
        (far, far, near, far_chip, near_chip, far_chip, far_link, near_link, far_link),
        "add_rest",
        coarse,
    )
    return coarse.transpose(1, 0, 2)


def gathered(stiffness, block_cols, basis, patch_reach):
    blocks, slots, size, _ = stiffness.shape
    rows, groups, width = basis.shape
    slabs = lax.axis_size("blk")
    slab = lax.axis_index("blk")
    total_blocks = blocks * slabs
    ring = [(i, (i + 1) % slabs) for i in range(slabs)]
    back = [(j, i) for i, j in ring]
    low = lax.dynamic_index_in_dim(patch_reach, (slab - 1) % slabs, 0, False)[:, 1]
    high = lax.dynamic_index_in_dim(patch_reach, (slab + 1) % slabs, 0, False)[:, 0]
    block_row = jnp.arange(rows, dtype=jnp.int32) // size
    lower = block_row[:, None] < low[None, :]
    upper = block_row[:, None] >= blocks - high[None, :]
    support = jnp.stack([lower, jnp.ones_like(lower), upper], 1)
    masked = jnp.where(support, basis, jnp.zeros_like(basis))
    rim = RIM * size
    before = lax.ppermute(masked[rows - rim :, 1:], "blk", ring)
    after = lax.ppermute(masked[:rim, :2], "blk", back)
    none = jnp.zeros((rim, 1, width), masked.dtype)
    extended = jnp.concatenate(
        [jnp.concatenate([before, none], 1), masked, jnp.concatenate([none, after], 1)], 0
    ).reshape(blocks + 2 * RIM, size, groups * width)
    position = (block_cols - slab * blocks + RIM) % total_blocks
    picked = jnp.take(extended, position, axis=0)
    image = jnp.einsum("rsij,rsjc->ric", stiffness, picked, preferred_element_type=F32)
    image = image.astype(BF16).reshape(rows, groups, width)
    image = lax.all_gather(image, "col", axis=2, tiled=True)
    tiles = jnp.einsum("rgl,rhc->glhc", masked, image, preferred_element_type=F32)
    from_prev = lax.ppermute(tiles[2], "blk", ring)
    from_next = lax.ppermute(tiles[0], "blk", back)

    def place(tile, offset):
        return jnp.pad(tile, ((0, 0), (offset, 2 - offset), (0, 0)))

    return place(from_prev, 0) + place(tiles[1], 1) + place(from_next, 2)


def solution(mesh):
    in_specs = (
        P("blk", None, None, None),
        P("blk", None),
        P("blk", None, "col"),
        P(None, "col", None),
    )
    out_specs = P(("blk", "col"), None, None)
    body = shards if mesh.shape["col"] == 4 and mesh.shape["blk"] % 2 == 0 else gathered
    return jax.shard_map(body, mesh=mesh, in_specs=in_specs, out_specs=out_specs, check_vma=False)
```

```python
import functools

import jax
import jax.numpy as jnp
from jax import lax
from jax.experimental import pallas as pl
from jax.experimental.pallas import tpu as pltpu
from jax.sharding import PartitionSpec as P

BF16 = jnp.bfloat16
F32 = jnp.float32
VMEM = pl.BlockSpec(memory_space=pltpu.VMEM)
SMEM = pl.BlockSpec(memory_space=pltpu.SMEM)
HBM = pl.BlockSpec(memory_space=pltpu.HBM)
RIM = 2


def shape(dims, dtype):
    return jax.ShapeDtypeStruct(dims, dtype)


def dot(left, right):
    return jnp.dot(left, right, preferred_element_type=F32)


def call(kernel, out_shape, in_specs, out_specs, args, scratch=(), flops=0, aliases=None, name=None):
    outs = jax.tree.leaves(out_shape)
    moved = sum(x.size * x.dtype.itemsize for x in (*args, *outs))
    return pl.pallas_call(
        kernel,
        out_shape=out_shape,
        in_specs=in_specs,
        out_specs=out_specs,
        scratch_shapes=list(scratch),
        input_output_aliases=aliases or {},
        cost_estimate=pl.CostEstimate(flops=flops, bytes_accessed=moved, transcendentals=0),
        compiler_params=pltpu.CompilerParams(vmem_limit_bytes=24 << 20),
        name=name,
    )(*args)


def block_image(stiffness, source, b, block_size, starts):
    blocks = [source[pl.ds(pl.multiple_of(start * block_size, block_size), block_size), :] for start in starts]
    left = jnp.concatenate([stiffness[b, k] for k in range(len(starts))], axis=1)
    return dot(left, jnp.concatenate(blocks, axis=0)).astype(BF16)


def positions(cols, b, blocks, slots, total_blocks):
    first = lax.axis_index("blk") * blocks
    return [
        jnp.clip(lax.rem(cols[k, b] - first + RIM + total_blocks, total_blocks), 0, blocks + 2 * RIM - 1)
        for k in range(slots)
    ]


def reaches(reach):
    slabs = reach.shape[0]
    slab = lax.axis_index("blk")
    low = reach[pl.ds(lax.rem(slab + slabs - 1, slabs), 1), 1, :]
    high = reach[pl.ds(lax.rem(slab + 1, slabs), 1), 0, :]
    return low, high


def mask_block(basis, b, blocks, size, low, high, masked):
    groups, _, width = basis.shape
    rows = slice(b * size, (b + 1) * size)
    keep = {0: (b < low).astype(F32).astype(BF16), 2: (b >= blocks - high).astype(F32).astype(BF16)}
    for g in range(groups):
        value = basis[g, rows, :]
        masked[rows, g * width : (g + 1) * width] = value * keep[g] if g in keep else value


def mask_and_inner(
    total_blocks, cols_hbm, basis_hbm, reach_hbm, stiffness_hbm, masked, to_link, to_chip, inner, cols, basis, reach, stiffness, sem
):
    blocks, slots, size, _ = stiffness.shape
    width = basis.shape[2]
    inner_blocks = pl.ds(RIM, blocks - 2 * RIM)
    moves = [(reach_hbm, reach), (cols_hbm, cols)]
    moves += [
        (basis_hbm.at[:, pl.ds(b * size, RIM * size)], basis.at[:, pl.ds(b * size, RIM * size)])
        for b in range(0, blocks, RIM)
    ]
    moves.append((stiffness_hbm.at[inner_blocks], stiffness.at[inner_blocks]))
    copies = [pltpu.make_async_copy(source, target, sem.at[n]) for n, (source, target) in enumerate(moves)]
    for copy in copies:
        copy.start()
    copies[0].wait()
    low, high = reaches(reach)
    for b in range(blocks):
        if b % RIM == 0:
            copies[2 + b // RIM].wait()
        mask_block(basis, b, blocks, size, low, high, masked)
    odd = parity()

    @pl.when(odd == 0)
    def _():
        to_link[...] = masked[: RIM * size, : 2 * width]
        to_chip[...] = masked[(blocks - RIM) * size :, width:]

    @pl.when(odd == 1)
    def _():
        to_link[...] = masked[(blocks - RIM) * size :, width:]
        to_chip[...] = masked[: RIM * size, : 2 * width]

    copies[1].wait()
    copies[-1].wait()
    for b in range(RIM, blocks - RIM):
        starts = [jnp.clip(p - RIM, 0, blocks - 1) for p in positions(cols, b, blocks, slots, total_blocks)]
        inner[(b - RIM) * size : (b - RIM + 1) * size, :] = block_image(stiffness, masked, b, size, starts)


def outer_image(total_blocks, cols, stiffness, masked, from_link, from_chip, outer, extended):
    blocks, slots, size, _ = stiffness.shape
    rows, wide = masked.shape
    rim = RIM * size
    width = wide // 3
    odd = parity()

    @pl.when(odd == 0)
    def _():
        extended[:rim, : 2 * width] = from_link[...]
        extended[rim + rows :, width:] = from_chip[...]

    @pl.when(odd == 1)
    def _():
        extended[:rim, : 2 * width] = from_chip[...]
        extended[rim + rows :, width:] = from_link[...]

    extended[:rim, 2 * width :] = jnp.zeros((rim, width), BF16)
    extended[rim : rim + rows, :] = masked[...]
    extended[rim + rows :, :width] = jnp.zeros((rim, width), BF16)
    for n, b in enumerate([*range(RIM), *range(blocks - RIM, blocks)]):
        starts = positions(cols, b, blocks, slots, total_blocks)
        outer[n * size : (n + 1) * size, :] = block_image(stiffness, extended, b, size, starts)


def parity():
    return lax.rem(lax.axis_index("blk"), 2)


def store_tile(tile, own, link, chip):
    width = tile.shape[0] // 3
    odd = parity()
    own[...] = tile[width : 2 * width].astype(own.dtype)
    down, up = tile[:width].astype(BF16), tile[2 * width :].astype(BF16)

    @pl.when(odd == 0)
    def _():
        link[...] = down
        chip[...] = up

    @pl.when(odd == 1)
    def _():
        link[...] = up
        chip[...] = down


def turn(size, masked, left_inner, left_outer):
    rows = masked.shape[0]
    rim = RIM * size
    left_inner[...] = masked[rim : rows - rim, :].T
    left_outer[:, :rim] = masked[:rim, :].T
    left_outer[:, rim:] = masked[rows - rim :, :].T


def own_tile(size, masked, inner, outer, own, link, chip, left_inner, left_outer):
    turn(size, masked, left_inner, left_outer)
    store_tile(dot(left_inner[...], inner[...]) + dot(left_outer[...], outer[...]), own, link, chip)


def partner_tile(
    size, basis, reach, inner, outer, near_left, inner_r, own, link, chip, far_outer, far, near, masked, far_inner
):
    low, high = reaches(reach)
    blocks = basis.shape[1] // size
    for b in range(blocks):
        mask_block(basis, b, blocks, size, low, high, masked)
    turn(size, masked, far_inner, far_outer)
    store_tile(dot(far_inner[...], inner[...]) + dot(far_outer[...], outer[...]), own, link, chip)
    far[...] = dot(far_inner[...], inner_r[...])
    near[...] = dot(near_left[...], inner_r[...])


def far_tile(part, part_link, part_chip, base, left_outer, outer_r, far, far_link, far_chip):
    wide = outer_r.shape[1]
    far[:, :wide] = part[...]
    far_link[:, :wide] = part_link[...]
    far_chip[:, :wide] = part_chip[...]
    tile = base[...] + dot(left_outer[...], outer_r[...])
    store_tile(tile, far.at[:, wide:], far_link.at[:, wide:], far_chip.at[:, wide:])


def near_tile(base, left_outer, outer_r, near, near_link, near_chip):
    store_tile(base[...] + dot(left_outer[...], outer_r[...]), near, near_link, near_chip)


def add_tiles(steps, *refs):
    count = len(steps)
    terms = refs[: 3 * count]
    coarse, total, sem = refs[-3:]
    width = total.shape[2]
    me = lax.axis_index("col")
    even = parity() == 0
    copies = []
    for n, ((even_step, odd_step), chunks) in enumerate(steps):
        chip, link, own = (
            terms[n + k * count][:, m * 3 * width : (m + 1) * 3 * width].astype(F32) for k, m in enumerate(chunks)
        )
        prev = jnp.where(even, link, chip)
        nxt = jnp.where(even, chip, link)
        for d in range(5):
            value = None
            for offset, term in ((0, prev), (1, own), (2, nxt)):
                if 0 <= d - offset <= 2:
                    part = term[:, (d - offset) * width : (d - offset + 1) * width]
                    value = part if value is None else value + part
            total[n, d] = value
        column = lax.bitwise_xor(me, jnp.where(even, even_step, odd_step))
        start = pl.multiple_of(column * width, width)
        copy = pltpu.make_async_copy(total.at[n], coarse.at[:, :, pl.ds(start, width)], sem.at[n])
        copy.start()
        copies.append(copy)
    for copy in copies:
        copy.wait()


def tile_shapes(width, wide, own):
    return shape((width, wide), own), shape((width, wide), BF16), shape((width, wide), BF16)


def shards(stiffness, block_cols, basis, patch_reach):
    blocks, slots, size, _ = stiffness.shape
    rows, groups, width = basis.shape
    wide = groups * width
    slabs = lax.axis_size("blk")
    total_blocks = blocks * slabs
    pairs = [(i, i ^ 1) for i in range(slabs)]
    cross = [(i, (i - 1 if i % 2 == 0 else i + 1) % slabs) for i in range(slabs)]

    def over_chip(value):
        return lax.ppermute(value, "blk", pairs)

    def over_link(value):
        return lax.ppermute(value, "blk", cross)

    def to(value, slab_of, column_of):
        perm = [(4 * i + q, 4 * (slab_of(i) % slabs) + column_of(i, q)) for i in range(slabs) for q in range(4)]
        return lax.ppermute(value, ("blk", "col"), perm)

    def partner(i, q):
        return q ^ (1 + i % 2)

    def side(i, q):
        return q ^ (2 - i % 2)

    def to_partner(value):
        return to(value, lambda i: i, partner)

    def to_side(value):
        return to(value, lambda i: i, side)

    def to_partner_link(value):
        return to(value, lambda i: i + 1 if i % 2 else i - 1, partner)

    basis_p = to_partner(basis).transpose(1, 0, 2)
    reach_p = to_partner(patch_reach).transpose(0, 2, 1)
    cols = block_cols.T
    flat = basis.transpose(1, 0, 2)
    reach = patch_reach.transpose(0, 2, 1)
    inner_rows = (blocks - 2 * RIM) * size
    rim = RIM * size
    row_flops = 2 * slots * size * size * wide
    masked, rim_link, rim_chip, inner = call(
        functools.partial(mask_and_inner, total_blocks),
        (shape((rows, wide), BF16), shape((rim, 2 * width), BF16), shape((rim, 2 * width), BF16), shape((inner_rows, wide), BF16)),
        [HBM] * 4,
        [VMEM] * 4,
        tuple(pltpu.with_memory_space_constraint(x, pltpu.HBM) for x in (cols, flat, reach, stiffness)),
        scratch=[
            pltpu.SMEM(cols.shape, cols.dtype),
            pltpu.VMEM(flat.shape, BF16),
            pltpu.VMEM(reach.shape, reach.dtype),
            pltpu.VMEM(stiffness.shape, BF16),
            pltpu.SemaphoreType.DMA((3 + blocks // RIM,)),
        ],
        flops=row_flops * (blocks - 2 * RIM),
        name="mask_and_inner",
    )
    inner_r = to_side(inner)
    rim_link = over_link(rim_link)
    rim_chip = over_chip(rim_chip)
    outer = call(
        functools.partial(outer_image, total_blocks),
        shape((2 * rim, wide), BF16),
        [SMEM] + [VMEM] * 4,
        VMEM,
        (cols, stiffness, masked, rim_link, rim_chip),
        scratch=[pltpu.VMEM((rows + 2 * rim, wide), BF16)],
        flops=row_flops * 2 * RIM,
        name="outer_image",
    )
    outer_r = to_side(outer)
    tile_flops = 2 * rows * wide * wide
    left_shapes = (shape((wide, inner_rows), BF16), shape((wide, 2 * rim), BF16))
    base_shape = shape((wide, wide), F32)

    own, own_link, own_chip, left_inner, left_outer = call(
        functools.partial(own_tile, size),
        (*tile_shapes(width, wide, F32), *left_shapes),
        [VMEM] * 3,
        [VMEM] * 5,
        (masked, inner, outer),
        flops=tile_flops,
        name="own_tile",
    )
    own_link, own_chip = over_link(own_link), over_chip(own_chip)
    inner_r, own_link = lax.optimization_barrier((inner_r, own_link))
    part, part_link, part_chip, far_outer, far_base, near_base = call(
        functools.partial(partner_tile, size),
        (*tile_shapes(width, wide, BF16), left_shapes[1], base_shape, base_shape),
        [VMEM] * 6,
        [VMEM] * 6,
        (basis_p, reach_p, inner, outer, left_inner, inner_r),
        scratch=[pltpu.VMEM((rows, wide), BF16), pltpu.VMEM((wide, inner_rows), BF16)],
        flops=2 * tile_flops,
        name="partner_tile",
    )
    outer_r, own_link, own_chip, far_base = lax.optimization_barrier((outer_r, own_link, own_chip, far_base))
    far, far_link, far_chip = call(
        far_tile,
        (shape((width, 2 * wide), BF16),) * 3,
        [VMEM] * 6,
        [VMEM] * 3,
        (part, part_link, part_chip, far_base, far_outer, outer_r),
        flops=tile_flops // 2,
        name="far_tile",
    )
    near, near_link, near_chip = call(
        near_tile,
        tile_shapes(width, wide, F32),
        [VMEM] * 3,
        [VMEM] * 3,
        (near_base, left_outer, outer_r),
        flops=tile_flops // 2,
        name="near_tile",
    )
    far_link = to_partner_link(far_link)
    near_link = over_link(near_link)
    far_chip = to(far_chip, lambda i: i ^ 1, partner)
    far = to_partner(far)
    near_chip = over_chip(near_chip)

    def add(steps, terms, name, base=None):
        extra = () if base is None else (base,)
        return call(
            functools.partial(add_tiles, steps),
            shape((5, width, 4 * width), F32),
            [VMEM] * len(terms) + [HBM] * len(extra),
            HBM,
            (*terms, *extra),
            scratch=[pltpu.VMEM((len(steps), 5, width, width), F32), pltpu.SemaphoreType.DMA((len(steps),))],
            flops=5 * len(steps) * width * width,
            aliases={len(terms): 0} if extra else None,
            name=name,
        )

    coarse = add((((0, 0), (0, 0, 0)),), (own_chip, own_link, own), "add_own")
    coarse = add(
        (((3, 3), (1, 1, 1)), ((1, 2), (0, 0, 0)), ((2, 1), (0, 0, 0))),
        (far_chip, near_chip, far_chip, far_link, near_link, far_link, far, far, near),
        "add_rest",
        coarse,
    )
    return coarse.transpose(1, 0, 2)


def gathered(stiffness, block_cols, basis, patch_reach):
    blocks, slots, size, _ = stiffness.shape
    rows, groups, width = basis.shape
    slabs = lax.axis_size("blk")
    slab = lax.axis_index("blk")
    total_blocks = blocks * slabs
    ring = [(i, (i + 1) % slabs) for i in range(slabs)]
    back = [(j, i) for i, j in ring]
    low = lax.dynamic_index_in_dim(patch_reach, (slab - 1) % slabs, 0, False)[:, 1]
    high = lax.dynamic_index_in_dim(patch_reach, (slab + 1) % slabs, 0, False)[:, 0]
    block_row = jnp.arange(rows, dtype=jnp.int32) // size
    lower = block_row[:, None] < low[None, :]
    upper = block_row[:, None] >= blocks - high[None, :]
    support = jnp.stack([lower, jnp.ones_like(lower), upper], 1)
    masked = jnp.where(support, basis, jnp.zeros_like(basis))
    rim = RIM * size
    before = lax.ppermute(masked[rows - rim :, 1:], "blk", ring)
    after = lax.ppermute(masked[:rim, :2], "blk", back)
    none = jnp.zeros((rim, 1, width), masked.dtype)
    extended = jnp.concatenate(
        [jnp.concatenate([before, none], 1), masked, jnp.concatenate([none, after], 1)], 0
    ).reshape(blocks + 2 * RIM, size, groups * width)
    position = (block_cols - slab * blocks + RIM) % total_blocks
    picked = jnp.take(extended, position, axis=0)
    image = jnp.einsum("rsij,rsjc->ric", stiffness, picked, preferred_element_type=F32)
    image = image.astype(BF16).reshape(rows, groups, width)
    image = lax.all_gather(image, "col", axis=2, tiled=True)
    tiles = jnp.einsum("rgl,rhc->glhc", masked, image, preferred_element_type=F32)
    from_prev = lax.ppermute(tiles[2], "blk", ring)
    from_next = lax.ppermute(tiles[0], "blk", back)

    def place(tile, offset):
        return jnp.pad(tile, ((0, 0), (offset, 2 - offset), (0, 0)))

    return place(from_prev, 0) + place(tiles[1], 1) + place(from_next, 2)


def solution(mesh):
    in_specs = (
        P("blk", None, None, None),
        P("blk", None),
        P("blk", None, "col"),
        P(None, "col", None),
    )
    out_specs = P(("blk", "col"), None, None)
    body = shards if mesh.shape["col"] == 4 and mesh.shape["blk"] % 2 == 0 else gathered
    return jax.shard_map(body, mesh=mesh, in_specs=in_specs, out_specs=out_specs, check_vma=False)
```
